32 devices in a mesh: dp: 16 (over z, y, core), tensor: 2 (over x).
Axes of the slice: x: 2, y: 2, z: 4, core: 2. Of those that a mesh axis runs over, the one named last changes fastest.
Arguments:
- tokens: bfloat16 [16384, 1024], P('dp'), may hold values from -6 to 6
- lengths: int32 [16], P('dp'), may hold values from 256 to 1024, as said below
- w_query: bfloat16 [1024, 1024], P(None, 'tensor'), may hold values from -0.1875 to 0.1875
- w_key: bfloat16 [1024, 1024], P(None, 'tensor'), may hold values from -0.1875 to 0.1875
- w_value: bfloat16 [1024, 1024], P(None, 'tensor'), may hold values from -0.1875 to 0.1875
- w_out: bfloat16 [1024, 1024], P('tensor'), may hold values from -0.1875 to 0.1875
- w_up: bfloat16 [1024, 4096], P(None, 'tensor'), may hold values from -0.1875 to 0.1875
- w_down: bfloat16 [4096, 1024], P('tensor'), may hold values from -0.09375 to 0.09375
- norm_gain: float32 [4, 1024], replicated, may hold values from 0.1 to 1.9
- norm_bias: float32 [4, 1024], replicated, may hold values from -1.5 to 1.5
- cotangent: bfloat16 [16384, 1024], P('dp'), may hold values from -6 to 6
Outputs:
- result: bfloat16 [16384, 1024], P('dp')
- input_grad: bfloat16 [16384, 1024], P('dp')
- grad_query: float32 [1024, 1024], P('dp', 'tensor')
- grad_key: float32 [1024, 1024], P('dp', 'tensor')
- grad_value: float32 [1024, 1024], P('dp', 'tensor')
- grad_out: float32 [1024, 1024], P('tensor', 'dp')
- grad_up: float32 [1024, 4096], P('dp', 'tensor')
- grad_down: float32 [4096, 1024], P('tensor', 'dp')
- grad_gain: float32 [4, 1024], P(None, 'dp')
- grad_bias: float32 [4, 1024], P(None, 'dp')
The draws below stay inside these ranges and needn't reach their ends.
Inputs may be any that keep to these rules, and one draw needn't show every extreme that they name: Each sequence's real tokens fill its first lengths[s] slots of 1024; some sequence is full and some has 256.
All inputs are finite; a program needn't handle non-finite values.
Results may differ from the reference program's by a relative error of at most 0.018.
Values may be sent and summed in bfloat16 or wider, within the bound.
A program may use at most 192 MiB of HBM per device.

```python
import jax
import jax.numpy as jnp
from jax import lax

D = 1024
HEADS = 16
HD = 64
FF = 4096
LEN = 1024
SEQUENCES = 16
TOKENS = 16384
N_TENSOR = 2


def draw_lengths(key, part):
    sampled = jax.random.randint(key, (SEQUENCES,), LEN // 4, LEN + 1, dtype=jnp.int32)
    placing = jax.random.permutation(jax.random.fold_in(key, 7), SEQUENCES)
    sampled = sampled.at[placing[0]].set(LEN)
    return sampled.at[placing[1]].set(LEN // 4)


def level_of(own_key, dims, cuts, smallest, largest):
    def one(position, shards_of):
        heights = jax.random.uniform(jax.random.fold_in(jax.random.fold_in(own_key, 6), position), (shards_of,), jnp.float32, smallest / len(cuts), largest / len(cuts))
        return jnp.repeat(jnp.exp(heights), dims[position] // shards_of).reshape((-1,) + (1,) * (len(dims) - position - 1))

    level = one(*cuts[0])
    for cut in cuts[1:]:
        level = level * one(*cut)
    return level


def noise(stream_key, shape, scale, most, cuts=(), kind=jnp.bfloat16):
    drawn = scale * jax.random.normal(stream_key, shape, jnp.float32)
    if cuts:
        drawn = drawn * level_of(stream_key, shape, cuts, -0.22, 0.18)
    return jnp.clip(drawn, -most, most).astype(kind)


def setup_inputs(seed: int = 0) -> dict:
    key_list = jax.random.split(jax.random.key(seed), 12)
    tokens = noise(key_list[0], (TOKENS, D), 1.0, 6.0, ((0, 16),))
    lengths = draw_lengths(jax.random.fold_in(key_list[11], 71), 0)
    w_query = noise(key_list[2], (D, D), D ** -0.5, 0.1875, ((1, 2),))
    w_key = noise(key_list[3], (D, D), D ** -0.5, 0.1875, ((1, 2),))
    w_value = noise(key_list[4], (D, D), D ** -0.5, 0.1875, ((1, 2),))
    w_out = noise(key_list[5], (D, D), D ** -0.5, 0.1875, ((0, 2),))
    w_up = noise(key_list[6], (D, FF), D ** -0.5, 0.1875, ((1, 2),))
    w_down = noise(key_list[7], (FF, D), FF ** -0.5, 0.09375, ((0, 2),))
    norm_gain = jnp.clip(1.0 + 0.18 * jax.random.normal(key_list[8], (4, D), jnp.float32), 0.1, 1.9)
    norm_bias = noise(key_list[9], (4, D), 0.3, 1.5, (), jnp.float32)
    cotangent = noise(key_list[10], (TOKENS, D), 1.0, 6.0, ((0, 16),))
    return dict(tokens=tokens, lengths=lengths, w_query=w_query, w_key=w_key, w_value=w_value, w_out=w_out, w_up=w_up, w_down=w_down, norm_gain=norm_gain, norm_bias=norm_bias, cotangent=cotangent)


@jax.custom_vjp
def low(v):
    return lax.optimization_barrier(v.astype(jnp.bfloat16)).astype(jnp.float32)

@jax.custom_vjp
def low_back(v):
    return v

def low_keep(v):
    return (low(v), None)

def low_pass(kept, grad):
    return (grad,)

def back_keep(v):
    return (v, None)

def back_low(kept, grad):
    return (low(grad),)
low.defvjp(low_keep, low_pass)
low_back.defvjp(back_keep, back_low)
epsilon = 1e-05
highest = lax.Precision.HIGHEST

def product(left, right):
    return jnp.dot(left, right, precision=highest, preferred_element_type=jnp.float32)

def layer_norm(values, gain_vec, bias_vec):
    average = lax.optimization_barrier(jnp.mean(values, axis=-1, keepdims=True))
    centered = values - average
    variance = lax.optimization_barrier(jnp.mean(centered * centered, axis=-1, keepdims=True))
    return centered * lax.rsqrt(variance + epsilon) * gain_vec + bias_vec

def rank_sum(partial_in, weight, inner):
    length = partial_in.shape[0]
    pieces = partial_in.reshape(length, N_TENSOR, inner // N_TENSOR)
    blocks = weight.reshape(N_TENSOR, inner // N_TENSOR, weight.shape[1])
    terms = jnp.einsum('lrk,rkd->lrd', pieces, blocks, precision=highest)
    return low_back(lax.optimization_barrier(jnp.sum(low(terms), axis=1)))

def layer_forward(seq_tokens, key_valid, w_query, w_key, w_value, w_out, w_up, w_down, norm_gain, norm_bias):
    length = seq_tokens.shape[0]
    normed_in = low(layer_norm(seq_tokens, norm_gain[0], norm_bias[0]))
    queries = low_back(low(product(normed_in, w_query))).reshape(length, HEADS, HD)
    key_rows = low_back(low(product(normed_in, w_key))).reshape(length, HEADS, HD)
    value_rows = low_back(low(product(normed_in, w_value))).reshape(length, HEADS, HD)
    scores = jnp.einsum('qhd,khd->hqk', queries * (1.0 / 256.0), key_rows, precision=highest) * 32.0
    scores = low_back(jnp.where(key_valid[None, None, :], scores, -1000000000.0))
    soft_weights = low(jax.nn.softmax(scores, axis=-1))
    attended = jnp.einsum('hqk,khd->qhd', soft_weights, value_rows, precision=highest).reshape(length, D)
    attended = low_back(low(attended))
    attn_total = rank_sum(attended, w_out, D)
    middle = seq_tokens + layer_norm(attn_total, norm_gain[1], norm_bias[1])
    normed_mid = low(layer_norm(middle, norm_gain[2], norm_bias[2]))
    up_proj = low_back(product(normed_mid, w_up))
    hidden = low(jax.nn.gelu(up_proj))
    ffn_total = rank_sum(hidden, w_down, FF)
    return middle + layer_norm(ffn_total, norm_gain[3], norm_bias[3])

def reference(tokens, lengths, w_query, w_key, w_value, w_out, w_up, w_down, norm_gain, norm_bias, cotangent):
    params = tuple((weight_in.astype(jnp.float32) for weight_in in (w_query, w_key, w_value, w_out, w_up, w_down, norm_gain, norm_bias)))
    tokens_all = tokens.astype(jnp.float32).reshape(SEQUENCES, LEN, D)
    grads_all = cotangent.astype(jnp.float32).reshape(SEQUENCES, LEN, D)
    positions = jnp.arange(LEN, dtype=jnp.int32)

    def one_sequence(totals, slices):
        seq_tokens, seq_grad, seq_length = slices
        key_valid = positions < seq_length

        def bound_forward(inner_tokens, *weights):
            return layer_forward(inner_tokens, key_valid, *weights)
        outcome, pull = jax.vjp(bound_forward, seq_tokens, *params)
        grads = pull(seq_grad * key_valid[:, None].astype(jnp.float32))
        totals = tuple((running + increment for running, increment in zip(totals, grads[1:])))
        return (totals, (outcome.astype(jnp.bfloat16), grads[0].astype(jnp.bfloat16)))
    initial = tuple((jnp.zeros_like(weight_in) for weight_in in params))
    totals, (outcomes, input_grads) = lax.scan(one_sequence, initial, (tokens_all, grads_all, lengths))
    return (outcomes.reshape(TOKENS, D), input_grads.reshape(TOKENS, D), totals[0], totals[1], totals[2], totals[3], totals[4], totals[5], totals[6], totals[7])
```

```python
import jax
import jax.numpy as jnp
from jax import lax
from jax.sharding import PartitionSpec as P

HD = 64


epsilon = 1e-05
relax_scale = 0.125


def layer_norm(values, gain_vec, bias_vec):
    average = jnp.mean(values, axis=-1, keepdims=True)
    centered = values - average
    variance = jnp.mean(centered * centered, axis=-1, keepdims=True)
    return centered * lax.rsqrt(variance + epsilon) * gain_vec + bias_vec


def norm_back(values, gain_vec, bias_vec, grad_output):
    unused, pull = jax.vjp(layer_norm, values, gain_vec, bias_vec)
    return pull(grad_output)


def pair_sum(part):
    other = lax.ppermute(part, "tensor", [(0, 1), (1, 0)])
    return part.astype(jnp.float32) + other.astype(jnp.float32)


def scatter_sum(grad, dp_size):
    index = lax.axis_index("dp")
    width = grad.shape[1]
    rows = grad.shape[0] // dp_size
    held = grad
    bit = 1
    while bit < dp_size:
        blocks = held.reshape(-1, 2, rows, width)
        side = (index // bit) % 2
        keep = lax.dynamic_index_in_dim(blocks, side, 1, keepdims=False)
        give = lax.dynamic_index_in_dim(blocks, 1 - side, 1, keepdims=False)
        come = lax.ppermute(
            give.astype(jnp.bfloat16), "dp", [(i, i ^ bit) for i in range(dp_size)]
        )
        held = (keep.astype(jnp.float32) + come.astype(jnp.float32)).reshape(-1, width)
        bit *= 2
    return held


def split_heads(matrix):
    return matrix.reshape(matrix.shape[0], -1, HD)


def masked_scores(query_block, key_heads, key_valid):
    scores = (
        jnp.einsum("qhd,khd->hqk", query_block, key_heads, preferred_element_type=jnp.float32)
        * relax_scale
    )
    return jnp.where(key_valid[None, None, :], scores, -1000000000.0)


def block_size():
    return 512


def attention_forward(queries, key_rows, value_rows, valid_mask):
    seq_count, seq_len = valid_mask.shape
    block_rows = block_size()
    outputs = []
    log_totals = []
    key_heads = split_heads(key_rows)
    value_heads = split_heads(value_rows)
    for block_index in range(seq_len // block_rows):
        row_start = block_index * block_rows
        query_block = split_heads(queries[row_start : row_start + block_rows])
        scores = masked_scores(query_block, key_heads, valid_mask[0])
        maxima = jnp.max(scores, axis=-1, keepdims=True)
        exponent = jnp.exp(scores - maxima)
        sums_soft = jnp.sum(exponent, axis=-1, keepdims=True)
        soft_weights = (exponent / sums_soft).astype(jnp.bfloat16)
        mixture = jnp.einsum(
            "hqk,khd->qhd", soft_weights, value_heads, preferred_element_type=jnp.float32
        )
        outputs.append(mixture.reshape(block_rows, -1).astype(jnp.bfloat16))
        log_totals.append(maxima + jnp.log(sums_soft))
    return (jnp.concatenate(outputs, axis=0), log_totals)


def attention_backward(queries, key_rows, value_rows, grad_attended, log_totals, valid_mask):
    seq_count, seq_len = valid_mask.shape
    block_rows = block_size()
    query_grads = []
    counter = 0
    key_heads = split_heads(key_rows)
    value_heads = split_heads(value_rows)
    key_sum = jnp.zeros(key_heads.shape, jnp.float32)
    value_sum = jnp.zeros(value_heads.shape, jnp.float32)
    for block_index in range(seq_len // block_rows):
        row_start = block_index * block_rows
        query_block = split_heads(queries[row_start : row_start + block_rows])
        grad_block = split_heads(grad_attended[row_start : row_start + block_rows])
        scores = masked_scores(query_block, key_heads, valid_mask[0])
        soft_weights = jnp.exp(scores - log_totals[counter])
        counter += 1
        grad_soft = jnp.einsum(
            "qhd,khd->hqk", grad_block, value_heads, preferred_element_type=jnp.float32
        )
        row_dots = jnp.sum(soft_weights * grad_soft, axis=-1, keepdims=True)
        grad_scores = (soft_weights * (grad_soft - row_dots)).astype(jnp.bfloat16)
        query_grad = (
            jnp.einsum("hqk,khd->qhd", grad_scores, key_heads, preferred_element_type=jnp.float32)
            * relax_scale
        )
        query_grads.append(query_grad.reshape(block_rows, -1).astype(jnp.bfloat16))
        key_sum = (
            key_sum
            + jnp.einsum(
                "hqk,qhd->khd", grad_scores, query_block, preferred_element_type=jnp.float32
            )
            * relax_scale
        )
        value_sum = value_sum + jnp.einsum(
            "hqk,qhd->khd",
            soft_weights.astype(jnp.bfloat16),
            grad_block,
            preferred_element_type=jnp.float32,
        )
    key_grads = key_sum.reshape(seq_len, -1).astype(jnp.bfloat16)
    value_grads = value_sum.reshape(seq_len, -1).astype(jnp.bfloat16)
    return (jnp.concatenate(query_grads, axis=0), key_grads, value_grads)


def on_device(
    tokens, lengths, w_query, w_key, w_value, w_out, w_up, w_down, norm_gain, norm_bias, cotangent
):
    row_count = tokens.shape[0]
    seq_count = lengths.shape[0]
    seq_len = row_count // seq_count
    inputs = tokens.astype(jnp.float32)
    positions = jnp.arange(seq_len, dtype=jnp.int32)
    valid_mask = positions[None, :] < lengths[:, None]
    row_valid = valid_mask.reshape(row_count, 1).astype(jnp.float32)
    normed_in = layer_norm(inputs, norm_gain[0], norm_bias[0]).astype(jnp.bfloat16)
    queries = jnp.dot(normed_in, w_query, preferred_element_type=jnp.float32).astype(jnp.bfloat16)
    key_rows = jnp.dot(normed_in, w_key, preferred_element_type=jnp.float32).astype(jnp.bfloat16)
    value_rows = jnp.dot(normed_in, w_value, preferred_element_type=jnp.float32).astype(
        jnp.bfloat16
    )
    attended, log_totals = attention_forward(queries, key_rows, value_rows, valid_mask)
    attn_total = pair_sum(
        jnp.dot(attended, w_out, preferred_element_type=jnp.float32).astype(jnp.bfloat16)
    )
    middle = inputs + layer_norm(attn_total, norm_gain[1], norm_bias[1])
    normed_mid = layer_norm(middle, norm_gain[2], norm_bias[2]).astype(jnp.bfloat16)
    up_proj = jnp.dot(normed_mid, w_up, preferred_element_type=jnp.float32)
    hidden = jax.nn.gelu(up_proj).astype(jnp.bfloat16)
    ffn_total = pair_sum(
        jnp.dot(hidden, w_down, preferred_element_type=jnp.float32).astype(jnp.bfloat16)
    )
    result = (middle + layer_norm(ffn_total, norm_gain[3], norm_bias[3])).astype(jnp.bfloat16)
    grad_output = cotangent.astype(jnp.float32) * row_valid
    grad_last = norm_back(ffn_total, norm_gain[3], norm_bias[3], grad_output)
    grad_ffn_low = grad_last[0].astype(jnp.bfloat16)
    grad_w_down = jnp.einsum("rd,rf->df", grad_ffn_low, hidden, preferred_element_type=jnp.float32)
    grad_hidden = jnp.einsum("rd,fd->rf", grad_ffn_low, w_down, preferred_element_type=jnp.float32)
    unused, gelu_pull = jax.vjp(jax.nn.gelu, up_proj)
    grad_upper = gelu_pull(grad_hidden)[0].astype(jnp.bfloat16)
    grad_w_up = jnp.einsum("rd,rf->df", normed_mid, grad_upper, preferred_element_type=jnp.float32)
    mid_part = jnp.einsum("rf,df->rd", grad_upper, w_up, preferred_element_type=jnp.float32)
    grad_normed_mid = pair_sum(mid_part.astype(jnp.bfloat16))
    grad_mid, gain_mid, bias_mid = norm_back(middle, norm_gain[2], norm_bias[2], grad_normed_mid)
    grad_middle = grad_output + grad_mid
    grad_attn, gain_post, bias_post = norm_back(attn_total, norm_gain[1], norm_bias[1], grad_middle)
    grad_attn_low = grad_attn.astype(jnp.bfloat16)
    gain_last = grad_last[1]
    bias_last = grad_last[2]
    grad_w_out = jnp.einsum(
        "rd,rk->dk", grad_attn_low, attended, preferred_element_type=jnp.float32
    )
    grad_attended = jnp.einsum(
        "rd,kd->rk", grad_attn_low, w_out, preferred_element_type=jnp.float32
    ).astype(jnp.bfloat16)
    grad_queries, grad_keys, grad_values = attention_backward(
        queries, key_rows, value_rows, grad_attended, log_totals, valid_mask
    )
    grad_w_query = jnp.einsum(
        "rd,re->de", normed_in, grad_queries, preferred_element_type=jnp.float32
    )
    grad_w_key = jnp.einsum("rd,re->de", normed_in, grad_keys, preferred_element_type=jnp.float32)
    grad_w_value = jnp.einsum(
        "rd,re->de", normed_in, grad_values, preferred_element_type=jnp.float32
    )
    in_part = jnp.einsum("re,de->rd", grad_queries, w_query, preferred_element_type=jnp.float32)
    in_part = in_part + jnp.einsum(
        "re,de->rd", grad_keys, w_key, preferred_element_type=jnp.float32
    )
    in_part = in_part + jnp.einsum(
        "re,de->rd", grad_values, w_value, preferred_element_type=jnp.float32
    )
    grad_normed_in = pair_sum(in_part.astype(jnp.bfloat16))
    grad_in, gain_in, bias_in = norm_back(inputs, norm_gain[0], norm_bias[0], grad_normed_in)
    input_grad = (grad_middle + grad_in).astype(jnp.bfloat16)
    gain_grads = jnp.stack([gain_in, gain_post, gain_mid, gain_last])
    bias_grads = jnp.stack([bias_in, bias_post, bias_mid, bias_last])
    dp_size = lax.axis_size("dp")
    up_sum = scatter_sum(grad_w_up, dp_size)
    down_sum = scatter_sum(grad_w_down, dp_size).T
    norm_sum = scatter_sum(jnp.concatenate([gain_grads, bias_grads]).T, dp_size).T
    summed = (
        scatter_sum(grad_w_query, dp_size),
        scatter_sum(grad_w_key, dp_size),
        scatter_sum(grad_w_value, dp_size),
        scatter_sum(grad_w_out, dp_size).T,
        up_sum,
        down_sum,
        norm_sum[:4],
        norm_sum[4:],
    )
    return (
        result,
        input_grad,
        summed[0],
        summed[1],
        summed[2],
        summed[3],
        summed[4],
        summed[5],
        summed[6],
        summed[7],
    )


def solution(mesh):
    in_specs = (
        P("dp", None),
        P("dp"),
        P(None, "tensor"),
        P(None, "tensor"),
        P(None, "tensor"),
        P("tensor", None),
        P(None, "tensor"),
        P("tensor", None),
        P(),
        P(),
        P("dp", None),
    )
    out_specs = (
        P("dp", None),
        P("dp", None),
        P("dp", "tensor"),
        P("dp", "tensor"),
        P("dp", "tensor"),
        P("tensor", "dp"),
        P("dp", "tensor"),
        P("tensor", "dp"),
        P(None, "dp"),
        P(None, "dp"),
    )
    return jax.shard_map(
        on_device, mesh=mesh, in_specs=in_specs, out_specs=out_specs, check_vma=False
    )
```

```python
import functools

import jax
import jax.numpy as jnp
from jax import lax
from jax.experimental import pallas as pl
from jax.experimental.pallas import tpu as pltpu
from jax.sharding import PartitionSpec as P

HD = 64
LANES = 128
EPS = 1e-05
CHUNK = 256
BLOCK = 32
NEG = -1000000000.0
F32 = jnp.float32
BF16 = jnp.bfloat16
MESH = pl.DeviceIdType.MESH
NN = (((1,), (0,)), ((), ()))
NT = (((1,), (1,)), ((), ()))
TN = (((0,), (0,)), ((), ()))
ROOT = 0.7978845608028654
CUBE = 0.044715


def dot(left, right, dims):
    return lax.dot_general(left, right, dims, preferred_element_type=F32)


def row_mean(values):
    return jnp.sum(values, axis=-1, keepdims=True) * (1.0 / values.shape[-1])


def normalize(values):
    centered = values - row_mean(values)
    scale = lax.rsqrt(row_mean(centered * centered) + EPS)
    return centered * scale, scale


def norm_pull(hat, scale, gain, grad):
    weighed = grad * gain
    return scale * (weighed - row_mean(weighed) - hat * row_mean(weighed * hat))


def gelu_both(v):
    square = v * v
    tanh = jnp.tanh(v * (ROOT + (ROOT * CUBE) * square))
    half = 0.5 + 0.5 * tanh
    slope = half + (0.5 * v) * (1.0 - tanh * tanh) * (ROOT + (3.0 * ROOT * CUBE) * square)
    return v * half, slope


def lane_index(shape):
    return lax.broadcasted_iota(jnp.int32, shape, 1)


def head_of_pair(values, side):
    low = lane_index(values.shape) < HD
    return jnp.where(low if side == 0 else jnp.logical_not(low), values, jnp.zeros_like(values))


def join_pair(first, second):
    return jnp.where(lane_index(first.shape) < HD, first, second)


def fold_rows(values):
    return jnp.sum(values.reshape(-1, 8, values.shape[-1]), axis=0)


def layer_kernel(
    length_ref, tokens_hbm, wq_hbm, wk_hbm, wv_hbm, wo_hbm, wu_hbm, wd_hbm, gain_ref, bias_ref, cot_hbm,
    result_hbm, gmid_hbm, nin_hbm, att_hbm, nmid_hbm, hid_hbm, gffn_hbm, gup_hbm, gattn_hbm,
    gq_hbm, gk_hbm, gv_hbm, ngrad_ref,
    tokens, wq, wk, wv, wo, wu, wd, cot,
    nin, q, k, v, att, lse, own1, got1, own2, got2, got3, middle, hid, slope, gffn, gattn, gatt, gk, gv,
    stage, acc, load_sem, save_sem, stage_sem, send_sem, recv_sem,
):
    rows = tokens.shape[0]
    chunks = rows // CHUNK
    pairs = q.shape[1] // LANES
    inner = hid.shape[1]
    peer = {"tensor": 1 - lax.axis_index("tensor")}

    def load(index, source, target):
        return pltpu.make_async_copy(source, target, load_sem.at[index])

    def save(index, source, target):
        return pltpu.make_async_copy(source, target, save_sem.at[index])

    loads = [
        load(0, tokens_hbm, tokens), load(1, wq_hbm, wq), load(2, wk_hbm, wk), load(3, wv_hbm, wv),
        load(4, wo_hbm, wo), load(5, wu_hbm, wu), load(6, wd_hbm, wd), load(7, cot_hbm, cot),
    ]
    for copy in loads:
        copy.start()

    barrier = pltpu.get_barrier_semaphore()
    pl.semaphore_signal(barrier, inc=1, device_id=peer, device_id_type=MESH)
    pl.semaphore_wait(barrier, 1)

    def rows_of(c):
        return pl.ds(pl.multiple_of(c * CHUNK, CHUNK), CHUNK)

    def exchange(step, c, source, target):
        index = step * chunks + c
        return pltpu.make_async_remote_copy(
            src_ref=source.at[rows_of(c)],
            dst_ref=target.at[rows_of(c)],
            send_sem=send_sem.at[index],
            recv_sem=recv_sem.at[index],
            device_id=peer,
            device_id_type=MESH,
        )

    length = length_ref[0]

    def gain(j):
        return gain_ref[j : j + 1, :]

    def bias(j):
        return bias_ref[j : j + 1, :]

    def blocks(c, body):
        def step(b, carry):
            start = pl.multiple_of(c * CHUNK + b * BLOCK, BLOCK)
            body(start, pl.ds(start, BLOCK))
            return carry

        lax.fori_loop(0, CHUNK // BLOCK, step, 0)

    def real_rows(start):
        index = start + lax.broadcasted_iota(jnp.int32, (BLOCK, 1), 0)
        return jnp.where(index < length, 1.0, 0.0)

    acc[...] = jnp.zeros_like(acc)
    gk[...] = jnp.zeros_like(gk)
    gv[...] = jnp.zeros_like(gv)

    loads[0].wait()

    def project(c, carry):
        def norm_in(start, at):
            hat, _ = normalize(tokens[at, :].astype(F32))
            nin[at, :] = (hat * gain(0) + bias(0)).astype(BF16)

        blocks(c, norm_in)

        @pl.when(c == 0)
        def _():
            loads[1].wait()
            loads[2].wait()
            loads[3].wait()

        at = rows_of(c)
        normed = nin[at, :]
        q[at, :] = (dot(normed, wq[...], NN) * 0.125).astype(BF16)
        k[at, :] = dot(normed, wk[...], NN).astype(BF16)
        v[at, :] = dot(normed, wv[...], NN).astype(BF16)
        return carry

    lax.fori_loop(0, chunks, project, 0)
    save(0, nin, nin_hbm).start()
    loads[4].wait()

    key_bias = jnp.where(lane_index((1, rows)) < length, 0.0, NEG)

    def attend(c, carry):
        at = rows_of(c)

        def pair(p, carry):
            cols = pl.ds(pl.multiple_of(p * LANES, LANES), LANES)
            query, keys, values = q[at, cols], k[:, cols], v[:, cols]
            mixed = []
            logs = lse[at, :]
            for side in range(2):
                scores = dot(head_of_pair(query, side), keys, NT) + key_bias
                top = jnp.max(scores, axis=1, keepdims=True)
                weights = jnp.exp(scores - top)
                total = jnp.sum(weights, axis=1, keepdims=True)
                mixed.append(dot(weights.astype(BF16), values, NN) / total)
                logs = jnp.where(lane_index(logs.shape) == 2 * p + side, top + jnp.log(total), logs)
            lse[at, :] = logs
            att[at, cols] = join_pair(*mixed).astype(BF16)
            return carry

        lax.fori_loop(0, pairs, pair, 0)
        own1[at, :] = dot(att[at, :], wo[...], NN).astype(BF16)
        exchange(0, c, own1, got1).start()
        return carry

    lax.fori_loop(0, chunks, attend, 0)
    save(1, att, att_hbm).start()
    loads[5].wait()
    loads[6].wait()
    save(0, nin, nin_hbm).wait()
    nmid = nin

    def feed(c, carry):
        at = rows_of(c)
        exchange(0, c, own1, got1).wait_recv()

        def norms(start, at):
            hat, _ = normalize(own1[at, :].astype(F32) + got1[at, :].astype(F32))
            mid = tokens[at, :].astype(F32) + (hat * gain(1) + bias(1))
            middle[at, :] = mid
            hat, _ = normalize(mid)
            nmid[at, :] = (hat * gain(2) + bias(2)).astype(BF16)

        blocks(c, norms)
        normed = nmid[at, :]
        width = 512
        for n in range(inner // width):
            cols = pl.ds(n * width, width)
            value, grade = gelu_both(dot(normed, wu[:, cols], NN))
            hid[at, cols] = value.astype(BF16)
            slope[at, cols] = grade.astype(BF16)
        own2[at, :] = dot(hid[at, :], wd[...], NN).astype(BF16)
        exchange(1, c, own2, got2).start()
        return carry

    lax.fori_loop(0, chunks, feed, 0)
    save(2, nmid, nmid_hbm).start()
    save(3, hid, hid_hbm).start()
    loads[7].wait()

    def result_copy(c):
        slot = lax.rem(c, 2)
        return pltpu.make_async_copy(stage.at[slot], result_hbm.at[rows_of(c)], stage_sem.at[slot])

    def feed_back(c, carry):
        at = rows_of(c)
        slot = lax.rem(c, 2)
        exchange(1, c, own2, got2).wait_recv()

        @pl.when(c >= 2)
        def _():
            result_copy(c - 2).wait()

        def norms(start, at):
            hat, scale = normalize(own2[at, :].astype(F32) + got2[at, :].astype(F32))
            out = middle[at, :] + (hat * gain(3) + bias(3))
            stage[slot, pl.ds(pl.multiple_of(start - c * CHUNK, BLOCK), BLOCK), :] = out.astype(BF16)
            grad = cot[at, :].astype(F32) * real_rows(start)
            gffn[at, :] = norm_pull(hat, scale, gain(3), grad).astype(BF16)
            acc[2] += fold_rows(grad * hat)
            acc[5] += fold_rows(grad)

        blocks(c, norms)
        result_copy(c).start()
        grad = gffn[at, :]
        width = 512
        for n in range(inner // width):
            cols = pl.ds(n * width, width)
            wide = dot(grad, wd[cols, :], NT)
            slope[at, cols] = (wide * slope[at, cols].astype(F32)).astype(BF16)
        exchange(1, c, own2, got2).wait_send()
        own2[at, :] = dot(slope[at, :], wu[...], NT).astype(BF16)
        exchange(2, c, own2, got3).start()
        return carry

    lax.fori_loop(0, chunks, feed_back, 0)
    save(4, gffn, gffn_hbm).start()
    save(5, slope, gup_hbm).start()

    def attend_back(c, carry):
        at = rows_of(c)
        exchange(2, c, own2, got3).wait_recv()

        def norms(start, at):
            grad = own2[at, :].astype(F32) + got3[at, :].astype(F32)
            hat, scale = normalize(middle[at, :])
            out = cot[at, :].astype(F32) * real_rows(start)
            mid = out + norm_pull(hat, scale, gain(2), grad)
            acc[1] += fold_rows(grad * hat)
            acc[4] += fold_rows(grad)
            middle[at, :] = mid
            hat, scale = normalize(own1[at, :].astype(F32) + got1[at, :].astype(F32))
            gattn[at, :] = norm_pull(hat, scale, gain(1), mid).astype(BF16)
            acc[0] += fold_rows(mid * hat)
            acc[3] += fold_rows(mid)

        blocks(c, norms)
        gatt[...] = dot(gattn[at, :], wo[...], NT).astype(BF16)

        def pair(p, carry):
            cols = pl.ds(pl.multiple_of(p * LANES, LANES), LANES)
            query, keys, values, grad = q[at, cols], k[:, cols], v[:, cols], gatt[:, cols]
            through = grad.astype(F32) * att[at, cols].astype(F32)
            logs = lse[at, :]
            parts = []
            key_part = value_part = 0.0
            for side in range(2):
                one_query, one_grad = head_of_pair(query, side), head_of_pair(grad, side)
                log = jnp.sum(
                    jnp.where(lane_index(logs.shape) == 2 * p + side, logs, 0.0), axis=1, keepdims=True
                )
                weights = jnp.exp(dot(one_query, keys, NT) + key_bias - log)
                shift = jnp.sum(head_of_pair(through, side), axis=1, keepdims=True)
                slopes = (weights * (dot(one_grad, values, NT) - shift)).astype(BF16)
                parts.append(dot(slopes, keys, NN))
                key_part = key_part + dot(slopes, one_query, TN)
                value_part = value_part + dot(weights.astype(BF16), one_grad, TN)
            q[at, cols] = (join_pair(*parts) * 0.125).astype(BF16)
            gk[:, cols] += key_part
            gv[:, cols] += value_part
            return carry

        lax.fori_loop(0, pairs, pair, 0)
        return carry

    lax.fori_loop(0, chunks, attend_back, 0)
    k[...] = gk[...].astype(BF16)
    v[...] = gv[...].astype(BF16)
    tail = [
        save(6, middle, gmid_hbm), save(7, gattn, gattn_hbm), save(8, q, gq_hbm), save(9, k, gk_hbm), save(10, v, gv_hbm),
    ]
    for copy in tail:
        copy.start()
    ngrad_ref[...] = jnp.zeros_like(ngrad_ref)
    for j in range(6):
        ngrad_ref[j : j + 1, :] = jnp.sum(acc[j], axis=0, keepdims=True)
    save(1, att, att_hbm).wait()
    save(2, nmid, nmid_hbm).wait()
    save(3, hid, hid_hbm).wait()
    save(4, gffn, gffn_hbm).wait()
    save(5, slope, gup_hbm).wait()
    for copy in tail:
        copy.wait()
    for c in range(max(chunks - 2, 0), chunks):
        result_copy(c).wait()

    def drain(c, carry):
        exchange(0, c, own1, got1).wait_send()
        exchange(2, c, own2, got3).wait_send()
        return carry

    lax.fori_loop(0, chunks, drain, 0)


def run_layer(lengths, tokens, wq, wk, wv, wo, wu, wd, gains, biases, cot):
    rows, width = tokens.shape
    local, inner = wq.shape[1], wu.shape[1]
    chunks = rows // CHUNK
    shape = jax.ShapeDtypeStruct
    anywhere = pl.BlockSpec(memory_space=pl.ANY)
    vmem = pl.BlockSpec(memory_space=pltpu.VMEM)
    wide = (rows, width)
    thin = (rows, local)
    outs = [
        shape(wide, BF16), shape(wide, F32), shape(wide, BF16), shape(thin, BF16), shape(wide, BF16),
        shape((rows, inner), BF16), shape(wide, BF16), shape((rows, inner), BF16), shape(wide, BF16),
        shape(thin, BF16), shape(thin, BF16), shape(thin, BF16), shape((8, width), F32),
    ]
    scratch = [
        pltpu.VMEM(wide, BF16), pltpu.VMEM(wq.shape, BF16), pltpu.VMEM(wk.shape, BF16), pltpu.VMEM(wv.shape, BF16),
        pltpu.VMEM(wo.shape, BF16), pltpu.VMEM(wu.shape, BF16), pltpu.VMEM(wd.shape, BF16), pltpu.VMEM(wide, BF16),
        pltpu.VMEM(wide, BF16), pltpu.VMEM(thin, BF16), pltpu.VMEM(thin, BF16), pltpu.VMEM(thin, BF16),
        pltpu.VMEM(thin, BF16), pltpu.VMEM((rows, LANES), F32),
        pltpu.VMEM(wide, BF16), pltpu.VMEM(wide, BF16), pltpu.VMEM(wide, BF16), pltpu.VMEM(wide, BF16),
        pltpu.VMEM(wide, BF16), pltpu.VMEM(wide, F32), pltpu.VMEM((rows, inner), BF16), pltpu.VMEM((rows, inner), BF16),
        pltpu.VMEM(wide, BF16), pltpu.VMEM(wide, BF16), pltpu.VMEM((CHUNK, local), BF16),
        pltpu.VMEM(thin, F32), pltpu.VMEM(thin, F32),
        pltpu.VMEM((2, CHUNK, width), BF16), pltpu.VMEM((6, 8, width), F32),
        pltpu.SemaphoreType.DMA((8,)), pltpu.SemaphoreType.DMA((11,)), pltpu.SemaphoreType.DMA((2,)),
        pltpu.SemaphoreType.DMA((3 * chunks,)), pltpu.SemaphoreType.DMA((3 * chunks,)),
    ]
    return pl.pallas_call(
        layer_kernel,
        out_shape=outs,
        in_specs=[pl.BlockSpec(memory_space=pltpu.SMEM)] + [anywhere] * 7 + [vmem, vmem, anywhere],
        out_specs=[anywhere] * 12 + [vmem],
        scratch_shapes=scratch,
        compiler_params=pltpu.CompilerParams(
            collective_id=0, has_side_effects=True, vmem_limit_bytes=61 * 1024 * 1024
        ),
        name="layer",
    )(lengths, tokens, wq, wk, wv, wo, wu, wd, gains, biases, cot)


def pair_sum(part):
    other = lax.ppermute(part, "tensor", [(0, 1), (1, 0)])
    return part.astype(F32) + other.astype(F32)


def scatter_sum(grad, dp_size):
    index = lax.axis_index("dp")
    width = grad.shape[1]
    rows = grad.shape[0] // dp_size
    held = grad
    bit = 1
    while bit < dp_size:
        blocks = held.reshape(-1, 2, rows, width)
        side = (index // bit) % 2
        keep = lax.dynamic_index_in_dim(blocks, side, 1, keepdims=False)
        give = lax.dynamic_index_in_dim(blocks, 1 - side, 1, keepdims=False)
        come = lax.ppermute(give.astype(BF16), "dp", [(i, i ^ bit) for i in range(dp_size)])
        held = (keep.astype(F32) + come.astype(F32)).reshape(-1, width)
        bit *= 2
    return held


def on_device(tokens, lengths, wq, wk, wv, wo, wu, wd, gains, biases, cot):
    result, gmid, nin, att, nmid, hid, gffn, gup, gattn, gq, gk, gv, ngrad = run_layer(
        lengths, tokens, wq, wk, wv, wo, wu, wd, gains, biases, cot
    )
    part = dot(gq, wq, NT) + dot(gk, wk, NT) + dot(gv, wv, NT)
    grad = pair_sum(part.astype(BF16))
    hat, scale = normalize(tokens.astype(F32))
    input_grad = (gmid + norm_pull(hat, scale, gains[0:1], grad)).astype(BF16)
    gain_in, bias_in = jnp.sum(grad * hat, axis=0, keepdims=True), jnp.sum(grad, axis=0, keepdims=True)
    norms = jnp.concatenate([gain_in, ngrad[:3], bias_in, ngrad[3:6]])
    dp_size = lax.axis_size("dp")
    up = scatter_sum(dot(nmid, gup, TN), dp_size)
    down = scatter_sum(dot(gffn, hid, TN), dp_size).T
    out = scatter_sum(dot(gattn, att, TN), dp_size).T
    query = scatter_sum(dot(nin, gq, TN), dp_size)
    key = scatter_sum(dot(nin, gk, TN), dp_size)
    value = scatter_sum(dot(nin, gv, TN), dp_size)
    norm_sum = scatter_sum(norms.T, dp_size).T
    return result, input_grad, query, key, value, out, up, down, norm_sum[:4], norm_sum[4:]


def solution(mesh):
    in_specs = (
        P("dp", None), P("dp"), P(None, "tensor"), P(None, "tensor"), P(None, "tensor"), P("tensor", None),
        P(None, "tensor"), P("tensor", None), P(), P(), P("dp", None),
    )
    out_specs = (
        P("dp", None), P("dp", None), P("dp", "tensor"), P("dp", "tensor"), P("dp", "tensor"), P("tensor", "dp"),
        P("dp", "tensor"), P("tensor", "dp"), P(None, "dp"), P(None, "dp"),
    )
    return jax.shard_map(on_device, mesh=mesh, in_specs=in_specs, out_specs=out_specs, check_vma=False)
```

```python
import functools

import jax
import jax.numpy as jnp
from jax import lax
from jax.experimental import pallas as pl
from jax.experimental.pallas import tpu as pltpu
from jax.sharding import PartitionSpec as P

HD = 64
LANES = 128
EPS = 1e-05
CHUNK = 256
BLOCK = 32
NEG = -1000000000.0
F32 = jnp.float32
BF16 = jnp.bfloat16
MESH = pl.DeviceIdType.MESH
NN = (((1,), (0,)), ((), ()))
NT = (((1,), (1,)), ((), ()))
TN = (((0,), (0,)), ((), ()))
ROOT = 0.7978845608028654
CUBE = 0.044715
VMEM_BYTES = 61 * 1024 * 1024
SLOTS = {
    (2, 0): 0, (3, 0): 1, (0, 1): 4, (0, 2): 7, (0, 3): 10, (1, 1): 9, (1, 2): 12, (1, 3): 15, (2, 1): 14,
}


def dot(left, right, dims):
    return lax.dot_general(left, right, dims, preferred_element_type=F32)


def row_mean(values):
    return jnp.sum(values, axis=-1, keepdims=True) * (1.0 / values.shape[-1])


def normalize(values):
    centered = values - row_mean(values)
    scale = lax.rsqrt(row_mean(centered * centered) + EPS)
    return centered * scale, scale


def norm_pull(hat, scale, gain, grad):
    weighed = grad * gain
    return scale * (weighed - row_mean(weighed) - hat * row_mean(weighed * hat))


def gelu_both(v):
    square = v * v
    tanh = jnp.tanh(v * (ROOT + (ROOT * CUBE) * square))
    half = 0.5 + 0.5 * tanh
    slope = half + (0.5 * v) * (1.0 - tanh * tanh) * (ROOT + (3.0 * ROOT * CUBE) * square)
    return v * half, slope


def lane_index(shape):
    return lax.broadcasted_iota(jnp.int32, shape, 1)


def head_of_pair(values, side):
    low = lane_index(values.shape) < HD
    return jnp.where(low if side == 0 else jnp.logical_not(low), values, jnp.zeros_like(values))


def join_pair(first, second):
    return jnp.where(lane_index(first.shape) < HD, first, second)


def fold_rows(values):
    return jnp.sum(values.reshape(-1, 8, values.shape[-1]), axis=0)


def layer_kernel(
    dp_size,
    length_ref, tokens_hbm, wq_hbm, wk_hbm, wv_hbm, wo_hbm, wu_hbm, wd_hbm, gain_ref, bias_ref, cot_hbm,
    result_hbm, ingrad_hbm, nin_hbm, up_ref, down_ref, attn_ref, norm_ref,
    tokens, wq, wk, wv, wo, wu, wd, cot,
    nin, q, k, v, att, lse, own1, got1, own2, got2, got3, middle, hid, slope, gffn, gattn, gatt, gk, gv,
    stage, acc, norm_held, norm_box, norm_peer,
    load_sem, save_sem, stage_sem, send_sem, recv_sem, give_sem, take_sem, free_sem,
):
    rows = tokens.shape[0]
    chunks = rows // CHUNK
    local = q.shape[1]
    pairs = local // LANES
    inner = hid.shape[1]
    peer = {"tensor": 1 - lax.axis_index("tensor")}

    def load(index, source, target):
        return pltpu.make_async_copy(source, target, load_sem.at[index])

    def save(index, source, target):
        return pltpu.make_async_copy(source, target, save_sem.at[index])

    loads = [
        load(0, tokens_hbm, tokens), load(1, wq_hbm, wq), load(2, wk_hbm, wk), load(3, wv_hbm, wv),
        load(4, wo_hbm, wo), load(5, wu_hbm, wu), load(6, wd_hbm, wd), load(7, cot_hbm, cot),
    ]
    for copy in loads:
        copy.start()

    levels = dp_size.bit_length() - 1
    me = lax.axis_index("dp")
    partner, keep, give, half = [], [], [], []
    base, size = 0, dp_size
    for level in range(levels):
        bit = lax.rem(me // (1 << level), 2)
        partner.append({"dp": me + (1 << level) * (1 - 2 * bit)})
        size //= 2
        keep.append(base + bit * size)
        give.append(base + (1 - bit) * size)
        half.append(size)
        base = keep[-1]

    def position(index):
        return sum(lax.rem(index // (1 << b), 2) * (1 << (levels - 1 - b)) for b in range(levels))

    barrier = pltpu.get_barrier_semaphore()
    for other in [peer] + partner:
        pl.semaphore_signal(barrier, inc=1, device_id=other, device_id_type=MESH)
    pl.semaphore_wait(barrier, levels + 1)

    width = tokens.shape[1]
    blk = width // dp_size
    wide = 1024
    down_units = inner // wide
    units = 2 * down_units + 2
    norm_unit = units

    def held(unit):
        if unit < down_units:
            return wd.at[pl.ds(unit * width, width), :]
        if unit < 2 * down_units:
            return wu.at[:, pl.ds((unit - down_units) * wide, wide)]
        if unit < units:
            return hid.at[:, pl.ds((unit - 2 * down_units) * wide, wide)]
        return norm_held

    def inbox(unit, level):
        if unit == norm_unit:
            return norm_box.at[pl.ds(8 * (dp_size - 2 * half[level]), 8 * half[level]), :]
        count = half[level] * blk
        if unit >= 2 * down_units:
            start = width - 2 * count
            return slope.at[pl.ds(start, count), pl.ds((unit - 2 * down_units) * wide, wide)]
        if level == 0:
            room = got2 if unit < down_units else tokens
            return room.at[pl.ds((unit % down_units) * count, count), :]
        if level == 1:
            return gffn.at[pl.ds(unit * count, count), :]
        start = width // 4 - 2 * count
        return tokens.at[pl.ds(2 * down_units * start + unit * count, count), :]

    def block_of(unit):
        return 8 if unit == norm_unit else blk

    def hop(unit, level):
        rows_each = block_of(unit)
        index = unit * levels + level
        start = pl.multiple_of(give[level] * rows_each, 8)
        return pltpu.make_async_remote_copy(
            src_ref=held(unit).at[pl.ds(start, half[level] * rows_each), :],
            dst_ref=inbox(unit, level),
            send_sem=give_sem.at[index],
            recv_sem=take_sem.at[index],
            device_id=partner[level],
            device_id_type=MESH,
        )

    def release(level, phase):
        pl.semaphore_signal(
            free_sem.at[2 * level + phase], inc=1, device_id=partner[level], device_id_type=MESH
        )

    def send(unit, level):
        if unit == 0 or unit == 2 * down_units:
            pl.semaphore_wait(free_sem.at[2 * level + (0 if unit == 0 else 1)], 1)
        hop(unit, level).start()

    def final(unit):
        if unit < down_units:
            return down_ref.at[:, pl.ds(unit * wide, wide)]
        if unit < 2 * down_units:
            return up_ref.at[:, pl.ds((unit - down_units) * wide, wide)]
        if unit < units:
            return attn_ref.at[:, pl.ds((unit - 2 * down_units) * wide, wide)]
        return norm_ref

    def take(unit, level):
        hop(unit, level).wait_recv()
        rows_each = block_of(unit)
        count = half[level] * rows_each
        step_rows = min(count, 32)
        mine, came = held(unit), inbox(unit, level)
        last = level == levels - 1
        target = final(unit)

        def add(b, carry):
            here = pl.multiple_of(b * step_rows, step_rows)
            there = pl.multiple_of(keep[level] * rows_each + b * step_rows, 8)
            total = mine[pl.ds(there, step_rows), :].astype(F32) + came[pl.ds(here, step_rows), :].astype(F32)
            if last:
                target[pl.ds(here, step_rows), :] = total
            else:
                mine[pl.ds(there, step_rows), :] = total.astype(mine.dtype)
            return carry

        lax.fori_loop(0, count // step_rows, add, 0)
        if unit == 2 * down_units - 1 and level == 0:
            for other in range(2, levels):
                release(other, 0)
        if not last:
            send(unit, level + 1)

    def weight_grad(left, right, targets):
        span = 256

        def part(j, carry):
            cols = pl.ds(pl.multiple_of(j * span, span), span)
            grad = dot(left[:, cols], right[...], TN)
            for i in range(span // blk):
                start = pl.multiple_of(position(j * (span // blk) + i) * blk, 8)
                piece = grad[i * blk : (i + 1) * blk].astype(BF16)
                done = 0
                for ref, count in targets:
                    ref[pl.ds(start, blk), :] = piece[:, done : done + count]
                    done += count
            return carry

        lax.fori_loop(0, width // span, part, 0)

    def rows_of(c):
        return pl.ds(pl.multiple_of(c * CHUNK, CHUNK), CHUNK)

    def exchange(step, c, source, target):
        index = step * chunks + c
        return pltpu.make_async_remote_copy(
            src_ref=source.at[rows_of(c)],
            dst_ref=target.at[rows_of(c)],
            send_sem=send_sem.at[index],
            recv_sem=recv_sem.at[index],
            device_id=peer,
            device_id_type=MESH,
        )

    length = length_ref[0]

    def gain(j):
        return gain_ref[j : j + 1, :]

    def bias(j):
        return bias_ref[j : j + 1, :]

    def blocks(c, body):
        def step(b, carry):
            start = pl.multiple_of(c * CHUNK + b * BLOCK, BLOCK)
            body(start, pl.ds(start, BLOCK))
            return carry

        lax.fori_loop(0, CHUNK // BLOCK, step, 0)

    def real_rows(start):
        index = start + lax.broadcasted_iota(jnp.int32, (BLOCK, 1), 0)
        return jnp.where(index < length, 1.0, 0.0)

    acc[...] = jnp.zeros_like(acc)
    gk[...] = jnp.zeros_like(gk)
    gv[...] = jnp.zeros_like(gv)

    loads[0].wait()

    def project(c, carry):
        def norm_in(start, at):
            hat, _ = normalize(tokens[at, :].astype(F32))
            nin[at, :] = (hat * gain(0) + bias(0)).astype(BF16)

        blocks(c, norm_in)

        @pl.when(c == 0)
        def _():
            loads[1].wait()
            loads[2].wait()
            loads[3].wait()

        at = rows_of(c)
        normed = nin[at, :]
        q[at, :] = (dot(normed, wq[...], NN) * 0.125).astype(BF16)
        k[at, :] = dot(normed, wk[...], NN).astype(BF16)
        v[at, :] = dot(normed, wv[...], NN).astype(BF16)
        return carry

    lax.fori_loop(0, chunks, project, 0)
    save(0, nin, nin_hbm).start()
    loads[4].wait()

    key_bias = jnp.where(lane_index((1, rows)) < length, 0.0, NEG)

    def attend(c, carry):
        at = rows_of(c)

        def pair(p, carry):
            cols = pl.ds(pl.multiple_of(p * LANES, LANES), LANES)
            query, keys, values = q[at, cols], k[:, cols], v[:, cols]
            mixed = []
            logs = lse[at, :]
            for side in range(2):
                scores = dot(head_of_pair(query, side), keys, NT) + key_bias
                top = jnp.max(scores, axis=1, keepdims=True)
                weights = jnp.exp(scores - top)
                total = jnp.sum(weights, axis=1, keepdims=True)
                mixed.append(dot(weights.astype(BF16), values, NN) / total)
                logs = jnp.where(lane_index(logs.shape) == 2 * p + side, top + jnp.log(total), logs)
            lse[at, :] = logs
            att[at, cols] = join_pair(*mixed).astype(BF16)
            return carry

        lax.fori_loop(0, pairs, pair, 0)
        own1[at, :] = dot(att[at, :], wo[...], NN).astype(BF16)
        exchange(0, c, own1, got1).start()
        return carry

    lax.fori_loop(0, chunks, attend, 0)
    loads[5].wait()
    loads[6].wait()
    save(0, nin, nin_hbm).wait()
    nmid = nin

    def feed(c, carry):
        at = rows_of(c)
        exchange(0, c, own1, got1).wait_recv()

        def norms(start, at):
            hat, _ = normalize(own1[at, :].astype(F32) + got1[at, :].astype(F32))
            mid = tokens[at, :].astype(F32) + (hat * gain(1) + bias(1))
            middle[at, :] = mid
            hat, _ = normalize(mid)
            nmid[at, :] = (hat * gain(2) + bias(2)).astype(BF16)

        blocks(c, norms)
        normed = nmid[at, :]
        span = 512
        for n in range(inner // span):
            cols = pl.ds(n * span, span)
            value, grade = gelu_both(dot(normed, wu[:, cols], NN))
            hid[at, cols] = value.astype(BF16)
            slope[at, cols] = grade.astype(BF16)
        own2[at, :] = dot(hid[at, :], wd[...], NN).astype(BF16)
        exchange(1, c, own2, got2).start()
        return carry

    lax.fori_loop(0, chunks, feed, 0)
    loads[7].wait()

    def result_copy(c):
        slot = lax.rem(c, 2)
        return pltpu.make_async_copy(stage.at[slot], result_hbm.at[rows_of(c)], stage_sem.at[slot])

    def feed_back(c, carry):
        at = rows_of(c)
        slot = lax.rem(c, 2)
        exchange(1, c, own2, got2).wait_recv()

        @pl.when(c >= 2)
        def _():
            result_copy(c - 2).wait()

        def norms(start, at):
            hat, scale = normalize(own2[at, :].astype(F32) + got2[at, :].astype(F32))
            out = middle[at, :] + (hat * gain(3) + bias(3))
            stage[slot, pl.ds(pl.multiple_of(start - c * CHUNK, BLOCK), BLOCK), :] = out.astype(BF16)
            grad = cot[at, :].astype(F32) * real_rows(start)
            gffn[at, :] = norm_pull(hat, scale, gain(3), grad).astype(BF16)
            acc[2] += fold_rows(grad * hat)
            acc[5] += fold_rows(grad)

        blocks(c, norms)
        result_copy(c).start()
        grad = gffn[at, :]
        span = 512
        for n in range(inner // span):
            cols = pl.ds(n * span, span)
            grown = dot(grad, wd[cols, :], NT)
            slope[at, cols] = (grown * slope[at, cols].astype(F32)).astype(BF16)
        exchange(1, c, own2, got2).wait_send()
        own2[at, :] = dot(slope[at, :], wu[...], NT).astype(BF16)
        exchange(2, c, own2, got3).start()
        return carry

    lax.fori_loop(0, chunks, feed_back, 0)
    release(0, 0)

    weight_grad(gffn, hid, [(held(u), wide) for u in range(down_units)])
    release(1, 0)
    for u in range(down_units):
        send(u, 0)
    weight_grad(nmid, slope, [(held(u), wide) for u in range(down_units, 2 * down_units)])
    for level in range(levels):
        release(level, 1)
    for u in range(down_units, 2 * down_units):
        send(u, 0)
    nin_back = pltpu.make_async_copy(nin_hbm, nin, save_sem.at[1])
    nin_back.start()
    for u in range(down_units):
        take(u, 0)

    agenda, later = {}, []
    for u in range(2 * down_units):
        for level in range(0 if u >= down_units else 1, levels):
            slot = SLOTS.get((u, level), chunks * pairs)
            if slot < chunks * pairs:
                agenda.setdefault(slot, []).append((u, level))
            else:
                later.append((u, level))

    tokens_back = pltpu.make_async_copy(tokens_hbm, own1, save_sem.at[2])

    def attend_back(c, carry):
        at = rows_of(c)
        exchange(2, c, own2, got3).wait_recv()

        def norms(start, at):
            grad = own2[at, :].astype(F32) + got3[at, :].astype(F32)
            hat, scale = normalize(middle[at, :])
            out = cot[at, :].astype(F32) * real_rows(start)
            mid = out + norm_pull(hat, scale, gain(2), grad)
            acc[1] += fold_rows(grad * hat)
            acc[4] += fold_rows(grad)
            middle[at, :] = mid
            hat, scale = normalize(own1[at, :].astype(F32) + got1[at, :].astype(F32))
            gattn[at, :] = norm_pull(hat, scale, gain(1), mid).astype(BF16)
            acc[0] += fold_rows(mid * hat)
            acc[3] += fold_rows(mid)

        blocks(c, norms)

        @pl.when(c == chunks - 1)
        def _():
            pl.semaphore_signal(free_sem.at[2 * levels], inc=1, device_id=peer, device_id_type=MESH)
            for done in range(chunks):
                exchange(0, done, own1, got1).wait_send()
            tokens_back.start()

        gatt[...] = dot(gattn[at, :], wo[...], NT).astype(BF16)

        def pair(p, carry):
            for slot, work in agenda.items():

                @pl.when(c * pairs + p == slot)
                def _(work=work):
                    for unit, level in work:
                        take(unit, level)

            cols = pl.ds(pl.multiple_of(p * LANES, LANES), LANES)
            query, keys, values, grad = q[at, cols], k[:, cols], v[:, cols], gatt[:, cols]
            through = grad.astype(F32) * att[at, cols].astype(F32)
            logs = lse[at, :]
            parts = []
            key_part = value_part = 0.0
            for side in range(2):
                one_query, one_grad = head_of_pair(query, side), head_of_pair(grad, side)
                log = jnp.sum(
                    jnp.where(lane_index(logs.shape) == 2 * p + side, logs, 0.0), axis=1, keepdims=True
                )
                weights = jnp.exp(dot(one_query, keys, NT) + key_bias - log)
                shift = jnp.sum(head_of_pair(through, side), axis=1, keepdims=True)
                slopes = (weights * (dot(one_grad, values, NT) - shift)).astype(BF16)
                parts.append(dot(slopes, keys, NN))
                key_part = key_part + dot(slopes, one_query, TN)
                value_part = value_part + dot(weights.astype(BF16), one_grad, TN)
            q[at, cols] = (join_pair(*parts) * 0.125).astype(BF16)
            gk[:, cols] += key_part
            gv[:, cols] += value_part
            return carry

        lax.fori_loop(0, pairs, pair, 0)
        return carry

    lax.fori_loop(0, chunks, attend_back, 0)
    k[...] = gk[...].astype(BF16)
    v[...] = gv[...].astype(BF16)

    pl.semaphore_wait(free_sem.at[2 * levels], 1)

    def input_part(c, carry):
        at = rows_of(c)
        exchange(2, c, own2, got3).wait_send()
        part = dot(q[at, :], wq[...], NT) + dot(k[at, :], wk[...], NT) + dot(v[at, :], wv[...], NT)
        own2[at, :] = part.astype(BF16)
        exchange(3, c, own2, got3).start()
        return carry

    lax.fori_loop(0, chunks, input_part, 0)

    nin_back.wait()
    first = hid.at[:, pl.ds(0, local)]
    second = hid.at[:, pl.ds(local, local)]
    third = hid.at[:, pl.ds(2 * local, local)]
    fourth = hid.at[:, pl.ds(3 * local, local)]
    weight_grad(nin, q, [(first, local)])
    weight_grad(nin, k, [(second, local)])
    send(2 * down_units, 0)
    weight_grad(nin, v, [(third, local)])
    weight_grad(gattn, att, [(fourth, local)])
    send(2 * down_units + 1, 0)

    tokens_back.wait()
    back = own1

    def first_norm(c, carry):
        def sums(start, at):
            hat, _ = normalize(back[at, :].astype(F32))
            grad = own2[at, :].astype(F32)
            acc[6] += fold_rows(grad * hat)
            acc[7] += fold_rows(grad)

        blocks(c, sums)
        return carry

    lax.fori_loop(0, chunks, first_norm, 0)
    table = jnp.concatenate([jnp.sum(acc[j], axis=0, keepdims=True) for j in (6, 0, 1, 2, 7, 3, 4, 5)])
    for index in range(dp_size):
        tile, shift = divmod(index * blk, LANES)
        piece = table[:, tile * LANES : (tile + 1) * LANES]
        if shift:
            piece = pltpu.roll(piece, LANES - shift, 1)
        spot = int(format(index, "b").zfill(levels)[::-1], 2)
        norm_held[8 * spot : 8 * spot + 8, :] = piece
    send(norm_unit, 0)

    def grad_copy(c):
        slot = lax.rem(c, 2)
        return pltpu.make_async_copy(stage.at[slot], ingrad_hbm.at[rows_of(c)], stage_sem.at[slot])

    def input_grad(c):
        at = rows_of(c)
        slot = c % 2
        exchange(3, c, own2, got3).wait_recv()
        (result_copy if c < 2 else grad_copy)(chunks - 2 + c if c < 2 else c - 2).wait()

        def norms(start, at):
            grad = own2[at, :].astype(F32) + got3[at, :].astype(F32)
            hat, scale = normalize(back[at, :].astype(F32))
            total = middle[at, :] + norm_pull(hat, scale, gain(0), grad)
            stage[slot, pl.ds(pl.multiple_of(start - c * CHUNK, BLOCK), BLOCK), :] = total.astype(BF16)

        blocks(c, norms)
        grad_copy(c).start()

    late = [2 * down_units, 2 * down_units + 1]
    plan = [("take", u, l) for u, l in later if l <= 1] + [("take", u, 0) for u in late + [norm_unit]]
    plan += [("take", u, l) for u, l in later if l > 1]
    plan += [("take", norm_unit, l) for l in range(1, levels)]
    plan += [("grad", 0, 0), ("grad", 1, 0), ("take", late[0], 1)]
    plan += [("take", late[0], 2), ("grad", 2, 0), ("take", late[1], 1), ("take", late[0], 3)]
    plan += [("take", late[1], l) for l in range(2, levels)]
    plan += [("take", late[0], l) for l in range(4, levels)]
    plan += [("grad", c, 0) for c in range(3, chunks)]
    for kind, which, level in plan:
        if kind == "take":
            take(which, level)
            if which == norm_unit and level == levels - 1:
                tell = pltpu.make_async_remote_copy(
                    src_ref=norm_ref,
                    dst_ref=norm_peer,
                    send_sem=send_sem.at[4 * chunks],
                    recv_sem=recv_sem.at[4 * chunks],
                    device_id=peer,
                    device_id_type=MESH,
                )
                tell.start()
        else:
            input_grad(which)
    tell.wait()
    row = lax.broadcasted_iota(jnp.int32, norm_ref.shape, 0)
    norm_ref[...] += jnp.where(lax.rem(row, 4) == 0, norm_peer[...], 0.0)

    for c in range(max(chunks - 2, 0), chunks):
        grad_copy(c).wait()

    def drain(c, carry):
        exchange(3, c, own2, got3).wait_send()
        return carry

    lax.fori_loop(0, chunks, drain, 0)
    for unit in range(units + 1):
        for level in range(levels):
            hop(unit, level).wait_send()


def run_layer(lengths, tokens, wq, wk, wv, wo, wu, wd, gains, biases, cot):
    dp_size = lax.axis_size("dp")
    rows, width = tokens.shape
    local, inner = wq.shape[1], wu.shape[1]
    chunks = rows // CHUNK
    levels = dp_size.bit_length() - 1
    units = 2 * (inner // 1024) + 2
    shape = jax.ShapeDtypeStruct
    anywhere = pl.BlockSpec(memory_space=pl.ANY)
    vmem = pl.BlockSpec(memory_space=pltpu.VMEM)
    wide = (rows, width)
    thin = (rows, local)
    blk = width // dp_size
    outs = [
        shape(wide, BF16), shape(wide, BF16), shape(wide, BF16),
        shape((blk, inner), F32), shape((blk, inner), F32), shape((blk, 4 * local), F32), shape((8, LANES), F32),
    ]
    scratch = [
        pltpu.VMEM(wide, BF16), pltpu.VMEM(wq.shape, BF16), pltpu.VMEM(wk.shape, BF16), pltpu.VMEM(wv.shape, BF16),
        pltpu.VMEM(wo.shape, BF16), pltpu.VMEM(wu.shape, BF16), pltpu.VMEM(wd.shape, BF16), pltpu.VMEM(wide, BF16),
        pltpu.VMEM(wide, BF16), pltpu.VMEM(thin, BF16), pltpu.VMEM(thin, BF16), pltpu.VMEM(thin, BF16),
        pltpu.VMEM(thin, BF16), pltpu.VMEM((rows, LANES), F32),
        pltpu.VMEM(wide, BF16), pltpu.VMEM(wide, BF16), pltpu.VMEM(wide, BF16), pltpu.VMEM(wide, BF16),
        pltpu.VMEM(wide, BF16), pltpu.VMEM(wide, F32), pltpu.VMEM((rows, inner), BF16), pltpu.VMEM((rows, inner), BF16),
        pltpu.VMEM(wide, BF16), pltpu.VMEM(wide, BF16), pltpu.VMEM((CHUNK, local), BF16),
        pltpu.VMEM(thin, F32), pltpu.VMEM(thin, F32),
        pltpu.VMEM((2, CHUNK, width), BF16), pltpu.VMEM((8, 8, width), F32),
        pltpu.VMEM((8 * dp_size, LANES), F32), pltpu.VMEM((8 * dp_size, LANES), F32), pltpu.VMEM((8, LANES), F32),
        pltpu.SemaphoreType.DMA((8,)), pltpu.SemaphoreType.DMA((3,)), pltpu.SemaphoreType.DMA((2,)),
        pltpu.SemaphoreType.DMA((4 * chunks + 1,)), pltpu.SemaphoreType.DMA((4 * chunks + 1,)),
        pltpu.SemaphoreType.DMA(((units + 1) * levels,)), pltpu.SemaphoreType.DMA(((units + 1) * levels,)),
        pltpu.SemaphoreType.REGULAR((2 * levels + 1,)),
    ]
    return pl.pallas_call(
        functools.partial(layer_kernel, dp_size),
        out_shape=outs,
        in_specs=[pl.BlockSpec(memory_space=pltpu.SMEM)] + [anywhere] * 7 + [vmem, vmem, anywhere],
        out_specs=[anywhere] * 3 + [vmem] * 4,
        scratch_shapes=scratch,
        compiler_params=pltpu.CompilerParams(
            collective_id=0, has_side_effects=True, vmem_limit_bytes=VMEM_BYTES
        ),
        name="layer",
    )(lengths, tokens, wq, wk, wv, wo, wu, wd, gains, biases, cot)


def on_device(tokens, lengths, wq, wk, wv, wo, wu, wd, gains, biases, cot):
    local = wq.shape[1]
    result, input_grad, _, up, down, attn, norms = run_layer(
        lengths, tokens, wq, wk, wv, wo, wu, wd, gains, biases, cot
    )
    blk = up.shape[0]
    query, key, value, out = (attn[:, i * local : (i + 1) * local] for i in range(4))
    return result, input_grad, query, key, value, out.T, up, down.T, norms[:4, :blk], norms[4:, :blk]


def solution(mesh):
    in_specs = (
        P("dp", None), P("dp"), P(None, "tensor"), P(None, "tensor"), P(None, "tensor"), P("tensor", None),
        P(None, "tensor"), P("tensor", None), P(), P(), P("dp", None),
    )
    out_specs = (
        P("dp", None), P("dp", None), P("dp", "tensor"), P("dp", "tensor"), P("dp", "tensor"), P("tensor", "dp"),
        P("dp", "tensor"), P("tensor", "dp"), P(None, "dp"), P(None, "dp"),
    )
    return jax.shard_map(on_device, mesh=mesh, in_specs=in_specs, out_specs=out_specs, check_vma=False)
```

```python
import functools

import jax
import jax.numpy as jnp
from jax import lax
from jax.experimental import pallas as pl
from jax.experimental.pallas import tpu as pltpu
from jax.sharding import PartitionSpec as P

HD = 64
LANES = 128
EPS = 1e-05
CHUNK = 256
BLOCK = 128
NEG = -1000000000.0
F32 = jnp.float32
BF16 = jnp.bfloat16
MESH = pl.DeviceIdType.MESH
NN = (((1,), (0,)), ((), ()))
NT = (((1,), (1,)), ((), ()))
TN = (((0,), (0,)), ((), ()))
ROOT = 0.7978845608028654
CUBE = 0.044715
VMEM_BYTES = 61 * 1024 * 1024
SLOTS = {
    (2, 0): 0, (3, 0): 1, (0, 1): 5, (0, 2): 8, (0, 3): 12, (1, 1): 10, (1, 2): 13, (1, 3): 15, (2, 1): 14, (2, 2): 16,
    (2, 3): 16, (3, 1): 16,
}
EARLY = 17
PLAN = [
    ("take", 3, 2), ("grad", 0, 0), ("take", 3, 3), ("take", 4, 1), ("grad", 1, 0), ("take", 4, 2), ("take", 5, 1), ("take", 4, 3),
    ("grad", 2, 0), ("take", 6, 1), ("take", 5, 2), ("take", 6, 2), ("take", 6, 3), ("take", 5, 3), ("grad", 3, 0),
]


def dot(left, right, dims):
    return lax.dot_general(left, right, dims, preferred_element_type=F32)


def row_mean(values):
    return jnp.sum(values, axis=-1, keepdims=True) * (1.0 / values.shape[-1])


def normalize(values):
    centered = values - row_mean(values)
    scale = lax.rsqrt(row_mean(centered * centered) + EPS)
    return centered * scale, scale


def norm_pull(hat, scale, gain, grad):
    weighed = grad * gain
    return scale * (weighed - row_mean(weighed) - hat * row_mean(weighed * hat))


def gelu_both(v):
    square = v * v
    tanh = jnp.tanh(v * (ROOT + (ROOT * CUBE) * square))
    half = 0.5 + 0.5 * tanh
    slope = half + (0.5 * v) * (1.0 - tanh * tanh) * (ROOT + (3.0 * ROOT * CUBE) * square)
    return v * half, slope


def lane_index(shape):
    return lax.broadcasted_iota(jnp.int32, shape, 1)


def head_of_pair(values, side):
    low = lane_index(values.shape) < HD
    return jnp.where(low if side == 0 else jnp.logical_not(low), values, jnp.zeros_like(values))


def join_pair(first, second):
    return jnp.where(lane_index(first.shape) < HD, first, second)


def fold_rows(values):
    return jnp.sum(values.reshape(-1, 8, values.shape[-1]), axis=0)


def layer_kernel(
    dp_size,
    length_ref, tokens_hbm, wq_hbm, wk_hbm, wv_hbm, wo_hbm, wu_hbm, wd_hbm, gain_ref, bias_ref, cot_hbm,
    result_hbm, ingrad_hbm, nin_hbm, up_ref, down_ref, attn_ref, norm_ref,
    tokens, wq, wk, wv, wo, wu, wd, cot,
    nin, q, k, v, att, lse, attn_total, own2, got2, got3, middle, hid, slope, gffn, gattn, gatt, gk, gv,
    stage, acc, norm_held, norm_box, norm_peer,
    token_sem, load_sem, wo_sem, save_sem, stage_sem, send_sem, recv_sem, give_sem, take_sem, free_sem,
):
    rows = tokens.shape[0]
    chunks = rows // CHUNK
    local = q.shape[1]
    pairs = local // LANES
    inner = hid.shape[1]
    peer = {"tensor": 1 - lax.axis_index("tensor")}

    def load(index, source, target):
        return pltpu.make_async_copy(source, target, load_sem.at[index])

    def save(index, source, target):
        return pltpu.make_async_copy(source, target, save_sem.at[index])

    def token_load(c):
        at = pl.ds(pl.multiple_of(c * CHUNK, CHUNK), CHUNK)
        return pltpu.make_async_copy(tokens_hbm.at[at], tokens.at[at], token_sem.at[c])

    for c in range(chunks):
        token_load(c).start()
    loads = [
        load(0, wq_hbm, wq), load(1, wk_hbm, wk), load(2, wv_hbm, wv),
        load(3, wo_hbm, wo), load(4, wu_hbm, wu), load(5, wd_hbm, wd), load(6, cot_hbm, cot),
    ]
    for copy in loads[:3]:
        copy.start()

    levels = dp_size.bit_length() - 1
    me = lax.axis_index("dp")
    partner, keep, give, half = [], [], [], []
    base, size = 0, dp_size
    for level in range(levels):
        bit = lax.rem(me // (1 << level), 2)
        partner.append({"dp": me + (1 << level) * (1 - 2 * bit)})
        size //= 2
        keep.append(base + bit * size)
        give.append(base + (1 - bit) * size)
        half.append(size)
        base = keep[-1]

    def position(index):
        return sum(lax.rem(index // (1 << b), 2) * (1 << (levels - 1 - b)) for b in range(levels))

    barrier = pltpu.get_barrier_semaphore()
    for other in [peer] + partner:
        pl.semaphore_signal(barrier, inc=1, device_id=other, device_id_type=MESH)
    pl.semaphore_wait(barrier, levels + 1)

    width = tokens.shape[1]
    blk = width // dp_size

    core = lax.rem(me, 2)
    split = local // 2
    att_peer = gffn.at[:, pl.ds(0, local)]

    def wo_piece(which, side):
        start = pl.multiple_of(which * split, split)
        return gffn.at[pl.ds(pl.multiple_of(side * local + start, split), split), pl.ds(width - local, local)]

    def wo_cross(side):
        return pltpu.make_async_remote_copy(
            src_ref=wo_hbm.at[pl.ds(pl.multiple_of(core * split, split), split), pl.ds(side * local, local)],
            dst_ref=wo_piece(core, side),
            send_sem=wo_sem.at[side],
            recv_sem=wo_sem.at[2 + side],
            device_id=peer,
            device_id_type=MESH,
        )

    def wo_share(side):
        return pltpu.make_async_remote_copy(
            src_ref=wo_piece(core, side),
            dst_ref=wo_piece(core, side),
            send_sem=wo_sem.at[4 + side],
            recv_sem=wo_sem.at[6 + side],
            device_id=partner[0],
            device_id_type=MESH,
        )

    for side in range(2):
        wo_cross(side).start()
    wide = 1024
    down_units = inner // wide
    units = 2 * down_units + 2
    norm_unit = units

    def held(unit):
        if unit < down_units:
            return wd.at[pl.ds(unit * width, width), :]
        if unit < 2 * down_units:
            return wu.at[:, pl.ds((unit - down_units) * wide, wide)]
        if unit < units:
            return hid.at[:, pl.ds((unit - 2 * down_units) * wide, wide)]
        return norm_held

    def inbox(unit, level):
        if unit == norm_unit:
            return norm_box.at[pl.ds(8 * (dp_size - 2 * half[level]), 8 * half[level]), :]
        count = half[level] * blk
        if unit >= 2 * down_units:
            start = width - 2 * count
            return slope.at[pl.ds(start, count), pl.ds((unit - 2 * down_units) * wide, wide)]
        if level == 0:
            room = got2 if unit < down_units else tokens
            return room.at[pl.ds((unit % down_units) * count, count), :]
        if level == 1:
            return gffn.at[pl.ds(unit * count, count), :]
        start = width // 4 - 2 * count
        return tokens.at[pl.ds(2 * down_units * start + unit * count, count), :]

    def block_of(unit):
        return 8 if unit == norm_unit else blk

    def hop(unit, level):
        rows_each = block_of(unit)
        index = unit * levels + level
        start = pl.multiple_of(give[level] * rows_each, 8)
        return pltpu.make_async_remote_copy(
            src_ref=held(unit).at[pl.ds(start, half[level] * rows_each), :],
            dst_ref=inbox(unit, level),
            send_sem=give_sem.at[index],
            recv_sem=take_sem.at[index],
            device_id=partner[level],
            device_id_type=MESH,
        )

    def release(level, phase):
        pl.semaphore_signal(
            free_sem.at[2 * level + phase], inc=1, device_id=partner[level], device_id_type=MESH
        )

    def send(unit, level):
        if unit == 0 or unit == 2 * down_units:
            pl.semaphore_wait(free_sem.at[2 * level + (0 if unit == 0 else 1)], 1)
        hop(unit, level).start()

    def final(unit):
        if unit < down_units:
            return down_ref.at[:, pl.ds(unit * wide, wide)]
        if unit < 2 * down_units:
            return up_ref.at[:, pl.ds((unit - down_units) * wide, wide)]
        if unit < units:
            return attn_ref.at[:, pl.ds((unit - 2 * down_units) * wide, wide)]
        return norm_ref

    def take(unit, level):
        hop(unit, level).wait_recv()
        rows_each = block_of(unit)
        count = half[level] * rows_each
        step_rows = min(count, 32)
        mine, came = held(unit), inbox(unit, level)
        last = level == levels - 1
        target = final(unit)

        def add(b, carry):
            here = pl.multiple_of(b * step_rows, step_rows)
            there = pl.multiple_of(keep[level] * rows_each + b * step_rows, 8)
            total = mine[pl.ds(there, step_rows), :].astype(F32) + came[pl.ds(here, step_rows), :].astype(F32)
            if last:
                target[pl.ds(here, step_rows), :] = total
            else:
                mine[pl.ds(there, step_rows), :] = total.astype(mine.dtype)
            return carry

        lax.fori_loop(0, count // step_rows, add, 0)
        if unit == 2 * down_units - 1 and level == 0:
            for other in range(2, levels):
                release(other, 0)
        if not last:
            send(unit, level + 1)

    def weight_grad(left, groups):
        span = 256

        def part(j, carry):
            turned = left[:, pl.ds(pl.multiple_of(j * span, span), span)].T
            starts = [
                pl.multiple_of(position(j * (span // blk) + i) * blk, 8) for i in range(span // blk)
            ]
            for right, ref, at in groups:
                grad = dot(turned, right[...], NN).astype(BF16)
                for i, start in enumerate(starts):
                    ref[pl.ds(start, blk), pl.ds(at, grad.shape[1])] = grad[i * blk : (i + 1) * blk]
            return carry

        lax.fori_loop(0, width // span, part, 0)

    def rows_of(c):
        return pl.ds(pl.multiple_of(c * CHUNK, CHUNK), CHUNK)

    def exchange(step, c, source, target):
        index = step * chunks + c
        return pltpu.make_async_remote_copy(
            src_ref=source.at[rows_of(c)],
            dst_ref=target.at[rows_of(c)],
            send_sem=send_sem.at[index],
            recv_sem=recv_sem.at[index],
            device_id=peer,
            device_id_type=MESH,
        )

    length = length_ref[0]

    def gain(j):
        return gain_ref[j : j + 1, :]

    def bias(j):
        return bias_ref[j : j + 1, :]

    def blocks(c, body):
        def step(b, carry):
            start = pl.multiple_of(c * CHUNK + b * BLOCK, BLOCK)
            body(start, pl.ds(start, BLOCK))
            return carry

        lax.fori_loop(0, CHUNK // BLOCK, step, 0)

    def real_rows(start):
        index = start + lax.broadcasted_iota(jnp.int32, (BLOCK, 1), 0)
        return jnp.where(index < length, 1.0, 0.0)

    acc[...] = jnp.zeros_like(acc)
    gk[...] = jnp.zeros_like(gk)
    gv[...] = jnp.zeros_like(gv)

    def project(c, carry):
        token_load(c).wait()

        def norm_in(start, at):
            hat, _ = normalize(tokens[at, :].astype(F32))
            nin[at, :] = (hat * gain(0) + bias(0)).astype(BF16)

        blocks(c, norm_in)

        @pl.when(c == 0)
        def _():
            for copy in loads[:3]:
                copy.wait()
            for copy in loads[3:]:
                copy.start()

        at = rows_of(c)
        normed = nin[at, :]
        q[at, :] = (dot(normed, wq[...], NN) * 0.125).astype(BF16)
        k[at, :] = dot(normed, wk[...], NN).astype(BF16)
        v[at, :] = dot(normed, wv[...], NN).astype(BF16)
        return carry

    lax.fori_loop(0, chunks, project, 0)
    save(0, nin, nin_hbm).start()

    key_bias = jnp.where(lane_index((1, rows)) < length, 0.0, NEG)

    def attend(c, carry):
        at = rows_of(c)

        def pair(p, carry):
            cols = pl.ds(pl.multiple_of(p * LANES, LANES), LANES)
            query, keys, values = q[at, cols], k[:, cols], v[:, cols]
            mixed = []
            logs = lse[at, :]
            for side in range(2):
                scores = dot(head_of_pair(query, side), keys, NT) + key_bias
                top = jnp.max(scores, axis=1, keepdims=True)
                weights = jnp.exp(scores - top)
                total = jnp.sum(weights, axis=1, keepdims=True)
                mixed.append(dot(weights.astype(BF16), values, NN) / total)
                logs = jnp.where(lane_index(logs.shape) == 2 * p + side, top + jnp.log(total), logs)
            lse[at, :] = logs
            att[at, cols] = join_pair(*mixed).astype(BF16)
            return carry

        lax.fori_loop(0, pairs, pair, 0)
        exchange(0, c, att, att_peer).start()

        @pl.when(c == 0)
        def _():
            for side in range(2):
                wo_cross(side).wait_recv()
                wo_share(side).start()

        return carry

    lax.fori_loop(0, chunks, attend, 0)
    for copy in loads[3:6]:
        copy.wait()
    for side in range(2):
        wo_share(side).wait()
    save(0, nin, nin_hbm).wait()
    nmid = nin

    def feed(c, carry):
        at = rows_of(c)
        exchange(0, c, att, att_peer).wait_recv()
        ours = dot(att[at, :], wo[...], NN).astype(BF16).astype(F32)
        other = att_peer[at, :]
        for side in range(2):
            cols = pl.ds(side * local, local)
            weight = gffn[pl.ds(side * local, local), pl.ds(width - local, local)]
            theirs = dot(other, weight, NN).astype(BF16).astype(F32)
            attn_total[at, cols] = ours[:, side * local : (side + 1) * local] + theirs

        def norms(start, at):
            hat, _ = normalize(attn_total[at, :])
            mid = tokens[at, :].astype(F32) + (hat * gain(1) + bias(1))
            middle[at, :] = mid
            hat, _ = normalize(mid)
            nmid[at, :] = (hat * gain(2) + bias(2)).astype(BF16)

        blocks(c, norms)
        normed = nmid[at, :]
        span = 512
        for n in range(inner // span):
            cols = pl.ds(n * span, span)
            value, grade = gelu_both(dot(normed, wu[:, cols], NN))
            hid[at, cols] = value.astype(BF16)
            slope[at, cols] = grade.astype(BF16)
        own2[at, :] = dot(hid[at, :], wd[...], NN).astype(BF16)
        exchange(1, c, own2, got2).start()
        return carry

    lax.fori_loop(0, chunks, feed, 0)
    loads[6].wait()

    def result_copy(c):
        slot = lax.rem(c, 2)
        return pltpu.make_async_copy(stage.at[slot], result_hbm.at[rows_of(c)], stage_sem.at[slot])

    def feed_back(c, carry):
        at = rows_of(c)
        slot = lax.rem(c, 2)
        exchange(1, c, own2, got2).wait_recv()

        @pl.when(c >= 2)
        def _():
            result_copy(c - 2).wait()

        def norms(start, at):
            hat, scale = normalize(own2[at, :].astype(F32) + got2[at, :].astype(F32))
            out = middle[at, :] + (hat * gain(3) + bias(3))
            stage[slot, pl.ds(pl.multiple_of(start - c * CHUNK, BLOCK), BLOCK), :] = out.astype(BF16)
            grad = cot[at, :].astype(F32) * real_rows(start)
            gffn[at, :] = norm_pull(hat, scale, gain(3), grad).astype(BF16)
            acc[2] += fold_rows(grad * hat)
            acc[5] += fold_rows(grad)

        blocks(c, norms)
        result_copy(c).start()
        grad = gffn[at, :]
        span = 512
        for n in range(inner // span):
            cols = pl.ds(n * span, span)
            grown = dot(grad, wd[cols, :], NT)
            slope[at, cols] = (grown * slope[at, cols].astype(F32)).astype(BF16)
        exchange(1, c, own2, got2).wait_send()
        own2[at, :] = dot(slope[at, :], wu[...], NT).astype(BF16)
        exchange(2, c, own2, got3).start()
        return carry

    lax.fori_loop(0, chunks, feed_back, 0)
    release(0, 0)

    def parts(source, first_unit):
        return [(source.at[:, pl.ds(u * wide, wide)], held(first_unit + u), 0) for u in range(down_units)]

    weight_grad(gffn, parts(hid, 0))
    release(1, 0)
    for u in range(down_units):
        send(u, 0)
    weight_grad(nmid, parts(slope, down_units))
    for level in range(levels):
        release(level, 1)
    for u in range(down_units, 2 * down_units):
        send(u, 0)
    nin_back = pltpu.make_async_copy(nin_hbm, nin, save_sem.at[1])
    nin_back.start()
    for u in range(down_units):
        take(u, 0)

    agenda, early, later = {}, [], []
    for u in range(2 * down_units):
        for level in range(0 if u >= down_units else 1, levels):
            slot = SLOTS.get((u, level), EARLY)
            if slot < chunks * pairs:
                agenda.setdefault(slot, []).append((u, level))
            elif slot < EARLY:
                early.append((u, level))
            else:
                later.append((u, level))

    tokens_back = pltpu.make_async_copy(tokens_hbm, got2, save_sem.at[2])

    def attend_back(c, carry):
        at = rows_of(c)
        exchange(2, c, own2, got3).wait_recv()

        def norms(start, at):
            grad = own2[at, :].astype(F32) + got3[at, :].astype(F32)
            hat, scale = normalize(middle[at, :])
            out = cot[at, :].astype(F32) * real_rows(start)
            mid = out + norm_pull(hat, scale, gain(2), grad)
            acc[1] += fold_rows(grad * hat)
            acc[4] += fold_rows(grad)
            middle[at, :] = mid
            hat, scale = normalize(attn_total[at, :])
            gattn[at, :] = norm_pull(hat, scale, gain(1), mid).astype(BF16)
            acc[0] += fold_rows(mid * hat)
            acc[3] += fold_rows(mid)

        blocks(c, norms)

        @pl.when(c == chunks - 1)
        def _():
            pl.semaphore_signal(free_sem.at[2 * levels], inc=1, device_id=peer, device_id_type=MESH)
            tokens_back.start()

        gatt[...] = dot(gattn[at, :], wo[...], NT).astype(BF16)

        def pair(p, carry):
            for slot, work in agenda.items():

                @pl.when(c * pairs + p == slot)
                def _(work=work):
                    for unit, level in work:
                        take(unit, level)

            cols = pl.ds(pl.multiple_of(p * LANES, LANES), LANES)
            query, keys, values, grad = q[at, cols], k[:, cols], v[:, cols], gatt[:, cols]
            through = grad.astype(F32) * att[at, cols].astype(F32)
            logs = lse[at, :]
            parts = []
            key_part = value_part = 0.0
            for side in range(2):
                one_query, one_grad = head_of_pair(query, side), head_of_pair(grad, side)
                log = jnp.sum(
                    jnp.where(lane_index(logs.shape) == 2 * p + side, logs, 0.0), axis=1, keepdims=True
                )
                weights = jnp.exp(dot(one_query, keys, NT) + key_bias - log)
                shift = jnp.sum(head_of_pair(through, side), axis=1, keepdims=True)
                slopes = (weights * (dot(one_grad, values, NT) - shift)).astype(BF16)
                parts.append(dot(slopes, keys, NN))
                key_part = key_part + dot(slopes, one_query, TN)
                value_part = value_part + dot(weights.astype(BF16), one_grad, TN)
            q[at, cols] = (join_pair(*parts) * 0.125).astype(BF16)
            gk[:, cols] += key_part
            gv[:, cols] += value_part
            return carry

        lax.fori_loop(0, pairs, pair, 0)
        return carry

    lax.fori_loop(0, chunks, attend_back, 0)
    k[...] = gk[...].astype(BF16)
    v[...] = gv[...].astype(BF16)

    pl.semaphore_wait(free_sem.at[2 * levels], 1)

    def input_part(c, carry):
        at = rows_of(c)
        exchange(2, c, own2, got3).wait_send()
        part = dot(q[at, :], wq[...], NT) + dot(k[at, :], wk[...], NT) + dot(v[at, :], wv[...], NT)
        own2[at, :] = part.astype(BF16)
        exchange(3, c, own2, got3).start()
        return carry

    lax.fori_loop(0, chunks, input_part, 0)

    nin_back.wait()
    weight_grad(nin, [(q, hid, 0), (k, hid, local), (v, hid, 2 * local)])
    send(2 * down_units, 0)
    weight_grad(gattn, [(att, hid, 3 * local)])
    send(2 * down_units + 1, 0)

    for u, level in early:
        take(u, level)
    for u in (2 * down_units, 2 * down_units + 1):
        take(u, 0)
    tokens_back.wait()
    back = got2

    def first_norm(c, carry):
        def sums(start, at):
            hat, _ = normalize(back[at, :].astype(F32))
            grad = own2[at, :].astype(F32)
            acc[6] += fold_rows(grad * hat)
            acc[7] += fold_rows(grad)

        blocks(c, sums)
        return carry

    lax.fori_loop(0, chunks, first_norm, 0)
    table = jnp.concatenate([jnp.sum(acc[j], axis=0, keepdims=True) for j in (6, 0, 1, 2, 7, 3, 4, 5)])
    for index in range(dp_size):
        tile, shift = divmod(index * blk, LANES)
        piece = table[:, tile * LANES : (tile + 1) * LANES]
        if shift:
            piece = pltpu.roll(piece, LANES - shift, 1)
        spot = int(format(index, "b").zfill(levels)[::-1], 2)
        norm_held[8 * spot : 8 * spot + 8, :] = piece
    send(norm_unit, 0)
    take(norm_unit, 0)

    def grad_copy(c):
        slot = lax.rem(c, 2)
        return pltpu.make_async_copy(stage.at[slot], ingrad_hbm.at[rows_of(c)], stage_sem.at[slot])

    def input_grad(c):
        at = rows_of(c)
        slot = c % 2
        exchange(3, c, own2, got3).wait_recv()
        (result_copy if c < 2 else grad_copy)(chunks - 2 + c if c < 2 else c - 2).wait()

        def norms(start, at):
            grad = own2[at, :].astype(F32) + got3[at, :].astype(F32)
            hat, scale = normalize(back[at, :].astype(F32))
            total = middle[at, :] + norm_pull(hat, scale, gain(0), grad)
            stage[slot, pl.ds(pl.multiple_of(start - c * CHUNK, BLOCK), BLOCK), :] = total.astype(BF16)

        blocks(c, norms)
        grad_copy(c).start()

    late = [2 * down_units, 2 * down_units + 1]
    plan = [("take", u, l) for u, l in later]
    plan += [("take", norm_unit, l) for l in range(1, levels)]
    plan += [("take", u, l) for l in range(1, levels) for u in late]
    plan = PLAN if levels == 4 else plan + [("grad", c, 0) for c in range(chunks)]
    assert sorted(x for x in plan if x[0] == "take") == sorted(
        [("take", u, l) for u, l in later] + [("take", u, l) for u in late + [norm_unit] for l in range(1, levels)]
    )
    for kind, which, level in plan:
        if kind == "take":
            take(which, level)
            if which == norm_unit and level == levels - 1:
                tell = pltpu.make_async_remote_copy(
                    src_ref=norm_ref,
                    dst_ref=norm_peer,
                    send_sem=send_sem.at[4 * chunks],
                    recv_sem=recv_sem.at[4 * chunks],
                    device_id=peer,
                    device_id_type=MESH,
                )
                tell.start()
        else:
            input_grad(which)
    tell.wait()
    row = lax.broadcasted_iota(jnp.int32, norm_ref.shape, 0)
    norm_ref[...] += jnp.where(lax.rem(row, 4) == 0, norm_peer[...], 0.0)

    for c in range(max(chunks - 2, 0), chunks):
        grad_copy(c).wait()

    def drain(c, carry):
        exchange(0, c, att, att_peer).wait_send()
        exchange(3, c, own2, got3).wait_send()
        return carry

    lax.fori_loop(0, chunks, drain, 0)
    for side in range(2):
        wo_cross(side).wait_send()
    for unit in range(units + 1):
        for level in range(levels):
            hop(unit, level).wait_send()


def run_layer(lengths, tokens, wq, wk, wv, wo, wu, wd, gains, biases, cot):
    dp_size = lax.axis_size("dp")
    rows, width = tokens.shape
    local, inner = wq.shape[1], wu.shape[1]
    chunks = rows // CHUNK
    levels = dp_size.bit_length() - 1
    units = 2 * (inner // 1024) + 2
    shape = jax.ShapeDtypeStruct
    anywhere = pl.BlockSpec(memory_space=pl.ANY)
    vmem = pl.BlockSpec(memory_space=pltpu.VMEM)
    wide = (rows, width)
    thin = (rows, local)
    blk = width // dp_size
    outs = [
        shape(wide, BF16), shape(wide, BF16), shape(wide, BF16),
        shape((blk, inner), F32), shape((blk, inner), F32), shape((blk, 4 * local), F32), shape((8, LANES), F32),
    ]
    scratch = [
        pltpu.VMEM(wide, BF16), pltpu.VMEM(wq.shape, BF16), pltpu.VMEM(wk.shape, BF16), pltpu.VMEM(wv.shape, BF16),
        pltpu.VMEM(wo.shape, BF16), pltpu.VMEM(wu.shape, BF16), pltpu.VMEM(wd.shape, BF16), pltpu.VMEM(wide, BF16),
        pltpu.VMEM(wide, BF16), pltpu.VMEM(thin, BF16), pltpu.VMEM(thin, BF16), pltpu.VMEM(thin, BF16),
        pltpu.VMEM(thin, BF16), pltpu.VMEM((rows, LANES), F32),
        pltpu.VMEM(wide, F32), pltpu.VMEM(wide, BF16), pltpu.VMEM(wide, BF16), pltpu.VMEM(wide, BF16),
        pltpu.VMEM(wide, F32), pltpu.VMEM((rows, inner), BF16), pltpu.VMEM((rows, inner), BF16),
        pltpu.VMEM(wide, BF16), pltpu.VMEM(wide, BF16), pltpu.VMEM((CHUNK, local), BF16),
        pltpu.VMEM(thin, F32), pltpu.VMEM(thin, F32),
        pltpu.VMEM((2, CHUNK, width), BF16), pltpu.VMEM((8, 8, width), F32),
        pltpu.VMEM((8 * dp_size, LANES), F32), pltpu.VMEM((8 * dp_size, LANES), F32), pltpu.VMEM((8, LANES), F32),
        pltpu.SemaphoreType.DMA((chunks,)), pltpu.SemaphoreType.DMA((7,)), pltpu.SemaphoreType.DMA((8,)), pltpu.SemaphoreType.DMA((3,)), pltpu.SemaphoreType.DMA((2,)),
        pltpu.SemaphoreType.DMA((4 * chunks + 1,)), pltpu.SemaphoreType.DMA((4 * chunks + 1,)),
        pltpu.SemaphoreType.DMA(((units + 1) * levels,)), pltpu.SemaphoreType.DMA(((units + 1) * levels,)),
        pltpu.SemaphoreType.REGULAR((2 * levels + 1,)),
    ]
    return pl.pallas_call(
        functools.partial(layer_kernel, dp_size),
        out_shape=outs,
        in_specs=[pl.BlockSpec(memory_space=pltpu.SMEM)] + [anywhere] * 7 + [vmem, vmem, anywhere],
        out_specs=[anywhere] * 3 + [vmem] * 4,
        scratch_shapes=scratch,
        compiler_params=pltpu.CompilerParams(
            collective_id=0, has_side_effects=True, vmem_limit_bytes=VMEM_BYTES
        ),
        name="layer",
    )(lengths, tokens, wq, wk, wv, wo, wu, wd, gains, biases, cot)


def on_device(tokens, lengths, wq, wk, wv, wo, wu, wd, gains, biases, cot):
    local = wq.shape[1]
    result, input_grad, _, up, down, attn, norms = run_layer(
        lengths, tokens, wq, wk, wv, wo, wu, wd, gains, biases, cot
    )
    blk = up.shape[0]
    query, key, value, out = (attn[:, i * local : (i + 1) * local] for i in range(4))
    return result, input_grad, query, key, value, out.T, up, down.T, norms[:4, :blk], norms[4:, :blk]


def solution(mesh):
    in_specs = (
        P("dp", None), P("dp"), P(None, "tensor"), P(None, "tensor"), P(None, "tensor"), P("tensor", None),
        P(None, "tensor"), P("tensor", None), P(), P(), P("dp", None),
    )
    out_specs = (
        P("dp", None), P("dp", None), P("dp", "tensor"), P("dp", "tensor"), P("dp", "tensor"), P("tensor", "dp"),
        P("dp", "tensor"), P("tensor", "dp"), P(None, "dp"), P(None, "dp"),
    )
    return jax.shard_map(on_device, mesh=mesh, in_specs=in_specs, out_specs=out_specs, check_vma=False)
```

```python
import functools

import jax
import jax.numpy as jnp
from jax import lax
from jax.experimental import pallas as pl
from jax.experimental.pallas import tpu as pltpu
from jax.sharding import PartitionSpec as P

HD = 64
LANES = 128
EPS = 1e-05
CHUNK = 256
BLOCK = 128
NEG = -1000000000.0
F32 = jnp.float32
BF16 = jnp.bfloat16
MESH = pl.DeviceIdType.MESH
NN = (((1,), (0,)), ((), ()))
NT = (((1,), (1,)), ((), ()))
TN = (((0,), (0,)), ((), ()))
ROOT = 0.7978845608028654
CUBE = 0.044715
GROUP = 2
UNROLL = 2
VMEM_BYTES = 61 * 1024 * 1024
SLOTS = {(2, 0): 0, (3, 0): 1, (0, 1): 4, (2, 1): 5, (0, 2): 7, (1, 1): 7}
PLAN = [
    0, (3, 1), (2, 2), "project", (0, 3), (1, 2), 1, "out", (4, 0), 2, (5, 0), (6, 0), 3, "norm", (7, 0), (2, 3), (3, 2), (1, 3),
    ("grad", 0), (6, 1), (3, 3), (4, 1), ("grad", 1), (7, 1), (5, 1), (6, 2), (7, 2), (4, 2), (7, 3), (6, 3), (5, 2), ("grad", 2),
    (5, 3), (4, 3), ("grad", 3),
]


def dot(left, right, dims):
    return lax.dot_general(left, right, dims, preferred_element_type=F32)


def row_mean(values):
    return jnp.sum(values, axis=-1, keepdims=True) * (1.0 / values.shape[-1])


def normalize(values):
    centered = values - row_mean(values)
    scale = lax.rsqrt(row_mean(centered * centered) + EPS)
    return centered * scale, scale


def norm_pull(hat, scale, gain, grad):
    weighed = grad * gain
    return scale * (weighed - row_mean(weighed) - hat * row_mean(weighed * hat))


def gelu_both(v):
    square = v * v
    tanh = jnp.tanh(v * (ROOT + (ROOT * CUBE) * square))
    half = 0.5 + 0.5 * tanh
    slope = half + (0.5 * v) * (1.0 - tanh * tanh) * (ROOT + (3.0 * ROOT * CUBE) * square)
    return v * half, slope


def lane_index(shape):
    return lax.broadcasted_iota(jnp.int32, shape, 1)


def head_of_pair(values, side):
    low = lane_index(values.shape) < HD
    return jnp.where(low if side == 0 else jnp.logical_not(low), values, jnp.zeros_like(values))


def join_pair(first, second):
    return jnp.where(lane_index(first.shape) < HD, first, second)


def fold_rows(values):
    return jnp.sum(values.reshape(-1, 8, values.shape[-1]), axis=0)


def layer_kernel(
    dp_size,
    length_ref, tokens_hbm, wq_hbm, wk_hbm, wv_hbm, wo_hbm, wu_hbm, wd_hbm, gain_ref, bias_ref, cot_hbm,
    result_hbm, ingrad_hbm, nin_hbm, up_ref, down_ref, attn_ref, norm_ref,
    tokens, wq, wk, wv, wo, wu, wd, cot,
    nin, q, k, v, att, lse, attn_total, own2, got2, got3, middle, hid, slope, gffn, gattn, gatt, gk, gv,
    stage, acc, norm_held, norm_box, norm_peer,
    token_sem, load_sem, wo_sem, save_sem, stage_sem, send_sem, recv_sem, give_sem, take_sem, free_sem,
):
    rows = tokens.shape[0]
    chunks = rows // CHUNK
    local = q.shape[1]
    pairs = local // LANES
    inner = hid.shape[1]
    peer = {"tensor": 1 - lax.axis_index("tensor")}

    def load(index, source, target):
        return pltpu.make_async_copy(source, target, load_sem.at[index])

    def save(index, source, target):
        return pltpu.make_async_copy(source, target, save_sem.at[index])

    def token_load(c):
        at = pl.ds(pl.multiple_of(c * CHUNK, CHUNK), CHUNK)
        return pltpu.make_async_copy(tokens_hbm.at[at], tokens.at[at], token_sem.at[c])

    for c in range(chunks):
        token_load(c).start()
    loads = [
        load(0, wq_hbm, wq), load(1, wk_hbm, wk), load(2, wv_hbm, wv),
        load(3, wo_hbm, wo), load(4, wu_hbm, wu), load(5, wd_hbm, wd), load(6, cot_hbm, cot),
    ]
    for copy in loads[:3]:
        copy.start()

    levels = dp_size.bit_length() - 1
    me = lax.axis_index("dp")
    bits = [lax.rem(me // (1 << b), 2) for b in range(levels)]
    partner = [{"dp": me + (1 << b) * (1 - 2 * bits[b])} for b in range(levels)]
    half = [dp_size >> (level + 1) for level in range(levels)]
    routes = [list(range(levels)), [0] + list(range(2, levels)) + [1]]
    keep, give = [], []
    for route in routes:
        base, kept, given = 0, [], []
        for level in range(levels):
            kept.append(base + bits[route[level]] * half[level])
            given.append(base + (1 - bits[route[level]]) * half[level])
            base = kept[-1]
        keep.append(kept)
        give.append(given)

    def position(index, way):
        return sum(lax.rem(index // (1 << b), 2) * half[level] for level, b in enumerate(routes[way]))

    def fixed_position(index, way):
        return sum((index >> b) % 2 * half[level] for level, b in enumerate(routes[way]))

    barrier = pltpu.get_barrier_semaphore()
    for other in [peer] + partner:
        pl.semaphore_signal(barrier, inc=1, device_id=other, device_id_type=MESH)

    width = tokens.shape[1]
    blk = width // dp_size

    split = local // 4
    mine, far = lax.rem(me, 4), lax.rem(me + 2, 4)
    att_peer = gffn.at[:, pl.ds(0, local)]

    def wo_piece(which, side):
        start = pl.multiple_of(side * local + which * split, split)
        return gffn.at[pl.ds(start, split), pl.ds(width - local, local)]

    def wo_cross(side):
        return pltpu.make_async_remote_copy(
            src_ref=wo_hbm.at[pl.ds(pl.multiple_of(mine * split, split), split), pl.ds(side * local, local)],
            dst_ref=wo_piece(mine, side),
            send_sem=wo_sem.at[side],
            recv_sem=wo_sem.at[2 + side],
            device_id=peer,
            device_id_type=MESH,
        )

    def wo_share(step, side):
        which = far if step == 2 else mine
        return pltpu.make_async_remote_copy(
            src_ref=wo_piece(which, side),
            dst_ref=wo_piece(which, side),
            send_sem=wo_sem.at[4 * step + 4 + side],
            recv_sem=wo_sem.at[4 * step + 6 + side],
            device_id=partner[1] if step == 0 else partner[0],
            device_id_type=MESH,
        )

    wide = 1024
    count = inner // wide
    rows_at = lambda ref, start, size: ref.at[pl.ds(start, size), :]
    cols_at = lambda ref, start, size: ref.at[:, pl.ds(start, size)]
    table = [(rows_at(wd, u * width, width), cols_at(down_ref, u * wide, wide), None, 0) for u in range(count)]
    table += [
        (cols_at(wu, u * wide, wide), cols_at(up_ref, u * wide, wide), None, 1 if u == 0 else 0) for u in range(count)
    ]
    attn_first = 2 * count
    for start, size, way in ((0, 2 * local, 0), (2 * local, local, 0), (3 * local, local, 1)):
        table.append((cols_at(hid, start, size), cols_at(attn_ref, start, size), pl.ds(start, size), way))
    norm_unit = len(table)
    table.append((norm_held, norm_ref, None, 0))

    def held(unit):
        return table[unit][0]

    def inbox(unit, level):
        if unit == norm_unit:
            return norm_box.at[pl.ds(8 * (dp_size - 2 * half[level]), 8 * half[level]), :]
        size = half[level] * blk
        if unit >= attn_first:
            return slope.at[pl.ds(width - 2 * size, size), table[unit][2]]
        if level == 0:
            return rows_at(got2 if unit < count else tokens, (unit % count) * size, size)
        if level == 1:
            return rows_at(gffn, unit * size, size)
        return rows_at(tokens, 2 * count * (width // 4 - 2 * size) + unit * size, size)

    def block_of(unit):
        return 8 if unit == norm_unit else blk

    def hop(unit, level):
        way = table[unit][3]
        rows_each = block_of(unit)
        index = unit * levels + level
        start = pl.multiple_of(give[way][level] * rows_each, 8)
        return pltpu.make_async_remote_copy(
            src_ref=held(unit).at[pl.ds(start, half[level] * rows_each), :],
            dst_ref=inbox(unit, level),
            send_sem=give_sem.at[index],
            recv_sem=take_sem.at[index],
            device_id=partner[routes[way][level]],
            device_id_type=MESH,
        )

    def credit(unit, level):
        return free_sem.at[(2 * levels if unit >= attn_first else 0) + 2 * level + table[unit][3]]

    def release(which, level):
        for way in range(2):
            same = [u for u in which if table[u][3] == way]
            if same:
                pl.semaphore_signal(
                    credit(same[0], level), inc=len(same), device_id=partner[routes[way][level]], device_id_type=MESH
                )

    def send(unit, level):
        if unit != norm_unit:
            pl.semaphore_wait(credit(unit, level), 1)
        hop(unit, level).start()

    def take(unit, level):
        hop(unit, level).wait_recv()
        rows_each = block_of(unit)
        size = half[level] * rows_each
        step_rows = min(size, 32)
        ours, came = held(unit), inbox(unit, level)
        last = level == levels - 1
        target = table[unit][1]
        first = keep[table[unit][3]][level] * rows_each

        def add(b, carry):
            here = pl.multiple_of(b * step_rows, step_rows)
            there = pl.multiple_of(first + b * step_rows, 8)
            total = ours[pl.ds(there, step_rows), :].astype(F32) + came[pl.ds(here, step_rows), :].astype(F32)
            if last:
                target[pl.ds(here, step_rows), :] = total
            else:
                ours[pl.ds(there, step_rows), :] = total.astype(ours.dtype)
            return carry

        lax.fori_loop(0, size // step_rows, add, 0)
        if unit == 2 * count - 1 and level == 0:
            for other in range(2, levels):
                release(range(2 * count), other)
        if not last:
            send(unit, level + 1)

    def weight_grad(left, groups):
        span = 256

        def part(j, carry):
            turned = left[:, pl.ds(pl.multiple_of(j * span, span), span)].T
            for right, ref, at, way in groups:
                grad = dot(turned, right[...], NN).astype(BF16)
                for i in range(span // blk):
                    start = pl.multiple_of(position(j * (span // blk) + i, way) * blk, 8)
                    ref[pl.ds(start, blk), pl.ds(at, grad.shape[1])] = grad[i * blk : (i + 1) * blk]
            return carry

        lax.fori_loop(0, width // span, part, 0)

    def rows_of(c):
        return pl.ds(pl.multiple_of(c * CHUNK, CHUNK), CHUNK)

    def exchange(step, c, source, target):
        index = step * chunks + c
        return pltpu.make_async_remote_copy(
            src_ref=source.at[rows_of(c)],
            dst_ref=target.at[rows_of(c)],
            send_sem=send_sem.at[index],
            recv_sem=recv_sem.at[index],
            device_id=peer,
            device_id_type=MESH,
        )

    length = length_ref[0]

    def gain(j):
        return gain_ref[j : j + 1, :]

    def bias(j):
        return bias_ref[j : j + 1, :]

    def blocks(c, body):
        def step(b, carry):
            start = pl.multiple_of(c * CHUNK + b * BLOCK, BLOCK)
            body(start, pl.ds(start, BLOCK))
            return carry

        lax.fori_loop(0, CHUNK // BLOCK, step, 0)

    def real_rows(start):
        index = start + lax.broadcasted_iota(jnp.int32, (BLOCK, 1), 0)
        return jnp.where(index < length, 1.0, 0.0)

    acc[...] = jnp.zeros_like(acc)

    def project(c, carry):
        token_load(c).wait()

        def norm_in(start, at):
            hat, _ = normalize(tokens[at, :].astype(F32))
            nin[at, :] = (hat * gain(0) + bias(0)).astype(BF16)

        blocks(c, norm_in)

        if isinstance(c, int):
            for copy in loads[:3]:
                copy.wait()
            for copy in loads[3:]:
                copy.start()

        at = rows_of(c)
        normed = nin[at, :]
        q[at, :] = (dot(normed, wq[...], NN) * 0.125).astype(BF16)
        k[at, :] = dot(normed, wk[...], NN).astype(BF16)
        v[at, :] = dot(normed, wv[...], NN).astype(BF16)
        return carry

    project(0, 0)
    pl.semaphore_wait(barrier, levels + 1)
    for side in range(2):
        wo_cross(side).start()
    lax.fori_loop(1, chunks, project, 0)
    save(0, nin, nin_hbm).start()

    key_bias = jnp.where(lane_index((1, rows)) < length, 0.0, NEG)

    def attend(c, carry):
        at = rows_of(c)

        def pair(p, carry):
            cols = pl.ds(pl.multiple_of(p * LANES, LANES), LANES)
            query, keys, values = q[at, cols], k[:, cols], v[:, cols]
            mixed = []
            logs = lse[at, :]
            for side in range(2):
                scores = dot(head_of_pair(query, side), keys, NT) + key_bias
                top = jnp.max(scores, axis=1, keepdims=True)
                weights = jnp.exp(scores - top)
                total = jnp.sum(weights, axis=1, keepdims=True)
                mixed.append(dot(weights.astype(BF16), values, NN) / total)
                logs = jnp.where(lane_index(logs.shape) == 2 * p + side, top + jnp.log(total), logs)
            lse[at, :] = logs
            att[at, cols] = join_pair(*mixed).astype(BF16)
            return carry

        lax.fori_loop(0, pairs, pair, 0, unroll=UNROLL)
        exchange(0, c, att, att_peer).start()

        @pl.when(c == 0)
        def _():
            for side in range(2):
                wo_cross(side).wait_recv()
                wo_share(0, side).start()
                wo_share(1, side).start()

        @pl.when(c == chunks - 2)
        def _():
            for side in range(2):
                wo_share(0, side).wait_recv()
                wo_share(2, side).start()

        return carry

    lax.fori_loop(0, chunks, attend, 0)
    for copy in loads[3:6]:
        copy.wait()
    for side in range(2):
        wo_share(0, side).wait_send()
        wo_share(1, side).wait()
        wo_share(2, side).wait()
    save(0, nin, nin_hbm).wait()
    nmid = nin

    def feed(c, carry):
        at = rows_of(c)
        exchange(0, c, att, att_peer).wait_recv()
        ours = dot(att[at, :], wo[...], NN).astype(BF16).astype(F32)
        other = att_peer[at, :]
        for side in range(2):
            cols = pl.ds(side * local, local)
            weight = gffn[pl.ds(side * local, local), pl.ds(width - local, local)]
            theirs = dot(other, weight, NN).astype(BF16).astype(F32)
            attn_total[at, cols] = ours[:, side * local : (side + 1) * local] + theirs

        def norms(start, at):
            hat, _ = normalize(attn_total[at, :])
            mid = tokens[at, :].astype(F32) + (hat * gain(1) + bias(1))
            middle[at, :] = mid
            hat, _ = normalize(mid)
            nmid[at, :] = (hat * gain(2) + bias(2)).astype(BF16)

        blocks(c, norms)
        normed = nmid[at, :]
        span = 512
        for n in range(inner // span):
            cols = pl.ds(n * span, span)
            value, grade = gelu_both(dot(normed, wu[:, cols], NN))
            hid[at, cols] = value.astype(BF16)
            slope[at, cols] = grade.astype(BF16)
        own2[at, :] = dot(hid[at, :], wd[...], NN).astype(BF16)
        exchange(1, c, own2, got2).start()
        return carry

    lax.fori_loop(0, chunks, feed, 0)
    loads[6].wait()

    def result_copy(c):
        slot = lax.rem(c, 2)
        return pltpu.make_async_copy(stage.at[slot], result_hbm.at[rows_of(c)], stage_sem.at[slot])

    def feed_back(c, carry):
        at = rows_of(c)
        slot = lax.rem(c, 2)
        exchange(1, c, own2, got2).wait_recv()

        @pl.when(c >= 2)
        def _():
            result_copy(c - 2).wait()

        def norms(start, at):
            hat, scale = normalize(own2[at, :].astype(F32) + got2[at, :].astype(F32))
            out = middle[at, :] + (hat * gain(3) + bias(3))
            stage[slot, pl.ds(pl.multiple_of(start - c * CHUNK, BLOCK), BLOCK), :] = out.astype(BF16)
            grad = cot[at, :].astype(F32) * real_rows(start)
            gffn[at, :] = norm_pull(hat, scale, gain(3), grad).astype(BF16)
            acc[2] += fold_rows(grad * hat)
            acc[5] += fold_rows(grad)

        blocks(c, norms)
        result_copy(c).start()
        grad = gffn[at, :]
        span = 512
        for n in range(inner // span):
            cols = pl.ds(n * span, span)
            grown = dot(grad, wd[cols, :], NT)
            slope[at, cols] = (grown * slope[at, cols].astype(F32)).astype(BF16)
        exchange(1, c, own2, got2).wait_send()
        own2[at, :] = dot(slope[at, :], wu[...], NT).astype(BF16)
        exchange(2, c, own2, got3).start()
        return carry

    lax.fori_loop(0, chunks, feed_back, 0)
    release(range(2 * count), 0)

    def parts(source, first_unit):
        units = range(first_unit, first_unit + count)
        return [(cols_at(source, i * wide, wide), held(u), 0, table[u][3]) for i, u in enumerate(units)]

    weight_grad(gffn, parts(hid, 0))
    release(range(2 * count), 1)
    for u in range(count):
        send(u, 0)
    weight_grad(nmid, parts(slope, count))
    for level in range(levels):
        release(range(attn_first, norm_unit), level)
    for u in range(count, 2 * count):
        send(u, 0)
    nin_back = pltpu.make_async_copy(nin_hbm, nin, save_sem.at[1])
    nin_back.start()
    for u in range(count):
        take(u, 0)
    gk[...] = jnp.zeros_like(gk)
    gv[...] = jnp.zeros_like(gv)

    agenda = {}
    for (u, level), slot in sorted(SLOTS.items(), key=lambda item: item[1]):
        agenda.setdefault(slot, []).append((u, level))

    tokens_back = pltpu.make_async_copy(tokens_hbm, got2, save_sem.at[2])

    def attend_back(c, carry):
        at = rows_of(c)
        exchange(2, c, own2, got3).wait_recv()

        def norms(start, at):
            grad = own2[at, :].astype(F32) + got3[at, :].astype(F32)
            hat, scale = normalize(middle[at, :])
            out = cot[at, :].astype(F32) * real_rows(start)
            mid = out + norm_pull(hat, scale, gain(2), grad)
            acc[1] += fold_rows(grad * hat)
            acc[4] += fold_rows(grad)
            middle[at, :] = mid
            hat, scale = normalize(attn_total[at, :])
            gattn[at, :] = norm_pull(hat, scale, gain(1), mid).astype(BF16)
            acc[0] += fold_rows(mid * hat)
            acc[3] += fold_rows(mid)

        blocks(c, norms)

        @pl.when(c == chunks - 1)
        def _():
            pl.semaphore_signal(free_sem.at[4 * levels], inc=1, device_id=peer, device_id_type=MESH)
            tokens_back.start()

        gatt[...] = dot(gattn[at, :], wo[...], NT).astype(BF16)

        def pair(p):
            cols = pl.ds(pl.multiple_of(p * LANES, LANES), LANES)
            query, keys, values, grad = q[at, cols], k[:, cols], v[:, cols], gatt[:, cols]
            through = grad.astype(F32) * att[at, cols].astype(F32)
            logs = lse[at, :]
            parts = []
            key_part = value_part = 0.0
            for side in range(2):
                one_query, one_grad = head_of_pair(query, side), head_of_pair(grad, side)
                log = jnp.sum(
                    jnp.where(lane_index(logs.shape) == 2 * p + side, logs, 0.0), axis=1, keepdims=True
                )
                weights = jnp.exp(dot(one_query, keys, NT) + key_bias - log)
                shift = jnp.sum(head_of_pair(through, side), axis=1, keepdims=True)
                slopes = (weights * (dot(one_grad, values, NT) - shift)).astype(BF16)
                parts.append(dot(slopes, keys, NN))
                key_part = key_part + dot(one_query, slopes, TN)
                value_part = value_part + dot(one_grad, weights.astype(BF16), TN)
            q[at, cols] = (join_pair(*parts) * 0.125).astype(BF16)
            gk[cols, :] += key_part
            gv[cols, :] += value_part

        def some_pairs(h, carry):
            for slot, work in agenda.items():

                @pl.when(c * (pairs // GROUP) + h == slot)
                def _(work=work):
                    for unit, level in work:
                        take(unit, level)

            for i in range(GROUP):
                pair(h * GROUP + i)
            return carry

        lax.fori_loop(0, pairs // GROUP, some_pairs, 0)
        return carry

    lax.fori_loop(0, chunks, attend_back, 0)
    pl.semaphore_wait(free_sem.at[4 * levels], 1)
    back = got2

    def turn(c):
        at = rows_of(c)
        k[at, :] = gk[:, at].astype(BF16).T
        v[at, :] = gv[:, at].astype(BF16).T

    def input_part(c):
        at = rows_of(c)
        if c == 0:
            turn(c)
        exchange(2, c, own2, got3).wait_send()
        part = dot(q[at, :], wq[...], NT) + dot(k[at, :], wk[...], NT) + dot(v[at, :], wv[...], NT)
        own2[at, :] = part.astype(BF16)
        exchange(3, c, own2, got3).start()

    def project_grads():
        for c in range(1, chunks):
            turn(c)
        nin_back.wait()
        weight_grad(nin, [(q, hid, 0, 0), (k, hid, local, 0), (v, hid, 2 * local, 0)])
        send(attn_first, 0)
        send(attn_first + 1, 0)

    def out_grad():
        weight_grad(gattn, [(att, hid, 3 * local, table[attn_first + 2][3])])
        send(attn_first + 2, 0)

    def norm_grads():
        tokens_back.wait()

        def first_norm(c, carry):
            def sums(start, at):
                hat, _ = normalize(back[at, :].astype(F32))
                grad = own2[at, :].astype(F32)
                acc[6] += fold_rows(grad * hat)
                acc[7] += fold_rows(grad)

            blocks(c, sums)
            return carry

        lax.fori_loop(0, chunks, first_norm, 0)
        sums = jnp.concatenate([jnp.sum(acc[j], axis=0, keepdims=True) for j in (6, 0, 1, 2, 7, 3, 4, 5)])
        for index in range(dp_size):
            tile, shift = divmod(index * blk, LANES)
            piece = sums[:, tile * LANES : (tile + 1) * LANES]
            if shift:
                piece = pltpu.roll(piece, LANES - shift, 1)
            spot = 8 * fixed_position(index, 0)
            norm_held[spot : spot + 8, :] = piece
        send(norm_unit, 0)

    def grad_copy(c):
        slot = lax.rem(c, 2)
        return pltpu.make_async_copy(stage.at[slot], ingrad_hbm.at[rows_of(c)], stage_sem.at[slot])

    def input_grad(c):
        at = rows_of(c)
        slot = c % 2
        exchange(3, c, own2, got3).wait_recv()
        (result_copy if c < 2 else grad_copy)(chunks - 2 + c if c < 2 else c - 2).wait()

        def norms(start, at):
            grad = own2[at, :].astype(F32) + got3[at, :].astype(F32)
            hat, scale = normalize(back[at, :].astype(F32))
            total = middle[at, :] + norm_pull(hat, scale, gain(0), grad)
            stage[slot, pl.ds(pl.multiple_of(start - c * CHUNK, BLOCK), BLOCK), :] = total.astype(BF16)

        blocks(c, norms)
        grad_copy(c).start()

    tell = pltpu.make_async_remote_copy(
        src_ref=norm_ref,
        dst_ref=norm_peer,
        send_sem=send_sem.at[4 * chunks],
        recv_sem=recv_sem.at[4 * chunks],
        device_id=peer,
        device_id_type=MESH,
    )
    everything = [(u, level) for level in range(levels) for u in range(norm_unit + 1)]
    early = set(SLOTS) | {(u, 0) for u in range(count)}
    plan = PLAN
    if levels != 4:
        plan = [0, "project", 1, "out", 2, 3, "norm"] + [x for x in everything if x not in early]
        plan += [("grad", c) for c in range(chunks)]
    assert sorted(x for x in plan if isinstance(x, tuple) and x[0] != "grad") == sorted(set(everything) - early)
    for item in plan:
        if isinstance(item, int):
            input_part(item)
        elif item == "project":
            project_grads()
        elif item == "out":
            out_grad()
        elif item == "norm":
            norm_grads()
        elif item[0] == "grad":
            input_grad(item[1])
        else:
            take(*item)
            if item == (norm_unit, levels - 1):
                tell.start()
    tell.wait()
    row = lax.broadcasted_iota(jnp.int32, norm_ref.shape, 0)
    norm_ref[...] += jnp.where(lax.rem(row, 4) == 0, norm_peer[...], 0.0)

    for c in range(max(chunks - 2, 0), chunks):
        grad_copy(c).wait()

    def drain(c, carry):
        exchange(0, c, att, att_peer).wait_send()
        exchange(3, c, own2, got3).wait_send()
        return carry

    lax.fori_loop(0, chunks, drain, 0)
    for side in range(2):
        wo_cross(side).wait_send()
    for unit in range(norm_unit + 1):
        for level in range(levels):
            hop(unit, level).wait_send()


def run_layer(lengths, tokens, wq, wk, wv, wo, wu, wd, gains, biases, cot):
    dp_size = lax.axis_size("dp")
    rows, width = tokens.shape
    local, inner = wq.shape[1], wu.shape[1]
    chunks = rows // CHUNK
    levels = dp_size.bit_length() - 1
    units = 2 * (inner // 1024) + 4
    shape = jax.ShapeDtypeStruct
    anywhere = pl.BlockSpec(memory_space=pl.ANY)
    vmem = pl.BlockSpec(memory_space=pltpu.VMEM)
    wide = (rows, width)
    thin = (rows, local)
    blk = width // dp_size
    outs = [
        shape(wide, BF16), shape(wide, BF16), shape(wide, BF16),
        shape((blk, inner), F32), shape((blk, inner), F32), shape((blk, 4 * local), F32), shape((8, LANES), F32),
    ]
    scratch = [
        pltpu.VMEM(wide, BF16), pltpu.VMEM(wq.shape, BF16), pltpu.VMEM(wk.shape, BF16), pltpu.VMEM(wv.shape, BF16),
        pltpu.VMEM(wo.shape, BF16), pltpu.VMEM(wu.shape, BF16), pltpu.VMEM(wd.shape, BF16), pltpu.VMEM(wide, BF16),
        pltpu.VMEM(wide, BF16), pltpu.VMEM(thin, BF16), pltpu.VMEM(thin, BF16), pltpu.VMEM(thin, BF16),
        pltpu.VMEM(thin, BF16), pltpu.VMEM((rows, LANES), F32),
        pltpu.VMEM(wide, F32), pltpu.VMEM(wide, BF16), pltpu.VMEM(wide, BF16), pltpu.VMEM(wide, BF16),
        pltpu.VMEM(wide, F32), pltpu.VMEM((rows, inner), BF16), pltpu.VMEM((rows, inner), BF16),
        pltpu.VMEM(wide, BF16), pltpu.VMEM(wide, BF16), pltpu.VMEM((CHUNK, local), BF16),
        pltpu.VMEM((local, rows), F32), pltpu.VMEM((local, rows), F32),
        pltpu.VMEM((2, CHUNK, width), BF16), pltpu.VMEM((8, 8, width), F32),
        pltpu.VMEM((8 * dp_size, LANES), F32), pltpu.VMEM((8 * dp_size, LANES), F32), pltpu.VMEM((8, LANES), F32),
        pltpu.SemaphoreType.DMA((chunks,)), pltpu.SemaphoreType.DMA((7,)), pltpu.SemaphoreType.DMA((16,)), pltpu.SemaphoreType.DMA((3,)), pltpu.SemaphoreType.DMA((2,)),
        pltpu.SemaphoreType.DMA((4 * chunks + 1,)), pltpu.SemaphoreType.DMA((4 * chunks + 1,)),
        pltpu.SemaphoreType.DMA((units * levels,)), pltpu.SemaphoreType.DMA((units * levels,)),
        pltpu.SemaphoreType.REGULAR((4 * levels + 1,)),
    ]
    return pl.pallas_call(
        functools.partial(layer_kernel, dp_size),
        out_shape=outs,
        in_specs=[pl.BlockSpec(memory_space=pltpu.SMEM)] + [anywhere] * 7 + [vmem, vmem, anywhere],
        out_specs=[anywhere] * 3 + [vmem] * 4,
        scratch_shapes=scratch,
        compiler_params=pltpu.CompilerParams(
            collective_id=0, has_side_effects=True, vmem_limit_bytes=VMEM_BYTES
        ),
        name="layer",
    )(lengths, tokens, wq, wk, wv, wo, wu, wd, gains, biases, cot)


def finish_kernel(
    result_in, ingrad_in, up_in, down_in, attn_in, norm_in, result, ingrad, query, key, value, out, up, down, gain, bias
):
    local = query.shape[1]
    result[...] = result_in[...]
    ingrad[...] = ingrad_in[...]
    up[...] = up_in[...]
    down[...] = down_in[...]
    for i, ref in enumerate((query, key, value, out)):
        ref[...] = attn_in[:, i * local : (i + 1) * local]
    blk = gain.shape[1]
    gain[...] = norm_in[:4, :blk]
    bias[...] = norm_in[4:, :blk]


def on_device(tokens, lengths, wq, wk, wv, wo, wu, wd, gains, biases, cot):
    local, inner = wq.shape[1], wu.shape[1]
    result, input_grad, _, up, down, attn, norms = run_layer(
        lengths, tokens, wq, wk, wv, wo, wu, wd, gains, biases, cot
    )
    blk = up.shape[0]
    shape = jax.ShapeDtypeStruct
    steps = 2 if blk % 16 == 0 else 1

    def part(rows, columns):
        return pl.BlockSpec((rows // steps, columns), lambda i: (i, 0))

    def whole(*dims):
        return pl.BlockSpec(dims, lambda i: (0, 0))

    rows, width = result.shape
    result, input_grad, query, key, value, out, up, down, gain, bias = pl.pallas_call(
        finish_kernel,
        grid=(steps,),
        out_shape=[shape(result.shape, BF16), shape(result.shape, BF16)]
        + [shape((blk, local), F32)] * 4
        + [shape((blk, inner), F32)] * 2
        + [shape((4, blk), F32)] * 2,
        in_specs=[part(rows, width)] * 2 + [part(blk, inner)] * 2 + [part(blk, 4 * local), whole(8, LANES)],
        out_specs=[part(rows, width)] * 2 + [part(blk, local)] * 4 + [part(blk, inner)] * 2 + [whole(4, blk)] * 2,
        compiler_params=pltpu.CompilerParams(vmem_limit_bytes=VMEM_BYTES),
        name="finish",
    )(result, input_grad, up, down, attn, norms)
    return result, input_grad, query, key, value, out.T, up, down.T, gain, bias


def solution(mesh):
    in_specs = (
        P("dp", None), P("dp"), P(None, "tensor"), P(None, "tensor"), P(None, "tensor"), P("tensor", None),
        P(None, "tensor"), P("tensor", None), P(), P(), P("dp", None),
    )
    out_specs = (
        P("dp", None), P("dp", None), P("dp", "tensor"), P("dp", "tensor"), P("dp", "tensor"), P("tensor", "dp"),
        P("dp", "tensor"), P("tensor", "dp"), P(None, "dp"), P(None, "dp"),
    )
    return jax.shard_map(on_device, mesh=mesh, in_specs=in_specs, out_specs=out_specs, check_vma=False)
```

```python
import functools

import jax
import jax.numpy as jnp
from jax import lax
from jax.experimental import pallas as pl
from jax.experimental.pallas import tpu as pltpu
from jax.sharding import PartitionSpec as P

HD = 64
LANES = 128
EPS = 1e-05
CHUNK = 128
PROJECT = 256
BLOCK = 128
NEG = -1000000000.0
F32 = jnp.float32
BF16 = jnp.bfloat16
MESH = pl.DeviceIdType.MESH
NN = (((1,), (0,)), ((), ()))
NT = (((1,), (1,)), ((), ()))
TN = (((0,), (0,)), ((), ()))
ROOT = 0.7978845608028654
CUBE = 0.044715
UNROLL = 2
VMEM_BYTES = 61 * 1024 * 1024
WAYS = (0, 0, 1, 0, 0, 0, 0, 0)
SLOTS = {(2, 0): 1, (3, 0): 1, (0, 1): 4, (2, 1): 5, (0, 2): 7, (1, 1): 7}
PLAN = [
    ("part", 0, 1), ("part", 1, 1), (3, 1), "project", (2, 2), ("part", 2, 2), "out", (4, 0), (5, 0), (1, 2), (0, 3),
    ("part", 4, 2), ("part", 6, 2), "norm", (6, 0), (8, 0), (7, 0), (3, 2), (2, 3), ("grad", 0), ("grad", 1), (4, 1),
    (1, 3), ("grad", 2), (5, 1), (8, 1), (4, 2), (8, 2), (3, 3), ("grad", 3), (5, 2), (6, 1), (8, 3), (4, 3), ("grad", 4),
    (5, 3), (7, 1), (6, 2), ("grad", 5), (7, 2), (6, 3), ("grad", 6), (7, 3), ("grad", 7),
]


def dot(left, right, dims):
    return lax.dot_general(left, right, dims, preferred_element_type=F32)


def row_mean(values):
    return jnp.sum(values, axis=-1, keepdims=True) * (1.0 / values.shape[-1])


def normalize(values):
    centered = values - row_mean(values)
    scale = lax.rsqrt(row_mean(centered * centered) + EPS)
    return centered * scale, scale


def norm_pull(hat, scale, gain, grad):
    weighed = grad * gain
    return scale * (weighed - row_mean(weighed) - hat * row_mean(weighed * hat))


def gelu_both(v):
    square = v * v
    tanh = jnp.tanh(v * (ROOT + (ROOT * CUBE) * square))
    half = 0.5 + 0.5 * tanh
    slope = half + (0.5 * v) * (1.0 - tanh * tanh) * (ROOT + (3.0 * ROOT * CUBE) * square)
    return v * half, slope


def lane_index(shape):
    return lax.broadcasted_iota(jnp.int32, shape, 1)


def head_of_pair(values, side):
    low = lane_index(values.shape) < HD
    return jnp.where(low if side == 0 else jnp.logical_not(low), values, jnp.zeros_like(values))


def stack_pair(values):
    return jnp.concatenate([head_of_pair(values, 0), head_of_pair(values, 1)], axis=0)


def join_pair(stacked):
    first, second = jnp.split(stacked, 2, axis=0)
    return jnp.where(lane_index(first.shape) < HD, first, second)


def fold_rows(values):
    return jnp.sum(values.reshape(-1, 8, values.shape[-1]), axis=0)


def layer_kernel(
    dp_size,
    length_ref, tokens_hbm, wq_hbm, wk_hbm, wv_hbm, wo_hbm, wu_hbm, wd_hbm, gain_ref, bias_ref, cot_hbm,
    result_hbm, ingrad_hbm, nin_hbm, up_hbm, down_hbm, attn_hbm, norm_ref,
    tokens, wq, wk, wv, wo, wu, wd, cot,
    nin, q, k, v, att, lse, attn_total, own2, got2, got3, middle, hid, slope, gffn, gattn, gatt, gk, gv,
    stage, acc, up_ref, down_ref, attn_ref, norm_held, norm_box, norm_peer,
    final_sem, token_sem, load_sem, wo_sem, save_sem, stage_sem, send_sem, recv_sem, give_sem, take_sem, free_sem,
):
    rows = tokens.shape[0]
    chunks = rows // CHUNK
    local = q.shape[1]
    pairs = local // LANES
    inner = hid.shape[1]
    peer = {"tensor": 1 - lax.axis_index("tensor")}

    def load(index, source, target):
        return pltpu.make_async_copy(source, target, load_sem.at[index])

    def save(index, source, target):
        return pltpu.make_async_copy(source, target, save_sem.at[index])

    def span_of(c):
        return pl.ds(pl.multiple_of(c * PROJECT, PROJECT), PROJECT)

    def token_load(c):
        at = span_of(c)
        return pltpu.make_async_copy(tokens_hbm.at[at], tokens.at[at], token_sem.at[c])

    for c in range(rows // PROJECT):
        token_load(c).start()
    loads = [
        load(0, wq_hbm, wq), load(1, wk_hbm, wk), load(2, wv_hbm, wv),
        load(3, wo_hbm, wo), load(4, wu_hbm, wu), load(5, wd_hbm, wd), load(6, cot_hbm, cot),
    ]
    for copy in loads[:3]:
        copy.start()

    levels = dp_size.bit_length() - 1
    me = lax.axis_index("dp")
    bits = [lax.rem(me // (1 << b), 2) for b in range(levels)]
    partner = [{"dp": me + (1 << b) * (1 - 2 * bits[b])} for b in range(levels)]
    half = [dp_size >> (level + 1) for level in range(levels)]
    routes = [list(range(levels)), [0] + list(range(2, levels)) + [1]]
    keep, give = [], []
    for route in routes:
        base, kept, given = 0, [], []
        for level in range(levels):
            kept.append(base + bits[route[level]] * half[level])
            given.append(base + (1 - bits[route[level]]) * half[level])
            base = kept[-1]
        keep.append(kept)
        give.append(given)

    def position(index, way):
        return sum(lax.rem(index // (1 << b), 2) * half[level] for level, b in enumerate(routes[way]))

    def fixed_position(index, way):
        return sum((index >> b) % 2 * half[level] for level, b in enumerate(routes[way]))

    barrier = pltpu.get_barrier_semaphore()
    for other in [peer] + partner:
        pl.semaphore_signal(barrier, inc=1, device_id=other, device_id_type=MESH)

    width = tokens.shape[1]
    blk = width // dp_size

    split = local // 4
    mine, far = lax.rem(me, 4), lax.rem(me + 2, 4)
    att_peer = gffn.at[:, pl.ds(0, local)]

    def wo_piece(which, side):
        start = pl.multiple_of(side * local + which * split, split)
        return gffn.at[pl.ds(start, split), pl.ds(width - local, local)]

    def wo_cross(side):
        return pltpu.make_async_remote_copy(
            src_ref=wo_hbm.at[pl.ds(pl.multiple_of(mine * split, split), split), pl.ds(side * local, local)],
            dst_ref=wo_piece(mine, side),
            send_sem=wo_sem.at[side],
            recv_sem=wo_sem.at[2 + side],
            device_id=peer,
            device_id_type=MESH,
        )

    def wo_share(step, side):
        which = far if step == 2 else mine
        return pltpu.make_async_remote_copy(
            src_ref=wo_piece(which, side),
            dst_ref=wo_piece(which, side),
            send_sem=wo_sem.at[4 * step + 4 + side],
            recv_sem=wo_sem.at[4 * step + 6 + side],
            device_id=partner[1] if step == 0 else partner[0],
            device_id_type=MESH,
        )

    wide = 1024
    count = inner // wide
    rows_at = lambda ref, start, size: ref.at[pl.ds(start, size), :]
    cols_at = lambda ref, start, size: ref.at[:, pl.ds(start, size)]
    table = [(rows_at(wd, u * width, width), cols_at(down_ref, u * wide, wide), None, WAYS[u]) for u in range(count)]
    table += [
        (cols_at(wu, u * wide, wide), cols_at(up_ref, u * wide, wide), None, WAYS[count + u]) for u in range(count)
    ]
    attn_first = 2 * count
    for i in range(4):
        cols = pl.ds(i * local, local)
        table.append((hid.at[:, cols], attn_ref.at[:, cols], cols, WAYS[attn_first + i]))
    norm_unit = len(table)
    table.append((norm_held, norm_ref, None, 0))

    outputs = [cols_at(down_hbm, u * wide, wide) for u in range(count)]
    outputs += [cols_at(up_hbm, u * wide, wide) for u in range(count)]
    outputs += [cols_at(attn_hbm, i * local, local) for i in range(4)]

    def final_copy(unit):
        return pltpu.make_async_copy(table[unit][1], outputs[unit], final_sem.at[unit])

    def held(unit):
        return table[unit][0]

    def inbox(unit, level):
        if unit == norm_unit:
            return norm_box.at[pl.ds(8 * (dp_size - 2 * half[level]), 8 * half[level]), :]
        size = half[level] * blk
        if unit >= attn_first:
            return slope.at[pl.ds(width - 2 * size, size), table[unit][2]]
        if level == 0:
            return rows_at(got2 if unit < count else tokens, (unit % count) * size, size)
        if level == 1:
            return rows_at(gffn, unit * size, size)
        return rows_at(tokens, 2 * count * (width // 4 - 2 * size) + unit * size, size)

    def block_of(unit):
        return 8 if unit == norm_unit else blk

    def hop(unit, level):
        way = table[unit][3]
        rows_each = block_of(unit)
        index = unit * levels + level
        start = pl.multiple_of(give[way][level] * rows_each, 8)
        return pltpu.make_async_remote_copy(
            src_ref=held(unit).at[pl.ds(start, half[level] * rows_each), :],
            dst_ref=inbox(unit, level),
            send_sem=give_sem.at[index],
            recv_sem=take_sem.at[index],
            device_id=partner[routes[way][level]],
            device_id_type=MESH,
        )

    def credit(unit, level):
        return free_sem.at[(2 * levels if unit >= attn_first else 0) + 2 * level + table[unit][3]]

    def release(which, level):
        for way in range(2):
            same = [u for u in which if table[u][3] == way]
            if same:
                pl.semaphore_signal(
                    credit(same[0], level), inc=len(same), device_id=partner[routes[way][level]], device_id_type=MESH
                )

    def send(unit, level):
        if unit != norm_unit:
            pl.semaphore_wait(credit(unit, level), 1)
        hop(unit, level).start()

    def take(unit, level):
        hop(unit, level).wait_recv()
        rows_each = block_of(unit)
        size = half[level] * rows_each
        step_rows = min(size, 32)
        ours, came = held(unit), inbox(unit, level)
        last = level == levels - 1
        target = table[unit][1]
        first = keep[table[unit][3]][level] * rows_each

        def add(b, carry):
            here = pl.multiple_of(b * step_rows, step_rows)
            there = pl.multiple_of(first + b * step_rows, 8)
            total = ours[pl.ds(there, step_rows), :].astype(F32) + came[pl.ds(here, step_rows), :].astype(F32)
            if last:
                target[pl.ds(here, step_rows), :] = total
            else:
                ours[pl.ds(there, step_rows), :] = total.astype(ours.dtype)
            return carry

        lax.fori_loop(0, size // step_rows, add, 0)
        if last and unit != norm_unit:
            final_copy(unit).start()
        if unit == 2 * count - 1 and level == 0:
            for other in range(2, levels):
                release(range(2 * count), other)
        if not last:
            send(unit, level + 1)

    def weight_grad(left, groups):
        span = 256

        def part(j, carry):
            turned = left[:, pl.ds(pl.multiple_of(j * span, span), span)].T
            for right, ref, at, way in groups:
                grad = dot(turned, right[...], NN).astype(BF16)
                for i in range(span // blk):
                    start = pl.multiple_of(position(j * (span // blk) + i, way) * blk, 8)
                    ref[pl.ds(start, blk), pl.ds(at, grad.shape[1])] = grad[i * blk : (i + 1) * blk]
            return carry

        lax.fori_loop(0, width // span, part, 0)

    def rows_of(c):
        return pl.ds(pl.multiple_of(c * CHUNK, CHUNK), CHUNK)

    def exchange(step, c, source, target):
        index = step * chunks + c
        return pltpu.make_async_remote_copy(
            src_ref=source.at[rows_of(c)],
            dst_ref=target.at[rows_of(c)],
            send_sem=send_sem.at[index],
            recv_sem=recv_sem.at[index],
            device_id=peer,
            device_id_type=MESH,
        )

    length = length_ref[0]

    def gain(j):
        return gain_ref[j : j + 1, :]

    def bias(j):
        return bias_ref[j : j + 1, :]

    def blocks(c, body, size=CHUNK):
        def step(b, carry):
            start = pl.multiple_of(c * size + b * BLOCK, BLOCK)
            body(start, pl.ds(start, BLOCK))
            return carry

        lax.fori_loop(0, size // BLOCK, step, 0)

    def real_rows(start):
        index = start + lax.broadcasted_iota(jnp.int32, (BLOCK, 1), 0)
        return jnp.where(index < length, 1.0, 0.0)

    acc[...] = jnp.zeros_like(acc)

    def query_rows(at):
        q[at, :] = (dot(nin[at, :], wq[...], NN) * 0.125).astype(BF16)

    def norm_in(start, at):
        hat, _ = normalize(tokens[at, :].astype(F32))
        nin[at, :] = (hat * gain(0) + bias(0)).astype(BF16)

    for c in range(rows // PROJECT):
        token_load(c).wait()
        blocks(c, norm_in, PROJECT)
    for copy in loads[3:]:
        copy.start()
    pl.semaphore_wait(barrier, levels + 1)
    for side in range(2):
        wo_cross(side).start()
    for copy in loads[:3]:
        copy.wait()
    query_rows(span_of(0))
    for c in range(rows // (2 * PROJECT)):
        at = pl.ds(2 * PROJECT * c, 2 * PROJECT)
        normed = nin[at, :]
        k[at, :] = dot(normed, wk[...], NN).astype(BF16)
        v[at, :] = dot(normed, wv[...], NN).astype(BF16)
    save(0, nin, nin_hbm).start()

    key_bias = jnp.where(lane_index((1, rows)) < length, 0.0, NEG)

    def attend(c, carry):
        at = rows_of(c)

        ratio = PROJECT // CHUNK

        @pl.when(jnp.logical_and(lax.rem(c, ratio) == 0, c > 0))
        def _():
            query_rows(span_of(c // ratio))

        def pair(p, carry):
            cols = pl.ds(pl.multiple_of(p * LANES, LANES), LANES)
            keys, values = k[:, cols], v[:, cols]
            scores = dot(stack_pair(q[at, cols]), keys, NT) + key_bias
            top = jnp.max(scores, axis=1, keepdims=True)
            weights = jnp.exp(scores - top)
            total = jnp.sum(weights, axis=1, keepdims=True)
            mixed = dot(weights.astype(BF16), values, NN) / total
            first, second = jnp.split(top + jnp.log(total), 2, axis=0)
            logs = lse[at, :]
            lane = lane_index(logs.shape)
            lse[at, :] = jnp.where(lane == 2 * p, first, jnp.where(lane == 2 * p + 1, second, logs))
            att[at, cols] = join_pair(mixed).astype(BF16)
            return carry

        lax.fori_loop(0, pairs, pair, 0, unroll=UNROLL)
        exchange(0, c, att, att_peer).start()

        @pl.when(c == 2)
        def _():
            for side in range(2):
                wo_cross(side).wait_recv()
                wo_share(0, side).start()
                wo_share(1, side).start()

        @pl.when(c == chunks - 2)
        def _():
            for side in range(2):
                wo_share(0, side).wait_recv()
                wo_share(2, side).start()

        return carry

    lax.fori_loop(0, chunks, attend, 0)
    for copy in loads[3:6]:
        copy.wait()
    for side in range(2):
        wo_share(0, side).wait_send()
        wo_share(1, side).wait()
        wo_share(2, side).wait()
    save(0, nin, nin_hbm).wait()
    nmid = nin

    def feed(c, carry):
        at = rows_of(c)
        exchange(0, c, att, att_peer).wait_recv()
        ours = dot(att[at, :], wo[...], NN).astype(BF16).astype(F32)
        other = att_peer[at, :]
        for side in range(2):
            cols = pl.ds(side * local, local)
            weight = gffn[pl.ds(side * local, local), pl.ds(width - local, local)]
            theirs = dot(other, weight, NN).astype(BF16).astype(F32)
            attn_total[at, cols] = ours[:, side * local : (side + 1) * local] + theirs

        def norms(start, at):
            hat, scale = normalize(attn_total[at, :])
            attn_total[at, :] = hat
            lse[at, :] = jnp.where(lane_index((BLOCK, LANES)) == 2 * pairs, scale, lse[at, :])
            mid = tokens[at, :].astype(F32) + (hat * gain(1) + bias(1))
            middle[at, :] = mid
            hat, _ = normalize(mid)
            nmid[at, :] = (hat * gain(2) + bias(2)).astype(BF16)

        blocks(c, norms)
        normed = nmid[at, :]
        span = 512
        for n in range(inner // span):
            cols = pl.ds(n * span, span)
            value, grade = gelu_both(dot(normed, wu[:, cols], NN))
            hid[at, cols] = value.astype(BF16)
            slope[at, cols] = grade.astype(BF16)
        own2[at, :] = dot(hid[at, :], wd[...], NN).astype(BF16)
        exchange(1, c, own2, got2).start()
        return carry

    lax.fori_loop(0, chunks, feed, 0)
    loads[6].wait()

    def result_copy(c):
        slot = lax.rem(c, 2)
        return pltpu.make_async_copy(stage.at[slot], result_hbm.at[rows_of(c)], stage_sem.at[slot])

    def feed_back(c, carry):
        at = rows_of(c)
        slot = lax.rem(c, 2)
        exchange(1, c, own2, got2).wait_recv()

        @pl.when(c >= 2)
        def _():
            result_copy(c - 2).wait()

        def norms(start, at):
            hat, scale = normalize(own2[at, :].astype(F32) + got2[at, :].astype(F32))
            out = middle[at, :] + (hat * gain(3) + bias(3))
            stage[slot, pl.ds(pl.multiple_of(start - c * CHUNK, BLOCK), BLOCK), :] = out.astype(BF16)
            grad = cot[at, :].astype(F32) * real_rows(start)
            gffn[at, :] = norm_pull(hat, scale, gain(3), grad).astype(BF16)
            acc[2] += fold_rows(grad * hat)
            acc[5] += fold_rows(grad)
            hat, scale = normalize(middle[at, :])
            middle[at, :] = hat
            lse[at, :] = jnp.where(lane_index((BLOCK, LANES)) == 2 * pairs + 1, scale, lse[at, :])

        blocks(c, norms)
        result_copy(c).start()
        grad = gffn[at, :]
        span = 512
        for n in range(inner // span):
            cols = pl.ds(n * span, span)
            grown = dot(grad, wd[cols, :], NT)
            slope[at, cols] = (grown * slope[at, cols].astype(F32)).astype(BF16)
        exchange(1, c, own2, got2).wait_send()
        own2[at, :] = dot(slope[at, :], wu[...], NT).astype(BF16)
        exchange(2, c, own2, got3).start()
        return carry

    lax.fori_loop(0, chunks, feed_back, 0)
    release(range(2 * count), 0)

    def parts(source, first_unit):
        units = range(first_unit, first_unit + count)
        return [(cols_at(source, i * wide, wide), held(u), 0, table[u][3]) for i, u in enumerate(units)]

    weight_grad(gffn, parts(hid, 0))
    release(range(2 * count), 1)
    for u in range(count):
        send(u, 0)
    weight_grad(nmid, parts(slope, count))
    for level in range(levels):
        release(range(attn_first, norm_unit), level)
    for u in range(count, 2 * count):
        send(u, 0)
    nin_back = pltpu.make_async_copy(nin_hbm, nin, save_sem.at[1])
    nin_back.start()
    for u in range(count):
        take(u, 0)
    gk[...] = jnp.zeros_like(gk)
    gv[...] = jnp.zeros_like(gv)

    agenda = {}
    for (u, level), slot in sorted(SLOTS.items(), key=lambda item: item[1]):
        agenda.setdefault(slot, []).append((u, level))

    tokens_back = pltpu.make_async_copy(tokens_hbm, got2, save_sem.at[2])

    def attend_back(c, carry):
        at = rows_of(c)
        exchange(2, c, own2, got3).wait_recv()

        def norms(start, at):
            grad = own2[at, :].astype(F32) + got3[at, :].astype(F32)
            hat, scale = middle[at, :], lse[at, 2 * pairs + 1 : 2 * pairs + 2]
            out = cot[at, :].astype(F32) * real_rows(start)
            mid = out + norm_pull(hat, scale, gain(2), grad)
            acc[1] += fold_rows(grad * hat)
            acc[4] += fold_rows(grad)
            middle[at, :] = mid
            hat, scale = attn_total[at, :], lse[at, 2 * pairs : 2 * pairs + 1]
            gattn[at, :] = norm_pull(hat, scale, gain(1), mid).astype(BF16)
            acc[0] += fold_rows(mid * hat)
            acc[3] += fold_rows(mid)

        blocks(c, norms)

        @pl.when(c == chunks - 1)
        def _():
            pl.semaphore_signal(free_sem.at[4 * levels], inc=1, device_id=peer, device_id_type=MESH)
            tokens_back.start()

        gatt[...] = dot(gattn[at, :], wo[...], NT).astype(BF16)

        def pair(p):
            cols = pl.ds(p * LANES, LANES)
            keys, values, grad = k[:, cols], v[:, cols], gatt[:, cols]
            query, grads = stack_pair(q[at, cols]), stack_pair(grad)
            through = stack_pair(grad.astype(F32) * att[at, cols].astype(F32))
            shift = jnp.sum(through, axis=1, keepdims=True)
            logs = lse[at, :]
            log = jnp.concatenate([logs[:, 2 * p : 2 * p + 1], logs[:, 2 * p + 1 : 2 * p + 2]], axis=0)
            weights = jnp.exp(dot(query, keys, NT) + key_bias - log)
            slopes = (weights * (dot(grads, values, NT) - shift)).astype(BF16)
            q[at, cols] = (join_pair(dot(slopes, keys, NN)) * 0.125).astype(BF16)
            gk[cols, :] += dot(query, slopes, TN)
            gv[cols, :] += dot(grads, weights.astype(BF16), TN)

        for slot, work in agenda.items():

            @pl.when(c == slot)
            def _(work=work):
                for unit, level in work:
                    take(unit, level)

        for p in range(pairs):
            pair(p)
        return carry

    lax.fori_loop(0, chunks, attend_back, 0)
    pl.semaphore_wait(free_sem.at[4 * levels], 1)
    back = got2

    turned = set()

    def turn(c):
        if c not in turned:
            turned.add(c)
            at = rows_of(c)
            k[at, :] = gk[:, at].astype(BF16).T
            v[at, :] = gv[:, at].astype(BF16).T

    def input_part(first, number):
        at = pl.ds(first * CHUNK, number * CHUNK)
        for c in range(first, first + number):
            turn(c)
            exchange(2, c, own2, got3).wait_send()
        part = dot(q[at, :], wq[...], NT) + dot(k[at, :], wk[...], NT) + dot(v[at, :], wv[...], NT)
        own2[at, :] = part.astype(BF16)
        for c in range(first, first + number):
            exchange(3, c, own2, got3).start()

    def project_grads():
        for c in range(chunks):
            turn(c)
        nin_back.wait()
        weight_grad(nin, [(ref, hid, i * local, WAYS[attn_first + i]) for i, ref in enumerate((q, k, v))])
        for u in range(attn_first, attn_first + 3):
            send(u, 0)

    def out_grad():
        weight_grad(gattn, [(att, hid, 3 * local, WAYS[attn_first + 3])])
        send(attn_first + 3, 0)

    def norm_grads():
        tokens_back.wait()

        def first_norm(c, carry):
            def sums(start, at):
                hat, _ = normalize(back[at, :].astype(F32))
                grad = own2[at, :].astype(F32)
                acc[6] += fold_rows(grad * hat)
                acc[7] += fold_rows(grad)

            blocks(c, sums)
            return carry

        lax.fori_loop(0, chunks, first_norm, 0)
        sums = jnp.concatenate([jnp.sum(acc[j], axis=0, keepdims=True) for j in (6, 0, 1, 2, 7, 3, 4, 5)])
        for index in range(dp_size):
            tile, shift = divmod(index * blk, LANES)
            piece = sums[:, tile * LANES : (tile + 1) * LANES]
            if shift:
                piece = pltpu.roll(piece, LANES - shift, 1)
            spot = 8 * fixed_position(index, 0)
            norm_held[spot : spot + 8, :] = piece
        send(norm_unit, 0)

    def grad_copy(c):
        slot = lax.rem(c, 2)
        return pltpu.make_async_copy(stage.at[slot], ingrad_hbm.at[rows_of(c)], stage_sem.at[slot])

    def input_grad(c):
        at = rows_of(c)
        slot = c % 2
        exchange(3, c, own2, got3).wait_recv()
        (result_copy if c < 2 else grad_copy)(chunks - 2 + c if c < 2 else c - 2).wait()

        def norms(start, at):
            grad = own2[at, :].astype(F32) + got3[at, :].astype(F32)
            hat, scale = normalize(back[at, :].astype(F32))
            total = middle[at, :] + norm_pull(hat, scale, gain(0), grad)
            stage[slot, pl.ds(pl.multiple_of(start - c * CHUNK, BLOCK), BLOCK), :] = total.astype(BF16)

        blocks(c, norms)
        grad_copy(c).start()

    tell = pltpu.make_async_remote_copy(
        src_ref=norm_ref,
        dst_ref=norm_peer,
        send_sem=send_sem.at[4 * chunks],
        recv_sem=recv_sem.at[4 * chunks],
        device_id=peer,
        device_id_type=MESH,
    )
    everything = [(u, level) for level in range(levels) for u in range(norm_unit + 1)]
    early = set(SLOTS) | {(u, 0) for u in range(count)}
    plan = PLAN
    if levels != 4:
        plan = [("part", 0, 1), "project", "out", ("part", 1, chunks - 1), "norm"] + [x for x in everything if x not in early]
        plan += [("grad", c) for c in range(chunks)]
    assert sorted(x for x in plan if not isinstance(x[0], str)) == sorted(set(everything) - early)
    for item in plan:
        if item == "project":
            project_grads()
        elif item == "out":
            out_grad()
        elif item == "norm":
            norm_grads()
        elif item[0] == "part":
            input_part(*item[1:])
        elif item[0] == "grad":
            input_grad(item[1])
        else:
            take(*item)
            if item == (norm_unit, levels - 1):
                tell.start()
    tell.wait()
    row = lax.broadcasted_iota(jnp.int32, norm_ref.shape, 0)
    norm_ref[...] += jnp.where(lax.rem(row, 4) == 0, norm_peer[...], 0.0)

    for c in range(max(chunks - 2, 0), chunks):
        grad_copy(c).wait()

    def drain(c, carry):
        exchange(0, c, att, att_peer).wait_send()
        exchange(3, c, own2, got3).wait_send()
        return carry

    lax.fori_loop(0, chunks, drain, 0)
    for side in range(2):
        wo_cross(side).wait_send()
    for unit in range(norm_unit):
        final_copy(unit).wait()
    for unit in range(norm_unit + 1):
        for level in range(levels):
            hop(unit, level).wait_send()


def run_layer(lengths, tokens, wq, wk, wv, wo, wu, wd, gains, biases, cot):
    dp_size = lax.axis_size("dp")
    rows, width = tokens.shape
    local, inner = wq.shape[1], wu.shape[1]
    chunks = rows // CHUNK
    levels = dp_size.bit_length() - 1
    units = 2 * (inner // 1024) + 5
    shape = jax.ShapeDtypeStruct
    anywhere = pl.BlockSpec(memory_space=pl.ANY)
    vmem = pl.BlockSpec(memory_space=pltpu.VMEM)
    wide = (rows, width)
    thin = (rows, local)
    blk = width // dp_size
    outs = [
        shape(wide, BF16), shape(wide, BF16), shape(wide, BF16),
        shape((blk, inner), F32), shape((blk, inner), F32), shape((blk, 4 * local), F32), shape((8, LANES), F32),
    ]
    scratch = [
        pltpu.VMEM(wide, BF16), pltpu.VMEM(wq.shape, BF16), pltpu.VMEM(wk.shape, BF16), pltpu.VMEM(wv.shape, BF16),
        pltpu.VMEM(wo.shape, BF16), pltpu.VMEM(wu.shape, BF16), pltpu.VMEM(wd.shape, BF16), pltpu.VMEM(wide, BF16),
        pltpu.VMEM(wide, BF16), pltpu.VMEM(thin, BF16), pltpu.VMEM(thin, BF16), pltpu.VMEM(thin, BF16),
        pltpu.VMEM(thin, BF16), pltpu.VMEM((rows, LANES), F32),
        pltpu.VMEM(wide, F32), pltpu.VMEM(wide, BF16), pltpu.VMEM(wide, BF16), pltpu.VMEM(wide, BF16),
        pltpu.VMEM(wide, F32), pltpu.VMEM((rows, inner), BF16), pltpu.VMEM((rows, inner), BF16),
        pltpu.VMEM(wide, BF16), pltpu.VMEM(wide, BF16), pltpu.VMEM((CHUNK, local), BF16),
        pltpu.VMEM((local, rows), F32), pltpu.VMEM((local, rows), F32),
        pltpu.VMEM((2, CHUNK, width), BF16), pltpu.VMEM((8, 8, width), F32),
        pltpu.VMEM((blk, inner), F32), pltpu.VMEM((blk, inner), F32), pltpu.VMEM((blk, 4 * local), F32),
        pltpu.VMEM((8 * dp_size, LANES), F32), pltpu.VMEM((8 * dp_size, LANES), F32), pltpu.VMEM((8, LANES), F32),
        pltpu.SemaphoreType.DMA((units,)), pltpu.SemaphoreType.DMA((rows // PROJECT,)), pltpu.SemaphoreType.DMA((7,)), pltpu.SemaphoreType.DMA((16,)), pltpu.SemaphoreType.DMA((3,)), pltpu.SemaphoreType.DMA((2,)),
        pltpu.SemaphoreType.DMA((4 * chunks + 1,)), pltpu.SemaphoreType.DMA((4 * chunks + 1,)),
        pltpu.SemaphoreType.DMA((units * levels,)), pltpu.SemaphoreType.DMA((units * levels,)),
        pltpu.SemaphoreType.REGULAR((4 * levels + 1,)),
    ]
    return pl.pallas_call(
        functools.partial(layer_kernel, dp_size),
        out_shape=outs,
        in_specs=[pl.BlockSpec(memory_space=pltpu.SMEM)] + [anywhere] * 7 + [vmem, vmem, anywhere],
        out_specs=[anywhere] * 6 + [vmem],
        scratch_shapes=scratch,
        compiler_params=pltpu.CompilerParams(
            collective_id=0, has_side_effects=True, vmem_limit_bytes=VMEM_BYTES
        ),
        name="layer",
    )(lengths, tokens, wq, wk, wv, wo, wu, wd, gains, biases, cot)


def finish_kernel(
    result_in, ingrad_in, up_in, down_in, attn_in, norm_in, result, ingrad, query, key, value, out, up, down, gain, bias
):
    local = query.shape[1]
    result[...] = result_in[...]
    ingrad[...] = ingrad_in[...]
    up[...] = up_in[...]
    down[...] = down_in[...]
    for i, ref in enumerate((query, key, value, out)):
        ref[...] = attn_in[:, i * local : (i + 1) * local]
    blk = gain.shape[1]
    gain[...] = norm_in[:4, :blk]
    bias[...] = norm_in[4:, :blk]


def on_device(tokens, lengths, wq, wk, wv, wo, wu, wd, gains, biases, cot):
    local, inner = wq.shape[1], wu.shape[1]
    result, input_grad, _, up, down, attn, norms = run_layer(
        lengths, tokens, wq, wk, wv, wo, wu, wd, gains, biases, cot
    )
    blk = up.shape[0]
    shape = jax.ShapeDtypeStruct
    steps = 2 if blk % 16 == 0 else 1

    def part(rows, columns):
        return pl.BlockSpec((rows // steps, columns), lambda i: (i, 0))

    def whole(*dims):
        return pl.BlockSpec(dims, lambda i: (0, 0))

    rows, width = result.shape
    result, input_grad, query, key, value, out, up, down, gain, bias = pl.pallas_call(
        finish_kernel,
        grid=(steps,),
        out_shape=[shape(result.shape, BF16), shape(result.shape, BF16)]
        + [shape((blk, local), F32)] * 4
        + [shape((blk, inner), F32)] * 2
        + [shape((4, blk), F32)] * 2,
        in_specs=[part(rows, width)] * 2 + [part(blk, inner)] * 2 + [part(blk, 4 * local), whole(8, LANES)],
        out_specs=[part(rows, width)] * 2 + [part(blk, local)] * 4 + [part(blk, inner)] * 2 + [whole(4, blk)] * 2,
        compiler_params=pltpu.CompilerParams(vmem_limit_bytes=VMEM_BYTES),
        name="finish",
    )(result, input_grad, up, down, attn, norms)
    return result, input_grad, query, key, value, out.T, up, down.T, gain, bias


def solution(mesh):
    in_specs = (
        P("dp", None), P("dp"), P(None, "tensor"), P(None, "tensor"), P(None, "tensor"), P("tensor", None),
        P(None, "tensor"), P("tensor", None), P(), P(), P("dp", None),
    )
    out_specs = (
        P("dp", None), P("dp", None), P("dp", "tensor"), P("dp", "tensor"), P("dp", "tensor"), P("tensor", "dp"),
        P("dp", "tensor"), P("tensor", "dp"), P(None, "dp"), P(None, "dp"),
    )
    return jax.shard_map(on_device, mesh=mesh, in_specs=in_specs, out_specs=out_specs, check_vma=False)
```

```python
import functools

import jax
import jax.numpy as jnp
from jax import lax
from jax.experimental import pallas as pl
from jax.experimental.pallas import tpu as pltpu
from jax.sharding import PartitionSpec as P

HD = 64
LANES = 128
EPS = 1e-05
CHUNK = 128
PROJECT = 256
BLOCK = 128
NEG = -1000000000.0
F32 = jnp.float32
BF16 = jnp.bfloat16
MESH = pl.DeviceIdType.MESH
NN = (((1,), (0,)), ((), ()))
NT = (((1,), (1,)), ((), ()))
TN = (((0,), (0,)), ((), ()))
ROOT = 0.7978845608028654
CUBE = 0.044715
UNROLL = 2
VMEM_BYTES = 127 * 512 * 1024
WAYS = (0, 0, 1, 0, 0, 0, 0, 0)
SLOTS = {(2, 0): 1, (3, 0): 1, (0, 1): 4, (2, 1): 5, (0, 2): 7, (1, 1): 7}
PLAN = [
    ("part", 0, 1), ("part", 1, 1), (3, 1), "project", (2, 2), ("part", 2, 2), "out", (4, 0), (5, 0), (1, 2), (0, 3),
    ("part", 4, 2), ("part", 6, 2), "norm", (6, 0), (8, 0), (7, 0), (3, 2), (2, 3), ("grad", 0), ("grad", 1), (4, 1),
    (1, 3), ("grad", 2), (5, 1), (8, 1), (4, 2), (8, 2), (3, 3), ("grad", 3), (5, 2), (6, 1), (8, 3), (4, 3), ("grad", 4),
    (5, 3), (7, 1), (6, 2), ("grad", 5), (7, 2), (6, 3), ("grad", 6), (7, 3), ("grad", 7),
]


def dot(left, right, dims):
    return lax.dot_general(left, right, dims, preferred_element_type=F32)


def row_mean(values):
    return jnp.sum(values, axis=-1, keepdims=True) * (1.0 / values.shape[-1])


def normalize(values):
    centered = values - row_mean(values)
    scale = lax.rsqrt(row_mean(centered * centered) + EPS)
    return centered * scale, scale


def norm_pull(hat, scale, gain, grad):
    weighed = grad * gain
    return scale * (weighed - row_mean(weighed) - hat * row_mean(weighed * hat))


def gelu_both(v):
    square = v * v
    tanh = jnp.tanh(v * (ROOT + (ROOT * CUBE) * square))
    half = 0.5 + 0.5 * tanh
    slope = half + (0.5 * v) * (1.0 - tanh * tanh) * (ROOT + (3.0 * ROOT * CUBE) * square)
    return v * half, slope


def lane_index(shape):
    return lax.broadcasted_iota(jnp.int32, shape, 1)


def head_of_pair(values, side):
    low = lane_index(values.shape) < HD
    return jnp.where(low if side == 0 else jnp.logical_not(low), values, jnp.zeros_like(values))


def stack_pair(values):
    return jnp.concatenate([head_of_pair(values, 0), head_of_pair(values, 1)], axis=0)


def join_pair(stacked):
    first, second = jnp.split(stacked, 2, axis=0)
    return jnp.where(lane_index(first.shape) < HD, first, second)


def fold_rows(values):
    return jnp.sum(values.reshape(-1, 8, values.shape[-1]), axis=0)


def layer_kernel(
    dp_size,
    length_ref, tokens_hbm, wq_hbm, wk_hbm, wv_hbm, wo_hbm, wu_hbm, wd_hbm, gain_ref, bias_ref, cot_hbm,
    result_ref, ingrad_ref, nin_hbm, up_ref, down_ref, attn_ref, norm_ref,
    tokens, wq, wk, wv, wo, wu, wd, cot,
    nin, q, k, v, att, lse, attn_total, own2, got2, got3, middle, hid, slope, gffn, gattn, gatt, gk, gv,
    acc, norm_held, norm_box, norm_peer,
    token_sem, load_sem, wo_sem, save_sem, send_sem, recv_sem, give_sem, take_sem, free_sem,
):
    rows = tokens.shape[0]
    chunks = rows // CHUNK
    local = q.shape[1]
    pairs = local // LANES
    inner = hid.shape[1]
    peer = {"tensor": 1 - lax.axis_index("tensor")}

    def load(index, source, target):
        return pltpu.make_async_copy(source, target, load_sem.at[index])

    def save(index, source, target):
        return pltpu.make_async_copy(source, target, save_sem.at[index])

    def span_of(c):
        return pl.ds(pl.multiple_of(c * PROJECT, PROJECT), PROJECT)

    def token_load(c):
        at = span_of(c)
        return pltpu.make_async_copy(tokens_hbm.at[at], tokens.at[at], token_sem.at[c])

    for c in range(rows // PROJECT):
        token_load(c).start()
    loads = [
        load(0, wq_hbm, wq), load(1, wk_hbm, wk), load(2, wv_hbm, wv),
        load(3, wo_hbm, wo), load(4, wu_hbm, wu), load(5, wd_hbm, wd), load(6, cot_hbm, cot),
    ]
    for copy in loads[:3]:
        copy.start()

    levels = dp_size.bit_length() - 1
    me = lax.axis_index("dp")
    bits = [lax.rem(me // (1 << b), 2) for b in range(levels)]
    partner = [{"dp": me + (1 << b) * (1 - 2 * bits[b])} for b in range(levels)]
    half = [dp_size >> (level + 1) for level in range(levels)]
    routes = [list(range(levels)), [0] + list(range(2, levels)) + [1]]
    keep, give = [], []
    for route in routes:
        base, kept, given = 0, [], []
        for level in range(levels):
            kept.append(base + bits[route[level]] * half[level])
            given.append(base + (1 - bits[route[level]]) * half[level])
            base = kept[-1]
        keep.append(kept)
        give.append(given)

    def position(index, way):
        return sum(lax.rem(index // (1 << b), 2) * half[level] for level, b in enumerate(routes[way]))

    def fixed_position(index, way):
        return sum((index >> b) % 2 * half[level] for level, b in enumerate(routes[way]))

    barrier = pltpu.get_barrier_semaphore()
    for other in [peer] + partner:
        pl.semaphore_signal(barrier, inc=1, device_id=other, device_id_type=MESH)

    width = tokens.shape[1]
    blk = width // dp_size

    split = local // 4
    mine, far = lax.rem(me, 4), lax.rem(me + 2, 4)
    att_peer = gffn.at[:, pl.ds(0, local)]

    def wo_piece(which, side):
        start = pl.multiple_of(side * local + which * split, split)
        return gffn.at[pl.ds(start, split), pl.ds(width - local, local)]

    def wo_cross(side):
        return pltpu.make_async_remote_copy(
            src_ref=wo_hbm.at[pl.ds(pl.multiple_of(mine * split, split), split), pl.ds(side * local, local)],
            dst_ref=wo_piece(mine, side),
            send_sem=wo_sem.at[side],
            recv_sem=wo_sem.at[2 + side],
            device_id=peer,
            device_id_type=MESH,
        )

    def wo_share(step, side):
        which = far if step == 2 else mine
        return pltpu.make_async_remote_copy(
            src_ref=wo_piece(which, side),
            dst_ref=wo_piece(which, side),
            send_sem=wo_sem.at[4 * step + 4 + side],
            recv_sem=wo_sem.at[4 * step + 6 + side],
            device_id=partner[1] if step == 0 else partner[0],
            device_id_type=MESH,
        )

    wide = 1024
    count = inner // wide
    rows_at = lambda ref, start, size: ref.at[pl.ds(start, size), :]
    cols_at = lambda ref, start, size: ref.at[:, pl.ds(start, size)]
    table = [(rows_at(wd, u * width, width), cols_at(down_ref, u * wide, wide), None, WAYS[u]) for u in range(count)]
    table += [
        (cols_at(wu, u * wide, wide), cols_at(up_ref, u * wide, wide), None, WAYS[count + u]) for u in range(count)
    ]
    attn_first = 2 * count
    for i in range(4):
        cols = pl.ds(i * local, local)
        table.append((hid.at[:, cols], attn_ref.at[:, cols], cols, WAYS[attn_first + i]))
    norm_unit = len(table)
    table.append((norm_held, norm_ref, None, 0))

    def held(unit):
        return table[unit][0]

    def inbox(unit, level):
        if unit == norm_unit:
            return norm_box.at[pl.ds(8 * (dp_size - 2 * half[level]), 8 * half[level]), :]
        size = half[level] * blk
        if unit >= attn_first:
            return slope.at[pl.ds(width - 2 * size, size), table[unit][2]]
        if level == 0:
            return rows_at(got2 if unit < count else tokens, (unit % count) * size, size)
        if level == 1:
            return rows_at(gffn, unit * size, size)
        return rows_at(tokens, 2 * count * (width // 4 - 2 * size) + unit * size, size)

    def block_of(unit):
        return 8 if unit == norm_unit else blk

    def hop(unit, level):
        way = table[unit][3]
        rows_each = block_of(unit)
        index = unit * levels + level
        start = pl.multiple_of(give[way][level] * rows_each, 8)
        return pltpu.make_async_remote_copy(
            src_ref=held(unit).at[pl.ds(start, half[level] * rows_each), :],
            dst_ref=inbox(unit, level),
            send_sem=give_sem.at[index],
            recv_sem=take_sem.at[index],
            device_id=partner[routes[way][level]],
            device_id_type=MESH,
        )

    def credit(unit, level):
        return free_sem.at[(2 * levels if unit >= attn_first else 0) + 2 * level + table[unit][3]]

    def release(which, level):
        for way in range(2):
            same = [u for u in which if table[u][3] == way]
            if same:
                pl.semaphore_signal(
                    credit(same[0], level), inc=len(same), device_id=partner[routes[way][level]], device_id_type=MESH
                )

    def send(unit, level):
        if unit != norm_unit:
            pl.semaphore_wait(credit(unit, level), 1)
        hop(unit, level).start()

    def take(unit, level):
        hop(unit, level).wait_recv()
        rows_each = block_of(unit)
        size = half[level] * rows_each
        step_rows = min(size, 32)
        ours, came = held(unit), inbox(unit, level)
        last = level == levels - 1
        target = table[unit][1]
        first = keep[table[unit][3]][level] * rows_each

        def add(b, carry):
            here = pl.multiple_of(b * step_rows, step_rows)
            there = pl.multiple_of(first + b * step_rows, 8)
            total = ours[pl.ds(there, step_rows), :].astype(F32) + came[pl.ds(here, step_rows), :].astype(F32)
            if last:
                target[pl.ds(here, step_rows), :] = total
            else:
                ours[pl.ds(there, step_rows), :] = total.astype(ours.dtype)
            return carry

        lax.fori_loop(0, size // step_rows, add, 0)
        if unit == 2 * count - 1 and level == 0:
            for other in range(2, levels):
                release(range(2 * count), other)
        if not last:
            send(unit, level + 1)

    def weight_grad(left, groups):
        span = 256

        def part(j, carry):
            turned = left[:, pl.ds(pl.multiple_of(j * span, span), span)].T
            for right, ref, at, way in groups:
                grad = dot(turned, right[...], NN).astype(BF16)
                for i in range(span // blk):
                    start = pl.multiple_of(position(j * (span // blk) + i, way) * blk, 8)
                    ref[pl.ds(start, blk), pl.ds(at, grad.shape[1])] = grad[i * blk : (i + 1) * blk]
            return carry

        lax.fori_loop(0, width // span, part, 0)

    def rows_of(c):
        return pl.ds(pl.multiple_of(c * CHUNK, CHUNK), CHUNK)

    def exchange(step, c, source, target):
        index = step * chunks + c
        return pltpu.make_async_remote_copy(
            src_ref=source.at[rows_of(c)],
            dst_ref=target.at[rows_of(c)],
            send_sem=send_sem.at[index],
            recv_sem=recv_sem.at[index],
            device_id=peer,
            device_id_type=MESH,
        )

    length = length_ref[0]

    def gain(j):
        return gain_ref[j : j + 1, :]

    def bias(j):
        return bias_ref[j : j + 1, :]

    def blocks(c, body, size=CHUNK):
        def step(b, carry):
            start = pl.multiple_of(c * size + b * BLOCK, BLOCK)
            body(start, pl.ds(start, BLOCK))
            return carry

        lax.fori_loop(0, size // BLOCK, step, 0)

    def real_rows(start):
        index = start + lax.broadcasted_iota(jnp.int32, (BLOCK, 1), 0)
        return jnp.where(index < length, 1.0, 0.0)

    acc[...] = jnp.zeros_like(acc)

    def query_rows(at):
        q[at, :] = (dot(nin[at, :], wq[...], NN) * 0.125).astype(BF16)

    def norm_in(start, at):
        hat, _ = normalize(tokens[at, :].astype(F32))
        nin[at, :] = (hat * gain(0) + bias(0)).astype(BF16)

    for c in range(rows // PROJECT):
        token_load(c).wait()
        blocks(c, norm_in, PROJECT)
    for copy in loads[3:]:
        copy.start()
    pl.semaphore_wait(barrier, levels + 1)
    for side in range(2):
        wo_cross(side).start()
    for copy in loads[:3]:
        copy.wait()
    query_rows(span_of(0))
    for c in range(rows // (2 * PROJECT)):
        at = pl.ds(2 * PROJECT * c, 2 * PROJECT)
        normed = nin[at, :]
        k[at, :] = dot(normed, wk[...], NN).astype(BF16)
        v[at, :] = dot(normed, wv[...], NN).astype(BF16)
    save(0, nin, nin_hbm).start()

    key_bias = jnp.where(lane_index((1, rows)) < length, 0.0, NEG)

    def attend(c, carry):
        at = rows_of(c)

        ratio = PROJECT // CHUNK

        @pl.when(jnp.logical_and(lax.rem(c, ratio) == 0, c > 0))
        def _():
            query_rows(span_of(c // ratio))

        def pair(p, carry):
            cols = pl.ds(pl.multiple_of(p * LANES, LANES), LANES)
            keys, values = k[:, cols], v[:, cols]
            scores = dot(stack_pair(q[at, cols]), keys, NT) + key_bias
            top = jnp.max(scores, axis=1, keepdims=True)
            weights = jnp.exp(scores - top)
            total = jnp.sum(weights, axis=1, keepdims=True)
            mixed = dot(weights.astype(BF16), values, NN) / total
            first, second = jnp.split(top + jnp.log(total), 2, axis=0)
            logs = lse[at, :]
            lane = lane_index(logs.shape)
            lse[at, :] = jnp.where(lane == 2 * p, first, jnp.where(lane == 2 * p + 1, second, logs))
            att[at, cols] = join_pair(mixed).astype(BF16)
            return carry

        lax.fori_loop(0, pairs, pair, 0, unroll=UNROLL)
        exchange(0, c, att, att_peer).start()

        @pl.when(c == 2)
        def _():
            for side in range(2):
                wo_cross(side).wait_recv()
                wo_share(0, side).start()
                wo_share(1, side).start()

        @pl.when(c == chunks - 2)
        def _():
            for side in range(2):
                wo_share(0, side).wait_recv()
                wo_share(2, side).start()

        return carry

    lax.fori_loop(0, chunks, attend, 0)
    for copy in loads[3:6]:
        copy.wait()
    for side in range(2):
        wo_share(0, side).wait_send()
        wo_share(1, side).wait()
        wo_share(2, side).wait()
    save(0, nin, nin_hbm).wait()
    nmid = nin

    def feed(c, carry):
        at = rows_of(c)
        exchange(0, c, att, att_peer).wait_recv()
        ours = dot(att[at, :], wo[...], NN).astype(BF16).astype(F32)
        other = att_peer[at, :]
        for side in range(2):
            cols = pl.ds(side * local, local)
            weight = gffn[pl.ds(side * local, local), pl.ds(width - local, local)]
            theirs = dot(other, weight, NN).astype(BF16).astype(F32)
            attn_total[at, cols] = ours[:, side * local : (side + 1) * local] + theirs

        def norms(start, at):
            hat, scale = normalize(attn_total[at, :])
            attn_total[at, :] = hat
            lse[at, :] = jnp.where(lane_index((BLOCK, LANES)) == 2 * pairs, scale, lse[at, :])
            mid = tokens[at, :].astype(F32) + (hat * gain(1) + bias(1))
            middle[at, :] = mid
            hat, _ = normalize(mid)
            nmid[at, :] = (hat * gain(2) + bias(2)).astype(BF16)

        blocks(c, norms)
        normed = nmid[at, :]
        span = 512
        for n in range(inner // span):
            cols = pl.ds(n * span, span)
            value, grade = gelu_both(dot(normed, wu[:, cols], NN))
            hid[at, cols] = value.astype(BF16)
            slope[at, cols] = grade.astype(BF16)
        own2[at, :] = dot(hid[at, :], wd[...], NN).astype(BF16)
        exchange(1, c, own2, got2).start()
        return carry

    lax.fori_loop(0, chunks, feed, 0)
    loads[6].wait()

    def feed_back(c, carry):
        at = rows_of(c)
        exchange(1, c, own2, got2).wait_recv()

        def norms(start, at):
            hat, scale = normalize(own2[at, :].astype(F32) + got2[at, :].astype(F32))
            out = middle[at, :] + (hat * gain(3) + bias(3))
            result_ref[at, :] = out.astype(BF16)
            grad = cot[at, :].astype(F32) * real_rows(start)
            gffn[at, :] = norm_pull(hat, scale, gain(3), grad).astype(BF16)
            acc[2] += fold_rows(grad * hat)
            acc[5] += fold_rows(grad)
            hat, scale = normalize(middle[at, :])
            middle[at, :] = hat
            lse[at, :] = jnp.where(lane_index((BLOCK, LANES)) == 2 * pairs + 1, scale, lse[at, :])

        blocks(c, norms)
        grad = gffn[at, :]
        span = 512
        for n in range(inner // span):
            cols = pl.ds(n * span, span)
            grown = dot(grad, wd[cols, :], NT)
            slope[at, cols] = (grown * slope[at, cols].astype(F32)).astype(BF16)
        exchange(1, c, own2, got2).wait_send()
        own2[at, :] = dot(slope[at, :], wu[...], NT).astype(BF16)
        exchange(2, c, own2, got3).start()
        return carry

    lax.fori_loop(0, chunks, feed_back, 0)
    release(range(2 * count), 0)

    def parts(source, first_unit):
        units = range(first_unit, first_unit + count)
        return [(cols_at(source, i * wide, wide), held(u), 0, table[u][3]) for i, u in enumerate(units)]

    weight_grad(gffn, parts(hid, 0))
    release(range(2 * count), 1)
    for u in range(count):
        send(u, 0)
    weight_grad(nmid, parts(slope, count))
    for level in range(levels):
        release(range(attn_first, norm_unit), level)
    for u in range(count, 2 * count):
        send(u, 0)
    nin_back = pltpu.make_async_copy(nin_hbm, nin, save_sem.at[1])
    nin_back.start()
    for u in range(count):
        take(u, 0)
    gk[...] = jnp.zeros_like(gk)
    gv[...] = jnp.zeros_like(gv)

    agenda = {}
    for (u, level), slot in sorted(SLOTS.items(), key=lambda item: item[1]):
        agenda.setdefault(slot, []).append((u, level))

    tokens_back = pltpu.make_async_copy(tokens_hbm, got2, save_sem.at[2])

    def attend_back(c, carry):
        at = rows_of(c)
        exchange(2, c, own2, got3).wait_recv()

        def norms(start, at):
            grad = own2[at, :].astype(F32) + got3[at, :].astype(F32)
            hat, scale = middle[at, :], lse[at, 2 * pairs + 1 : 2 * pairs + 2]
            out = cot[at, :].astype(F32) * real_rows(start)
            mid = out + norm_pull(hat, scale, gain(2), grad)
            acc[1] += fold_rows(grad * hat)
            acc[4] += fold_rows(grad)
            middle[at, :] = mid
            hat, scale = attn_total[at, :], lse[at, 2 * pairs : 2 * pairs + 1]
            gattn[at, :] = norm_pull(hat, scale, gain(1), mid).astype(BF16)
            acc[0] += fold_rows(mid * hat)
            acc[3] += fold_rows(mid)

        blocks(c, norms)

        @pl.when(c == chunks - 1)
        def _():
            pl.semaphore_signal(free_sem.at[4 * levels], inc=1, device_id=peer, device_id_type=MESH)
            tokens_back.start()

        gatt[...] = dot(gattn[at, :], wo[...], NT).astype(BF16)

        def pair(p):
            cols = pl.ds(p * LANES, LANES)
            keys, values, grad = k[:, cols], v[:, cols], gatt[:, cols]
            query, grads = stack_pair(q[at, cols]), stack_pair(grad)
            through = stack_pair(grad.astype(F32) * att[at, cols].astype(F32))
            shift = jnp.sum(through, axis=1, keepdims=True)
            logs = lse[at, :]
            log = jnp.concatenate([logs[:, 2 * p : 2 * p + 1], logs[:, 2 * p + 1 : 2 * p + 2]], axis=0)
            weights = jnp.exp(dot(query, keys, NT) + key_bias - log)
            slopes = (weights * (dot(grads, values, NT) - shift)).astype(BF16)
            q[at, cols] = (join_pair(dot(slopes, keys, NN)) * 0.125).astype(BF16)
            gk[cols, :] += dot(query, slopes, TN)
            gv[cols, :] += dot(grads, weights.astype(BF16), TN)

        for slot, work in agenda.items():

            @pl.when(c == slot)
            def _(work=work):
                for unit, level in work:
                    take(unit, level)

        for p in range(pairs):
            pair(p)
        return carry

    lax.fori_loop(0, chunks, attend_back, 0)
    pl.semaphore_wait(free_sem.at[4 * levels], 1)
    back = got2

    turned = set()

    def turn(c):
        if c not in turned:
            turned.add(c)
            at = rows_of(c)
            k[at, :] = gk[:, at].astype(BF16).T
            v[at, :] = gv[:, at].astype(BF16).T

    def input_part(first, number):
        at = pl.ds(first * CHUNK, number * CHUNK)
        for c in range(first, first + number):
            turn(c)
            exchange(2, c, own2, got3).wait_send()
        part = dot(q[at, :], wq[...], NT) + dot(k[at, :], wk[...], NT) + dot(v[at, :], wv[...], NT)
        own2[at, :] = part.astype(BF16)
        for c in range(first, first + number):
            exchange(3, c, own2, got3).start()

    def project_grads():
        for c in range(chunks):
            turn(c)
        nin_back.wait()
        weight_grad(nin, [(ref, hid, i * local, WAYS[attn_first + i]) for i, ref in enumerate((q, k, v))])
        for u in range(attn_first, attn_first + 3):
            send(u, 0)

    def out_grad():
        weight_grad(gattn, [(att, hid, 3 * local, WAYS[attn_first + 3])])
        send(attn_first + 3, 0)

    def norm_grads():
        tokens_back.wait()

        def first_norm(c, carry):
            def sums(start, at):
                hat, _ = normalize(back[at, :].astype(F32))
                grad = own2[at, :].astype(F32)
                acc[6] += fold_rows(grad * hat)
                acc[7] += fold_rows(grad)

            blocks(c, sums)
            return carry

        lax.fori_loop(0, chunks, first_norm, 0)
        sums = jnp.concatenate([jnp.sum(acc[j], axis=0, keepdims=True) for j in (6, 0, 1, 2, 7, 3, 4, 5)])
        for index in range(dp_size):
            tile, shift = divmod(index * blk, LANES)
            piece = sums[:, tile * LANES : (tile + 1) * LANES]
            if shift:
                piece = pltpu.roll(piece, LANES - shift, 1)
            spot = 8 * fixed_position(index, 0)
            norm_held[spot : spot + 8, :] = piece
        send(norm_unit, 0)

    def input_grad(c):
        at = rows_of(c)
        exchange(3, c, own2, got3).wait_recv()

        def norms(start, at):
            grad = own2[at, :].astype(F32) + got3[at, :].astype(F32)
            hat, scale = normalize(back[at, :].astype(F32))
            total = middle[at, :] + norm_pull(hat, scale, gain(0), grad)
            ingrad_ref[at, :] = total.astype(BF16)

        blocks(c, norms)

    tell = pltpu.make_async_remote_copy(
        src_ref=norm_ref,
        dst_ref=norm_peer,
        send_sem=send_sem.at[4 * chunks],
        recv_sem=recv_sem.at[4 * chunks],
        device_id=peer,
        device_id_type=MESH,
    )
    everything = [(u, level) for level in range(levels) for u in range(norm_unit + 1)]
    early = set(SLOTS) | {(u, 0) for u in range(count)}
    plan = PLAN
    if levels != 4:
        plan = [("part", 0, 1), "project", "out", ("part", 1, chunks - 1), "norm"] + [x for x in everything if x not in early]
        plan += [("grad", c) for c in range(chunks)]
    assert sorted(x for x in plan if not isinstance(x[0], str)) == sorted(set(everything) - early)
    for item in plan:
        if item == "project":
            project_grads()
        elif item == "out":
            out_grad()
        elif item == "norm":
            norm_grads()
        elif item[0] == "part":
            input_part(*item[1:])
        elif item[0] == "grad":
            input_grad(item[1])
        else:
            take(*item)
            if item == (norm_unit, levels - 1):
                tell.start()
    tell.wait()
    row = lax.broadcasted_iota(jnp.int32, norm_ref.shape, 0)
    norm_ref[...] += jnp.where(lax.rem(row, 4) == 0, norm_peer[...], 0.0)

    def drain(c, carry):
        exchange(0, c, att, att_peer).wait_send()
        exchange(3, c, own2, got3).wait_send()
        return carry

    lax.fori_loop(0, chunks, drain, 0)
    for side in range(2):
        wo_cross(side).wait_send()
    for unit in range(norm_unit + 1):
        for level in range(levels):
            hop(unit, level).wait_send()


def run_layer(lengths, tokens, wq, wk, wv, wo, wu, wd, gains, biases, cot):
    dp_size = lax.axis_size("dp")
    rows, width = tokens.shape
    local, inner = wq.shape[1], wu.shape[1]
    chunks = rows // CHUNK
    levels = dp_size.bit_length() - 1
    units = 2 * (inner // 1024) + 5
    shape = jax.ShapeDtypeStruct
    anywhere = pl.BlockSpec(memory_space=pl.ANY)
    vmem = pl.BlockSpec(memory_space=pltpu.VMEM)
    wide = (rows, width)
    thin = (rows, local)
    blk = width // dp_size
    outs = [
        pltpu.VMEM(wide, BF16), pltpu.VMEM(wide, BF16), shape(wide, BF16),
        pltpu.VMEM((blk, inner), F32), pltpu.VMEM((blk, inner), F32), pltpu.VMEM((blk, 4 * local), F32),
        pltpu.VMEM((8, LANES), F32),
    ]
    scratch = [
        pltpu.VMEM(wide, BF16), pltpu.VMEM(wq.shape, BF16), pltpu.VMEM(wk.shape, BF16), pltpu.VMEM(wv.shape, BF16),
        pltpu.VMEM(wo.shape, BF16), pltpu.VMEM(wu.shape, BF16), pltpu.VMEM(wd.shape, BF16), pltpu.VMEM(wide, BF16),
        pltpu.VMEM(wide, BF16), pltpu.VMEM(thin, BF16), pltpu.VMEM(thin, BF16), pltpu.VMEM(thin, BF16),
        pltpu.VMEM(thin, BF16), pltpu.VMEM((rows, LANES), F32),
        pltpu.VMEM(wide, F32), pltpu.VMEM(wide, BF16), pltpu.VMEM(wide, BF16), pltpu.VMEM(wide, BF16),
        pltpu.VMEM(wide, F32), pltpu.VMEM((rows, inner), BF16), pltpu.VMEM((rows, inner), BF16),
        pltpu.VMEM(wide, BF16), pltpu.VMEM(wide, BF16), pltpu.VMEM((CHUNK, local), BF16),
        pltpu.VMEM((local, rows), F32), pltpu.VMEM((local, rows), F32),
        pltpu.VMEM((8, 8, width), F32),
        pltpu.VMEM((8 * dp_size, LANES), F32), pltpu.VMEM((8 * dp_size, LANES), F32), pltpu.VMEM((8, LANES), F32),
        pltpu.SemaphoreType.DMA((rows // PROJECT,)), pltpu.SemaphoreType.DMA((7,)), pltpu.SemaphoreType.DMA((16,)), pltpu.SemaphoreType.DMA((3,)),
        pltpu.SemaphoreType.DMA((4 * chunks + 1,)), pltpu.SemaphoreType.DMA((4 * chunks + 1,)),
        pltpu.SemaphoreType.DMA((units * levels,)), pltpu.SemaphoreType.DMA((units * levels,)),
        pltpu.SemaphoreType.REGULAR((4 * levels + 1,)),
    ]
    return pl.pallas_call(
        functools.partial(layer_kernel, dp_size),
        out_shape=outs,
        in_specs=[pl.BlockSpec(memory_space=pltpu.SMEM)] + [anywhere] * 7 + [vmem, vmem, anywhere],
        out_specs=[vmem, vmem, anywhere] + [vmem] * 4,
        scratch_shapes=scratch,
        compiler_params=pltpu.CompilerParams(
            collective_id=0, has_side_effects=True, vmem_limit_bytes=VMEM_BYTES - 4 * rows * width - 8 * blk * (inner + 2 * local)
        ),
        name="layer",
    )(lengths, tokens, wq, wk, wv, wo, wu, wd, gains, biases, cot)


def finish_kernel(
    result_in, ingrad_in, up_in, down_in, attn_in, norm_in, result, ingrad, query, key, value, out, up, down, gain, bias, sem
):
    local = query.shape[1]
    pairs = [(result_in, result), (ingrad_in, ingrad), (up_in, up), (down_in, down)]
    pairs += [(attn_in.at[:, pl.ds(i * local, local)], ref) for i, ref in enumerate((query, key, value, out))]
    copies = [pltpu.make_async_copy(source, target, sem.at[i]) for i, (source, target) in enumerate(pairs)]
    for copy in copies:
        copy.start()
    blk = gain.shape[1]
    gain[...] = norm_in[:4, :blk]
    bias[...] = norm_in[4:, :blk]
    for copy in copies:
        copy.wait()


def on_device(tokens, lengths, wq, wk, wv, wo, wu, wd, gains, biases, cot):
    local, inner = wq.shape[1], wu.shape[1]
    result, input_grad, _, up, down, attn, norms = run_layer(
        lengths, tokens, wq, wk, wv, wo, wu, wd, gains, biases, cot
    )
    blk = up.shape[0]
    shape = jax.ShapeDtypeStruct
    anywhere = pl.BlockSpec(memory_space=pl.ANY)
    vmem = pl.BlockSpec(memory_space=pltpu.VMEM)
    result, input_grad, query, key, value, out, up, down, gain, bias = pl.pallas_call(
        finish_kernel,
        out_shape=[shape(result.shape, BF16), shape(result.shape, BF16)]
        + [shape((blk, local), F32)] * 4
        + [shape((blk, inner), F32)] * 2
        + [shape((4, blk), F32)] * 2,
        in_specs=[vmem] * 6,
        out_specs=[anywhere] * 8 + [vmem] * 2,
        scratch_shapes=[pltpu.SemaphoreType.DMA((8,))],
        compiler_params=pltpu.CompilerParams(vmem_limit_bytes=4 * 1024 * 1024),
        name="finish",
    )(result, input_grad, up, down, attn, norms)
    return result, input_grad, query, key, value, out.T, up, down.T, gain, bias


def solution(mesh):
    in_specs = (
        P("dp", None), P("dp"), P(None, "tensor"), P(None, "tensor"), P(None, "tensor"), P("tensor", None),
        P(None, "tensor"), P("tensor", None), P(), P(), P("dp", None),
    )
    out_specs = (
        P("dp", None), P("dp", None), P("dp", "tensor"), P("dp", "tensor"), P("dp", "tensor"), P("tensor", "dp"),
        P("dp", "tensor"), P("tensor", "dp"), P(None, "dp"), P(None, "dp"),
    )
    return jax.shard_map(on_device, mesh=mesh, in_specs=in_specs, out_specs=out_specs, check_vma=False)
```

```python
import functools

import jax
import jax.numpy as jnp
from jax import lax
from jax.experimental import pallas as pl
from jax.experimental.pallas import tpu as pltpu
from jax.sharding import PartitionSpec as P

HD = 64
LANES = 128
EPS = 1e-05
CHUNK = 128
PROJECT = 256
BLOCK = 128
NEG = -1000000000.0
F32 = jnp.float32
BF16 = jnp.bfloat16
MESH = pl.DeviceIdType.MESH
NN = (((1,), (0,)), ((), ()))
NT = (((1,), (1,)), ((), ()))
TN = (((0,), (0,)), ((), ()))
ROOT = 0.7978845608028654
CUBE = 0.044715
UNROLL = 2
VMEM_BYTES = 127 * 512 * 1024
WAYS = (0, 0, 1, 0, 0, 0, 0, 0)
SLOTS = {(2, 0): 1, (3, 0): 1, (0, 1): 4, (2, 1): 5, (0, 2): 7, (1, 1): 7}
PLAN = [
    ("part", 0, 1), ("part", 1, 1), (3, 1), "project", (2, 2), ("part", 2, 2), "out", (4, 0), (5, 0), (1, 2), (0, 3),
    ("part", 4, 2), ("part", 6, 2), "norm", (6, 0), (8, 0), (7, 0), (3, 2), (2, 3), ("grad", 0), ("grad", 1), (4, 1),
    (1, 3), ("grad", 2), (5, 1), (8, 1), (4, 2), (8, 2), (3, 3), ("grad", 3), (5, 2), (6, 1), (8, 3), (4, 3), ("grad", 4),
    (5, 3), (7, 1), (6, 2), ("grad", 5), (7, 2), (6, 3), ("grad", 6), (7, 3), ("grad", 7),
]


def dot(left, right, dims):
    return lax.dot_general(left, right, dims, preferred_element_type=F32)


def row_mean(values):
    return jnp.sum(values, axis=-1, keepdims=True) * (1.0 / values.shape[-1])


def normalize(values):
    centered = values - row_mean(values)
    scale = lax.rsqrt(row_mean(centered * centered) + EPS)
    return centered * scale, scale


def norm_pull(hat, scale, gain, grad):
    weighed = grad * gain
    return scale * (weighed - row_mean(weighed) - hat * row_mean(weighed * hat))


def gelu_both(v):
    square = v * v
    tanh = jnp.tanh(v * (ROOT + (ROOT * CUBE) * square))
    half = 0.5 + 0.5 * tanh
    slope = half + (0.5 * v) * (1.0 - tanh * tanh) * (ROOT + (3.0 * ROOT * CUBE) * square)
    return v * half, slope


def lane_index(shape):
    return lax.broadcasted_iota(jnp.int32, shape, 1)


def head_of_pair(values, side):
    low = lane_index(values.shape) < HD
    return jnp.where(low if side == 0 else jnp.logical_not(low), values, jnp.zeros_like(values))


def stack_pair(values):
    return jnp.concatenate([head_of_pair(values, 0), head_of_pair(values, 1)], axis=0)


def join_pair(stacked):
    first, second = jnp.split(stacked, 2, axis=0)
    return jnp.where(lane_index(first.shape) < HD, first, second)


def fold_rows(values):
    return jnp.sum(values.reshape(-1, 8, values.shape[-1]), axis=0)


def layer_kernel(
    dp_size,
    length_ref, tokens_hbm, wq_hbm, wk_hbm, wv_hbm, wo_hbm, wu_hbm, wd_hbm, gain_ref, bias_ref, cot_hbm,
    result_ref, ingrad_ref, nin_hbm, up_ref, down_ref, attn_ref, norm_ref,
    tokens, wq, wk, wv, wo, wu, wd, cot,
    nin, q, k, v, att, lse, attn_total, own2, got2, got3, middle, hid, slope, gffn, gattn, gatt, gk, gv, ahead,
    acc, norm_held, norm_box, norm_peer,
    token_sem, load_sem, wo_sem, save_sem, send_sem, recv_sem, give_sem, take_sem, free_sem,
):
    rows = tokens.shape[0]
    chunks = rows // CHUNK
    local = q.shape[1]
    pairs = local // LANES
    inner = hid.shape[1]
    peer = {"tensor": 1 - lax.axis_index("tensor")}

    def load(index, source, target):
        return pltpu.make_async_copy(source, target, load_sem.at[index])

    def save(index, source, target):
        return pltpu.make_async_copy(source, target, save_sem.at[index])

    def span_of(c):
        return pl.ds(pl.multiple_of(c * PROJECT, PROJECT), PROJECT)

    def token_load(c):
        at = span_of(c)
        return pltpu.make_async_copy(tokens_hbm.at[at], tokens.at[at], token_sem.at[c])

    for c in range(rows // PROJECT):
        token_load(c).start()
    loads = [
        load(0, wq_hbm, wq), load(1, wk_hbm, wk), load(2, wv_hbm, wv),
        load(3, wo_hbm, wo), load(4, wu_hbm, wu), load(5, wd_hbm, wd), load(6, cot_hbm, cot),
    ]
    for copy in loads[:3]:
        copy.start()

    levels = dp_size.bit_length() - 1
    me = lax.axis_index("dp")
    bits = [lax.rem(me // (1 << b), 2) for b in range(levels)]
    partner = [{"dp": me + (1 << b) * (1 - 2 * bits[b])} for b in range(levels)]
    half = [dp_size >> (level + 1) for level in range(levels)]
    routes = [list(range(levels)), [0] + list(range(2, levels)) + [1]]
    keep, give = [], []
    for route in routes:
        base, kept, given = 0, [], []
        for level in range(levels):
            kept.append(base + bits[route[level]] * half[level])
            given.append(base + (1 - bits[route[level]]) * half[level])
            base = kept[-1]
        keep.append(kept)
        give.append(given)

    def position(index, way):
        return sum(lax.rem(index // (1 << b), 2) * half[level] for level, b in enumerate(routes[way]))

    def fixed_position(index, way):
        return sum((index >> b) % 2 * half[level] for level, b in enumerate(routes[way]))

    barrier = pltpu.get_barrier_semaphore()
    for other in [peer] + partner:
        pl.semaphore_signal(barrier, inc=1, device_id=other, device_id_type=MESH)

    width = tokens.shape[1]
    blk = width // dp_size

    split = local // 4
    mine, far = lax.rem(me, 4), lax.rem(me + 2, 4)
    att_peer = gffn.at[:, pl.ds(0, local)]

    def wo_piece(which, side):
        start = pl.multiple_of(side * local + which * split, split)
        return gffn.at[pl.ds(start, split), pl.ds(width - local, local)]

    def wo_cross(side):
        return pltpu.make_async_remote_copy(
            src_ref=wo_hbm.at[pl.ds(pl.multiple_of(mine * split, split), split), pl.ds(side * local, local)],
            dst_ref=wo_piece(mine, side),
            send_sem=wo_sem.at[side],
            recv_sem=wo_sem.at[2 + side],
            device_id=peer,
            device_id_type=MESH,
        )

    def wo_share(step, side):
        which = far if step == 2 else mine
        return pltpu.make_async_remote_copy(
            src_ref=wo_piece(which, side),
            dst_ref=wo_piece(which, side),
            send_sem=wo_sem.at[4 * step + 4 + side],
            recv_sem=wo_sem.at[4 * step + 6 + side],
            device_id=partner[1] if step == 0 else partner[0],
            device_id_type=MESH,
        )

    wide = 1024
    count = inner // wide
    rows_at = lambda ref, start, size: ref.at[pl.ds(start, size), :]
    cols_at = lambda ref, start, size: ref.at[:, pl.ds(start, size)]
    table = [(rows_at(wd, u * width, width), cols_at(down_ref, u * wide, wide), None, WAYS[u]) for u in range(count)]
    table += [
        (cols_at(wu, u * wide, wide), cols_at(up_ref, u * wide, wide), None, WAYS[count + u]) for u in range(count)
    ]
    attn_first = 2 * count
    for i in range(4):
        cols = pl.ds(i * local, local)
        table.append((hid.at[:, cols], attn_ref.at[:, cols], cols, WAYS[attn_first + i]))
    norm_unit = len(table)
    table.append((norm_held, norm_ref, None, 0))

    def held(unit):
        return table[unit][0]

    def inbox(unit, level):
        if unit == norm_unit:
            return norm_box.at[pl.ds(8 * (dp_size - 2 * half[level]), 8 * half[level]), :]
        size = half[level] * blk
        if unit >= attn_first:
            return slope.at[pl.ds(width - 2 * size, size), table[unit][2]]
        if level == 0:
            return rows_at(got2 if unit < count else tokens, (unit % count) * size, size)
        if level == 1:
            return rows_at(gffn, unit * size, size)
        return rows_at(tokens, 2 * count * (width // 4 - 2 * size) + unit * size, size)

    def block_of(unit):
        return 8 if unit == norm_unit else blk

    def hop(unit, level):
        way = table[unit][3]
        rows_each = block_of(unit)
        index = unit * levels + level
        start = pl.multiple_of(give[way][level] * rows_each, 8)
        return pltpu.make_async_remote_copy(
            src_ref=held(unit).at[pl.ds(start, half[level] * rows_each), :],
            dst_ref=inbox(unit, level),
            send_sem=give_sem.at[index],
            recv_sem=take_sem.at[index],
            device_id=partner[routes[way][level]],
            device_id_type=MESH,
        )

    def credit(unit, level):
        return free_sem.at[(2 * levels if unit >= attn_first else 0) + 2 * level + table[unit][3]]

    def release(which, level):
        for way in range(2):
            same = [u for u in which if table[u][3] == way]
            if same:
                pl.semaphore_signal(
                    credit(same[0], level), inc=len(same), device_id=partner[routes[way][level]], device_id_type=MESH
                )

    def send(unit, level):
        if unit != norm_unit:
            pl.semaphore_wait(credit(unit, level), 1)
        hop(unit, level).start()

    def take(unit, level):
        hop(unit, level).wait_recv()
        rows_each = block_of(unit)
        size = half[level] * rows_each
        step_rows = min(size, 32)
        ours, came = held(unit), inbox(unit, level)
        last = level == levels - 1
        target = table[unit][1]
        first = keep[table[unit][3]][level] * rows_each

        def add(b, carry):
            here = pl.multiple_of(b * step_rows, step_rows)
            there = pl.multiple_of(first + b * step_rows, 8)
            total = ours[pl.ds(there, step_rows), :].astype(F32) + came[pl.ds(here, step_rows), :].astype(F32)
            if last:
                target[pl.ds(here, step_rows), :] = total
            else:
                ours[pl.ds(there, step_rows), :] = total.astype(ours.dtype)
            return carry

        lax.fori_loop(0, size // step_rows, add, 0)
        if unit == 2 * count - 1 and level == 0:
            for other in range(2, levels):
                release(range(2 * count), other)
        if not last:
            send(unit, level + 1)

    def weight_grad(left, groups):
        span = 256

        def part(j, carry):
            turned = left[:, pl.ds(pl.multiple_of(j * span, span), span)].T
            for right, ref, at, way in groups:
                grad = dot(turned, right[...], NN).astype(BF16)
                for i in range(span // blk):
                    start = pl.multiple_of(position(j * (span // blk) + i, way) * blk, 8)
                    ref[pl.ds(start, blk), pl.ds(at, grad.shape[1])] = grad[i * blk : (i + 1) * blk]
            return carry

        lax.fori_loop(0, width // span, part, 0)

    def rows_of(c):
        return pl.ds(pl.multiple_of(c * CHUNK, CHUNK), CHUNK)

    def exchange(step, c, source, target):
        index = step * chunks + c
        return pltpu.make_async_remote_copy(
            src_ref=source.at[rows_of(c)],
            dst_ref=target.at[rows_of(c)],
            send_sem=send_sem.at[index],
            recv_sem=recv_sem.at[index],
            device_id=peer,
            device_id_type=MESH,
        )

    length = length_ref[0]

    def gain(j):
        return gain_ref[j : j + 1, :]

    def bias(j):
        return bias_ref[j : j + 1, :]

    def blocks(c, body, size=CHUNK):
        def step(b, carry):
            start = pl.multiple_of(c * size + b * BLOCK, BLOCK)
            body(start, pl.ds(start, BLOCK))
            return carry

        lax.fori_loop(0, size // BLOCK, step, 0)

    def real_rows(start):
        index = start + lax.broadcasted_iota(jnp.int32, (BLOCK, 1), 0)
        return jnp.where(index < length, 1.0, 0.0)

    acc[...] = jnp.zeros_like(acc)

    def query_rows(at):
        q[at, :] = (dot(nin[at, :], wq[...], NN) * 0.125).astype(BF16)

    def norm_in(start, at):
        hat, _ = normalize(tokens[at, :].astype(F32))
        nin[at, :] = (hat * gain(0) + bias(0)).astype(BF16)

    spans = rows // PROJECT
    for c in range(spans // 2):
        token_load(c).wait()
        blocks(c, norm_in, PROJECT)
        if c == 0:
            pl.semaphore_wait(barrier, levels + 1)
            for side in range(2):
                wo_cross(side).start()
    for c in range(spans // 2, spans):
        token_load(c).wait()
    for copy in loads[3:]:
        copy.start()
    for copy in loads[:3]:
        copy.wait()
    for h in range(2):
        at = pl.ds(h * rows // 2, rows // 2)
        normed = nin[at, :]
        k[at, :] = dot(normed, wk[...], NN).astype(BF16)
        v[at, :] = dot(normed, wv[...], NN).astype(BF16)
        if h == 0:
            for b in range(rows // 2 // BLOCK):
                start = rows // 2 + b * BLOCK
                norm_in(start, pl.ds(start, BLOCK))
    query_rows(span_of(0))
    save(0, nin, nin_hbm).start()

    key_bias = jnp.where(lane_index((1, rows)) < length, 0.0, NEG)

    def attend(c, carry):
        at = rows_of(c)

        ratio = PROJECT // CHUNK

        @pl.when(jnp.logical_and(lax.rem(c, ratio) == 0, c > 0))
        def _():
            query_rows(span_of(c // ratio))

        def pair(p, carry):
            cols = pl.ds(pl.multiple_of(p * LANES, LANES), LANES)
            keys, values = k[:, cols], v[:, cols]
            scores = dot(stack_pair(q[at, cols]), keys, NT) + key_bias
            top = jnp.max(scores, axis=1, keepdims=True)
            weights = jnp.exp(scores - top)
            total = jnp.sum(weights, axis=1, keepdims=True)
            mixed = dot(weights.astype(BF16), values, NN) / total
            first, second = jnp.split(top + jnp.log(total), 2, axis=0)
            logs = lse[at, :]
            lane = lane_index(logs.shape)
            lse[at, :] = jnp.where(lane == 2 * p, first, jnp.where(lane == 2 * p + 1, second, logs))
            att[at, cols] = join_pair(mixed).astype(BF16)
            return carry

        lax.fori_loop(0, pairs, pair, 0, unroll=UNROLL)
        exchange(0, c, att, att_peer).start()

        @pl.when(c == 2)
        def _():
            for side in range(2):
                wo_cross(side).wait_recv()
                wo_share(0, side).start()
                wo_share(1, side).start()

        @pl.when(c == chunks - 2)
        def _():
            for side in range(2):
                wo_share(0, side).wait_recv()
                wo_share(2, side).start()

        return carry

    lax.fori_loop(0, chunks, attend, 0)
    for copy in loads[3:6]:
        copy.wait()
    for side in range(2):
        wo_share(0, side).wait_send()
        wo_share(1, side).wait()
        wo_share(2, side).wait()
    save(0, nin, nin_hbm).wait()
    nmid = nin

    def feed(c, carry):
        at = rows_of(c)
        exchange(0, c, att, att_peer).wait_recv()
        ours = dot(att[at, :], wo[...], NN).astype(BF16).astype(F32)
        other = att_peer[at, :]
        for side in range(2):
            cols = pl.ds(side * local, local)
            weight = gffn[pl.ds(side * local, local), pl.ds(width - local, local)]
            theirs = dot(other, weight, NN).astype(BF16).astype(F32)
            attn_total[at, cols] = ours[:, side * local : (side + 1) * local] + theirs

        def norms(start, at):
            hat, scale = normalize(attn_total[at, :])
            attn_total[at, :] = hat
            lse[at, :] = jnp.where(lane_index((BLOCK, LANES)) == 2 * pairs, scale, lse[at, :])
            mid = tokens[at, :].astype(F32) + (hat * gain(1) + bias(1))
            middle[at, :] = mid
            hat, _ = normalize(mid)
            nmid[at, :] = (hat * gain(2) + bias(2)).astype(BF16)

        blocks(c, norms)
        normed = nmid[at, :]
        span = 512
        for n in range(inner // span):
            cols = pl.ds(n * span, span)
            value, grade = gelu_both(dot(normed, wu[:, cols], NN))
            hid[at, cols] = value.astype(BF16)
            slope[at, cols] = grade.astype(BF16)
        own2[at, :] = dot(hid[at, :], wd[...], NN).astype(BF16)
        exchange(1, c, own2, got2).start()
        return carry

    lax.fori_loop(0, chunks, feed, 0)
    loads[6].wait()

    def feed_back(c, carry):
        at = rows_of(c)
        exchange(1, c, own2, got2).wait_recv()

        def norms(start, at):
            hat, scale = normalize(own2[at, :].astype(F32) + got2[at, :].astype(F32))
            out = middle[at, :] + (hat * gain(3) + bias(3))
            result_ref[at, :] = out.astype(BF16)
            grad = cot[at, :].astype(F32) * real_rows(start)
            gffn[at, :] = norm_pull(hat, scale, gain(3), grad).astype(BF16)
            acc[2] += fold_rows(grad * hat)
            acc[5] += fold_rows(grad)
            hat, scale = normalize(middle[at, :])
            middle[at, :] = hat
            lse[at, :] = jnp.where(lane_index((BLOCK, LANES)) == 2 * pairs + 1, scale, lse[at, :])

        blocks(c, norms)
        grad = gffn[at, :]
        span = 512
        for n in range(inner // span):
            cols = pl.ds(n * span, span)
            grown = dot(grad, wd[cols, :], NT)
            slope[at, cols] = (grown * slope[at, cols].astype(F32)).astype(BF16)
        exchange(1, c, own2, got2).wait_send()
        own2[at, :] = dot(slope[at, :], wu[...], NT).astype(BF16)
        exchange(2, c, own2, got3).start()
        return carry

    lax.fori_loop(0, chunks, feed_back, 0)
    release(range(2 * count), 0)

    def parts(source, first_unit):
        units = range(first_unit, first_unit + count)
        return [(cols_at(source, i * wide, wide), held(u), 0, table[u][3]) for i, u in enumerate(units)]

    weight_grad(gffn, parts(hid, 0))
    release(range(2 * count), 1)
    for u in range(count):
        send(u, 0)
    weight_grad(nmid, parts(slope, count))
    for level in range(levels):
        release(range(attn_first, norm_unit), level)
    for u in range(count, 2 * count):
        send(u, 0)
    nin_back = pltpu.make_async_copy(nin_hbm, nin, save_sem.at[1])
    nin_back.start()
    for u in range(count):
        take(u, 0)
    gk[...] = jnp.zeros_like(gk)
    gv[...] = jnp.zeros_like(gv)

    agenda = {}
    for (u, level), slot in sorted(SLOTS.items(), key=lambda item: item[1]):
        agenda.setdefault(slot, []).append((u, level))

    tokens_back = pltpu.make_async_copy(tokens_hbm, got2, save_sem.at[2])

    def attend_back(c, carry):
        at = rows_of(c)

        @pl.when(c == chunks - 1)
        def _():
            ahead[...] = dot(q[:CHUNK, :], wq[...], NT)

        exchange(2, c, own2, got3).wait_recv()

        def norms(start, at):
            grad = own2[at, :].astype(F32) + got3[at, :].astype(F32)
            hat, scale = middle[at, :], lse[at, 2 * pairs + 1 : 2 * pairs + 2]
            out = cot[at, :].astype(F32) * real_rows(start)
            mid = out + norm_pull(hat, scale, gain(2), grad)
            acc[1] += fold_rows(grad * hat)
            acc[4] += fold_rows(grad)
            middle[at, :] = mid
            hat, scale = attn_total[at, :], lse[at, 2 * pairs : 2 * pairs + 1]
            gattn[at, :] = norm_pull(hat, scale, gain(1), mid).astype(BF16)
            acc[0] += fold_rows(mid * hat)
            acc[3] += fold_rows(mid)

        blocks(c, norms)

        @pl.when(c == chunks - 1)
        def _():
            pl.semaphore_signal(free_sem.at[4 * levels], inc=1, device_id=peer, device_id_type=MESH)
            tokens_back.start()

        gatt[...] = dot(gattn[at, :], wo[...], NT).astype(BF16)

        def pair(p):
            cols = pl.ds(p * LANES, LANES)
            keys, values, grad = k[:, cols], v[:, cols], gatt[:, cols]
            query, grads = stack_pair(q[at, cols]), stack_pair(grad)
            through = stack_pair(grad.astype(F32) * att[at, cols].astype(F32))
            shift = jnp.sum(through, axis=1, keepdims=True)
            logs = lse[at, :]
            log = jnp.concatenate([logs[:, 2 * p : 2 * p + 1], logs[:, 2 * p + 1 : 2 * p + 2]], axis=0)
            weights = jnp.exp(dot(query, keys, NT) + key_bias - log)
            slopes = (weights * (dot(grads, values, NT) - shift)).astype(BF16)
            q[at, cols] = (join_pair(dot(slopes, keys, NN)) * 0.125).astype(BF16)
            gk[cols, :] += dot(query, slopes, TN)
            gv[cols, :] += dot(grads, weights.astype(BF16), TN)

        for slot, work in agenda.items():

            @pl.when(c == slot)
            def _(work=work):
                for unit, level in work:
                    take(unit, level)

        for p in range(pairs):
            pair(p)
        return carry

    lax.fori_loop(0, chunks, attend_back, 0)
    pl.semaphore_wait(free_sem.at[4 * levels], 1)
    back = got2

    turned = set()

    def turn(c):
        if c not in turned:
            turned.add(c)
            at = rows_of(c)
            k[at, :] = gk[:, at].astype(BF16).T
            v[at, :] = gv[:, at].astype(BF16).T

    def input_part(first, number):
        at = pl.ds(first * CHUNK, number * CHUNK)
        for c in range(first, first + number):
            turn(c)
            exchange(2, c, own2, got3).wait_send()
        part = (ahead[...] if first == 0 else dot(q[at, :], wq[...], NT)) + dot(k[at, :], wk[...], NT) + dot(v[at, :], wv[...], NT)
        own2[at, :] = part.astype(BF16)
        for c in range(first, first + number):
            exchange(3, c, own2, got3).start()

    def project_grads():
        for c in range(chunks):
            turn(c)
        nin_back.wait()
        weight_grad(nin, [(ref, hid, i * local, WAYS[attn_first + i]) for i, ref in enumerate((q, k, v))])
        for u in range(attn_first, attn_first + 3):
            send(u, 0)

    def out_grad():
        weight_grad(gattn, [(att, hid, 3 * local, WAYS[attn_first + 3])])
        send(attn_first + 3, 0)

    def norm_grads():
        tokens_back.wait()

        def first_norm(c, carry):
            def sums(start, at):
                hat, _ = normalize(back[at, :].astype(F32))
                grad = own2[at, :].astype(F32)
                acc[6] += fold_rows(grad * hat)
                acc[7] += fold_rows(grad)

            blocks(c, sums)
            return carry

        lax.fori_loop(0, chunks, first_norm, 0)
        sums = jnp.concatenate([jnp.sum(acc[j], axis=0, keepdims=True) for j in (6, 0, 1, 2, 7, 3, 4, 5)])
        for index in range(dp_size):
            tile, shift = divmod(index * blk, LANES)
            piece = sums[:, tile * LANES : (tile + 1) * LANES]
            if shift:
                piece = pltpu.roll(piece, LANES - shift, 1)
            spot = 8 * fixed_position(index, 0)
            norm_held[spot : spot + 8, :] = piece
        send(norm_unit, 0)

    def input_grad(c):
        at = rows_of(c)
        exchange(3, c, own2, got3).wait_recv()

        def norms(start, at):
            grad = own2[at, :].astype(F32) + got3[at, :].astype(F32)
            hat, scale = normalize(back[at, :].astype(F32))
            total = middle[at, :] + norm_pull(hat, scale, gain(0), grad)
            ingrad_ref[at, :] = total.astype(BF16)

        blocks(c, norms)

    tell = pltpu.make_async_remote_copy(
        src_ref=norm_ref,
        dst_ref=norm_peer,
        send_sem=send_sem.at[4 * chunks],
        recv_sem=recv_sem.at[4 * chunks],
        device_id=peer,
        device_id_type=MESH,
    )
    everything = [(u, level) for level in range(levels) for u in range(norm_unit + 1)]
    early = set(SLOTS) | {(u, 0) for u in range(count)}
    plan = PLAN
    if levels != 4:
        plan = [("part", 0, 1), "project", "out", ("part", 1, chunks - 1), "norm"] + [x for x in everything if x not in early]
        plan += [("grad", c) for c in range(chunks)]
    assert sorted(x for x in plan if not isinstance(x[0], str)) == sorted(set(everything) - early)
    def finished(level):
        for u in range(norm_unit + 1):
            if level < levels - 1 or u != norm_unit - 1:
                hop(u, level).wait_send()

    if levels == 4:
        for level, spot in ((3, ("grad", chunks - 1)), (2, (7, 3)), (1, (7, 2)), (0, ("grad", 3))):
            plan = plan[: plan.index(spot)] + [("done", level)] + plan[plan.index(spot) :]
    else:
        plan = plan + [("done", level) for level in range(levels)]
    for item in plan:
        if item == "project":
            project_grads()
        elif item == "out":
            out_grad()
        elif item == "norm":
            norm_grads()
        elif item[0] == "done":
            finished(item[1])
        elif item[0] == "part":
            input_part(*item[1:])
        elif item[0] == "grad":
            input_grad(item[1])
        else:
            take(*item)
            if item == (norm_unit, levels - 1):
                tell.start()
    tell.wait()
    row = lax.broadcasted_iota(jnp.int32, norm_ref.shape, 0)
    norm_ref[...] += jnp.where(lax.rem(row, 4) == 0, norm_peer[...], 0.0)

    def drain(c, carry):
        exchange(0, c, att, att_peer).wait_send()
        exchange(3, c, own2, got3).wait_send()
        return carry

    lax.fori_loop(0, chunks, drain, 0)
    for side in range(2):
        wo_cross(side).wait_send()
    hop(norm_unit - 1, levels - 1).wait_send()


def run_layer(lengths, tokens, wq, wk, wv, wo, wu, wd, gains, biases, cot):
    dp_size = lax.axis_size("dp")
    rows, width = tokens.shape
    local, inner = wq.shape[1], wu.shape[1]
    chunks = rows // CHUNK
    levels = dp_size.bit_length() - 1
    units = 2 * (inner // 1024) + 5
    shape = jax.ShapeDtypeStruct
    anywhere = pl.BlockSpec(memory_space=pl.ANY)
    vmem = pl.BlockSpec(memory_space=pltpu.VMEM)
    wide = (rows, width)
    thin = (rows, local)
    blk = width // dp_size
    outs = [
        pltpu.VMEM(wide, BF16), pltpu.VMEM(wide, BF16), shape(wide, BF16),
        pltpu.VMEM((blk, inner), F32), pltpu.VMEM((blk, inner), F32), pltpu.VMEM((blk, 4 * local), F32),
        pltpu.VMEM((8, LANES), F32),
    ]
    scratch = [
        pltpu.VMEM(wide, BF16), pltpu.VMEM(wq.shape, BF16), pltpu.VMEM(wk.shape, BF16), pltpu.VMEM(wv.shape, BF16),
        pltpu.VMEM(wo.shape, BF16), pltpu.VMEM(wu.shape, BF16), pltpu.VMEM(wd.shape, BF16), pltpu.VMEM(wide, BF16),
        pltpu.VMEM(wide, BF16), pltpu.VMEM(thin, BF16), pltpu.VMEM(thin, BF16), pltpu.VMEM(thin, BF16),
        pltpu.VMEM(thin, BF16), pltpu.VMEM((rows, LANES), F32),
        pltpu.VMEM(wide, F32), pltpu.VMEM(wide, BF16), pltpu.VMEM(wide, BF16), pltpu.VMEM(wide, BF16),
        pltpu.VMEM(wide, F32), pltpu.VMEM((rows, inner), BF16), pltpu.VMEM((rows, inner), BF16),
        pltpu.VMEM(wide, BF16), pltpu.VMEM(wide, BF16), pltpu.VMEM((CHUNK, local), BF16),
        pltpu.VMEM((local, rows), F32), pltpu.VMEM((local, rows), F32), pltpu.VMEM((CHUNK, width), F32),
        pltpu.VMEM((8, 8, width), F32),
        pltpu.VMEM((8 * dp_size, LANES), F32), pltpu.VMEM((8 * dp_size, LANES), F32), pltpu.VMEM((8, LANES), F32),
        pltpu.SemaphoreType.DMA((rows // PROJECT,)), pltpu.SemaphoreType.DMA((7,)), pltpu.SemaphoreType.DMA((16,)), pltpu.SemaphoreType.DMA((3,)),
        pltpu.SemaphoreType.DMA((4 * chunks + 1,)), pltpu.SemaphoreType.DMA((4 * chunks + 1,)),
        pltpu.SemaphoreType.DMA((units * levels,)), pltpu.SemaphoreType.DMA((units * levels,)),
        pltpu.SemaphoreType.REGULAR((4 * levels + 1,)),
    ]
    return pl.pallas_call(
        functools.partial(layer_kernel, dp_size),
        out_shape=outs,
        in_specs=[pl.BlockSpec(memory_space=pltpu.SMEM)] + [anywhere] * 7 + [vmem, vmem, anywhere],
        out_specs=[vmem, vmem, anywhere] + [vmem] * 4,
        scratch_shapes=scratch,
        compiler_params=pltpu.CompilerParams(
            collective_id=0, has_side_effects=True, vmem_limit_bytes=VMEM_BYTES - 4 * rows * width - 8 * blk * (inner + 2 * local)
        ),
        name="layer",
    )(lengths, tokens, wq, wk, wv, wo, wu, wd, gains, biases, cot)


def finish_kernel(
    result_in, ingrad_in, up_in, down_in, attn_in, norm_in, result, ingrad, query, key, value, out, up, down, gain, bias, sem
):
    local = query.shape[1]
    pairs = [(result_in, result), (ingrad_in, ingrad), (up_in, up), (down_in, down)]
    pairs += [(attn_in.at[:, pl.ds(i * local, local)], ref) for i, ref in enumerate((query, key, value, out))]
    copies = [pltpu.make_async_copy(source, target, sem.at[i]) for i, (source, target) in enumerate(pairs)]
    for copy in copies:
        copy.start()
    blk = gain.shape[1]
    gain[...] = norm_in[:4, :blk]
    bias[...] = norm_in[4:, :blk]
    for copy in copies:
        copy.wait()


def on_device(tokens, lengths, wq, wk, wv, wo, wu, wd, gains, biases, cot):
    local, inner = wq.shape[1], wu.shape[1]
    result, input_grad, _, up, down, attn, norms = run_layer(
        lengths, tokens, wq, wk, wv, wo, wu, wd, gains, biases, cot
    )
    blk = up.shape[0]
    shape = jax.ShapeDtypeStruct
    anywhere = pl.BlockSpec(memory_space=pl.ANY)
    vmem = pl.BlockSpec(memory_space=pltpu.VMEM)
    result, input_grad, query, key, value, out, up, down, gain, bias = pl.pallas_call(
        finish_kernel,
        out_shape=[shape(result.shape, BF16), shape(result.shape, BF16)]
        + [shape((blk, local), F32)] * 4
        + [shape((blk, inner), F32)] * 2
        + [shape((4, blk), F32)] * 2,
        in_specs=[vmem] * 6,
        out_specs=[anywhere] * 8 + [vmem] * 2,
        scratch_shapes=[pltpu.SemaphoreType.DMA((8,))],
        compiler_params=pltpu.CompilerParams(vmem_limit_bytes=4 * 1024 * 1024),
        name="finish",
    )(result, input_grad, up, down, attn, norms)
    return result, input_grad, query, key, value, out.T, up, down.T, gain, bias


def solution(mesh):
    in_specs = (
        P("dp", None), P("dp"), P(None, "tensor"), P(None, "tensor"), P(None, "tensor"), P("tensor", None),
        P(None, "tensor"), P("tensor", None), P(), P(), P("dp", None),
    )
    out_specs = (
        P("dp", None), P("dp", None), P("dp", "tensor"), P("dp", "tensor"), P("dp", "tensor"), P("tensor", "dp"),
        P("dp", "tensor"), P("tensor", "dp"), P(None, "dp"), P(None, "dp"),
    )
    return jax.shard_map(on_device, mesh=mesh, in_specs=in_specs, out_specs=out_specs, check_vma=False)
```

```python
import functools

import jax
import jax.numpy as jnp
from jax import lax
from jax.experimental import pallas as pl
from jax.experimental.pallas import tpu as pltpu
from jax.sharding import PartitionSpec as P

HD = 64
LANES = 128
EPS = 1e-05
CHUNK = 128
PROJECT = 256
BLOCK = 128
NEG = -1000000000.0
F32 = jnp.float32
BF16 = jnp.bfloat16
MESH = pl.DeviceIdType.MESH
NN = (((1,), (0,)), ((), ()))
NT = (((1,), (1,)), ((), ()))
TN = (((0,), (0,)), ((), ()))
ROOT = 0.7978845608028654
CUBE = 0.044715
UNROLL = 2
VMEM_BYTES = 255 * 256 * 1024
WAYS = (0, 0, 1, 0, 0, 0, 0, 0)
SLOTS = {(2, 0): 1, (3, 0): 2, (0, 1): 4, (2, 1): 5, (1, 1): 7, (0, 2): 7}
PLAN = [
    ("part", 1, 1), "query", (3, 1), ("part", 2, 2), (4, 0), "keyvalue", (2, 2), "out", (5, 0), (1, 2), (0, 3), (6, 0), ("part", 4, 2),
    (7, 0), ("part", 6, 2), "norm", (3, 2), (8, 0), (2, 3), ("grad", 0), ("grad", 1), (4, 1), ("grad", 2), (1, 3), (8, 1), (5, 1), (4, 2),
    (3, 3), (8, 2), ("grad", 3), (6, 1), (5, 2), (4, 3), ("grad", 4), (7, 1), (6, 2), (8, 3), (5, 3), ("grad", 5), (7, 2), (6, 3),
    ("grad", 6), (7, 3), ("grad", 7),
]


def dot(left, right, dims):
    return lax.dot_general(left, right, dims, preferred_element_type=F32)


def row_mean(values):
    return jnp.sum(values, axis=-1, keepdims=True) * (1.0 / values.shape[-1])


def normalize(values):
    centered = values - row_mean(values)
    scale = lax.rsqrt(row_mean(centered * centered) + EPS)
    return centered * scale, scale


def norm_pull(hat, scale, gain, grad):
    weighed = grad * gain
    return scale * (weighed - row_mean(weighed) - hat * row_mean(weighed * hat))


def gelu_both(v):
    square = v * v
    tanh = jnp.tanh(v * (ROOT + (ROOT * CUBE) * square))
    half = 0.5 + 0.5 * tanh
    slope = half + (0.5 * v) * (1.0 - tanh * tanh) * (ROOT + (3.0 * ROOT * CUBE) * square)
    return v * half, slope


def lane_index(shape):
    return lax.broadcasted_iota(jnp.int32, shape, 1)


def head_of_pair(values, side):
    low = lane_index(values.shape) < HD
    return jnp.where(low if side == 0 else jnp.logical_not(low), values, jnp.zeros_like(values))


def stack_pair(values):
    return jnp.concatenate([head_of_pair(values, 0), head_of_pair(values, 1)], axis=0)


def join_pair(stacked):
    first, second = jnp.split(stacked, 2, axis=0)
    return jnp.where(lane_index(first.shape) < HD, first, second)


def fold_rows(values):
    return jnp.sum(values.reshape(-1, 8, values.shape[-1]), axis=0)


def layer_kernel(
    dp_size,
    length_ref, tokens_hbm, wq_hbm, wk_hbm, wv_hbm, wo_hbm, wu_hbm, wd_hbm, gain_ref, bias_ref, cot_hbm,
    result_ref, ingrad_ref, nin_hbm, up_ref, down_ref, attn_ref, norm_ref,
    tokens, wq, wk, wv, wo, wu, wd, cot,
    nin, q, k, v, att, lse, attn_total, own2, got2, got3, middle, hid, slope, gffn, gattn, gk, gv,
    acc, norm_held, norm_box, norm_peer,
    token_sem, load_sem, wo_sem, save_sem, send_sem, recv_sem, give_sem, take_sem, free_sem,
):
    rows = tokens.shape[0]
    chunks = rows // CHUNK
    local = q.shape[1]
    pairs = local // LANES
    inner = hid.shape[1]
    peer = {"tensor": 1 - lax.axis_index("tensor")}

    def load(index, source, target):
        return pltpu.make_async_copy(source, target, load_sem.at[index])

    def save(index, source, target):
        return pltpu.make_async_copy(source, target, save_sem.at[index])

    def span_of(c):
        return pl.ds(pl.multiple_of(c * PROJECT, PROJECT), PROJECT)

    def token_load(c):
        at = span_of(c)
        return pltpu.make_async_copy(tokens_hbm.at[at], tokens.at[at], token_sem.at[c])

    for c in range(rows // PROJECT):
        token_load(c).start()
    loads = [
        load(0, wq_hbm, wq), load(1, wk_hbm, wk), load(2, wv_hbm, wv),
        load(3, wo_hbm, wo), load(4, wu_hbm, wu), load(5, wd_hbm, wd), load(6, cot_hbm, cot),
    ]
    for copy in loads[:3]:
        copy.start()

    levels = dp_size.bit_length() - 1
    me = lax.axis_index("dp")
    bits = [lax.rem(me // (1 << b), 2) for b in range(levels)]
    partner = [{"dp": me + (1 << b) * (1 - 2 * bits[b])} for b in range(levels)]
    half = [dp_size >> (level + 1) for level in range(levels)]
    routes = [list(range(levels)), [0] + list(range(2, levels)) + [1]]
    keep, give = [], []
    for route in routes:
        base, kept, given = 0, [], []
        for level in range(levels):
            kept.append(base + bits[route[level]] * half[level])
            given.append(base + (1 - bits[route[level]]) * half[level])
            base = kept[-1]
        keep.append(kept)
        give.append(given)

    def position(index, way):
        return sum(lax.rem(index // (1 << b), 2) * half[level] for level, b in enumerate(routes[way]))

    def fixed_position(index, way):
        return sum((index >> b) % 2 * half[level] for level, b in enumerate(routes[way]))

    barrier = pltpu.get_barrier_semaphore()
    for other in [peer] + partner:
        pl.semaphore_signal(barrier, inc=1, device_id=other, device_id_type=MESH)

    width = tokens.shape[1]
    blk = width // dp_size

    split = local // 4
    mine, far = lax.rem(me, 4), lax.rem(me + 2, 4)
    att_peer = gffn.at[:, pl.ds(0, local)]

    def wo_piece(which, side):
        start = pl.multiple_of(side * local + which * split, split)
        return gffn.at[pl.ds(start, split), pl.ds(width - local, local)]

    def wo_cross(side):
        return pltpu.make_async_remote_copy(
            src_ref=wo_hbm.at[pl.ds(pl.multiple_of(mine * split, split), split), pl.ds(side * local, local)],
            dst_ref=wo_piece(mine, side),
            send_sem=wo_sem.at[side],
            recv_sem=wo_sem.at[2 + side],
            device_id=peer,
            device_id_type=MESH,
        )

    def wo_share(step, side):
        which = far if step == 2 else mine
        return pltpu.make_async_remote_copy(
            src_ref=wo_piece(which, side),
            dst_ref=wo_piece(which, side),
            send_sem=wo_sem.at[4 * step + 4 + side],
            recv_sem=wo_sem.at[4 * step + 6 + side],
            device_id=partner[1] if step == 0 else partner[0],
            device_id_type=MESH,
        )

    wide = 1024
    count = inner // wide
    rows_at = lambda ref, start, size: ref.at[pl.ds(start, size), :]
    cols_at = lambda ref, start, size: ref.at[:, pl.ds(start, size)]
    table = [(rows_at(wd, u * width, width), cols_at(down_ref, u * wide, wide), None, WAYS[u]) for u in range(count)]
    table += [
        (cols_at(wu, u * wide, wide), cols_at(up_ref, u * wide, wide), None, WAYS[count + u]) for u in range(count)
    ]
    attn_first = 2 * count
    for i in range(4):
        cols = pl.ds(i * local, local)
        table.append((hid.at[:, cols], attn_ref.at[:, cols], cols, WAYS[attn_first + i]))
    norm_unit = len(table)
    table.append((norm_held, norm_ref, None, 1))

    def held(unit):
        return table[unit][0]

    def inbox(unit, level):
        if unit == norm_unit:
            return norm_box.at[pl.ds(8 * (dp_size - 2 * half[level]), 8 * half[level]), :]
        size = half[level] * blk
        if unit >= attn_first:
            return slope.at[pl.ds(width - 2 * size, size), table[unit][2]]
        if level == 0:
            return rows_at(got2 if unit < count else tokens, (unit % count) * size, size)
        if level == 1:
            return rows_at(gffn, unit * size, size)
        return rows_at(tokens, 2 * count * (width // 4 - 2 * size) + unit * size, size)

    def block_of(unit):
        return 8 if unit == norm_unit else blk

    def hop(unit, level):
        way = table[unit][3]
        rows_each = block_of(unit)
        index = unit * levels + level
        start = pl.multiple_of(give[way][level] * rows_each, 8)
        return pltpu.make_async_remote_copy(
            src_ref=held(unit).at[pl.ds(start, half[level] * rows_each), :],
            dst_ref=inbox(unit, level),
            send_sem=give_sem.at[index],
            recv_sem=take_sem.at[index],
            device_id=partner[routes[way][level]],
            device_id_type=MESH,
        )

    def credit(unit, level):
        return free_sem.at[(2 * levels if unit >= attn_first else 0) + 2 * level + table[unit][3]]

    def release(which, level):
        for way in range(2):
            same = [u for u in which if table[u][3] == way]
            if same:
                pl.semaphore_signal(
                    credit(same[0], level), inc=len(same), device_id=partner[routes[way][level]], device_id_type=MESH
                )

    def send(unit, level):
        if unit != norm_unit:
            pl.semaphore_wait(credit(unit, level), 1)
        hop(unit, level).start()

    def take(unit, level):
        hop(unit, level).wait_recv()
        rows_each = block_of(unit)
        size = half[level] * rows_each
        step_rows = min(size, 32)
        ours, came = held(unit), inbox(unit, level)
        last = level == levels - 1
        target = table[unit][1]
        first = keep[table[unit][3]][level] * rows_each

        def add(b, carry):
            here = pl.multiple_of(b * step_rows, step_rows)
            there = pl.multiple_of(first + b * step_rows, 8)
            total = ours[pl.ds(there, step_rows), :].astype(F32) + came[pl.ds(here, step_rows), :].astype(F32)
            if last:
                target[pl.ds(here, step_rows), :] = total
            else:
                ours[pl.ds(there, step_rows), :] = total.astype(ours.dtype)
            return carry

        lax.fori_loop(0, size // step_rows, add, 0)
        if unit == 2 * count - 1 and level == 0:
            for other in range(2, levels):
                release(range(2 * count), other)
        if not last:
            send(unit, level + 1)

    def weight_grad(left, groups):
        span = 256

        def part(j, carry):
            turned = left[:, pl.ds(pl.multiple_of(j * span, span), span)].T
            for right, ref, at, way in groups:
                grad = dot(turned, right[...], NN).astype(BF16)
                for i in range(span // blk):
                    start = pl.multiple_of(position(j * (span // blk) + i, way) * blk, 8)
                    ref[pl.ds(start, blk), pl.ds(at, grad.shape[1])] = grad[i * blk : (i + 1) * blk]
            return carry

        lax.fori_loop(0, width // span, part, 0)

    def rows_of(c):
        return pl.ds(pl.multiple_of(c * CHUNK, CHUNK), CHUNK)

    def exchange(step, c, source, target):
        index = step * chunks + c
        return pltpu.make_async_remote_copy(
            src_ref=source.at[rows_of(c)],
            dst_ref=target.at[rows_of(c)],
            send_sem=send_sem.at[index],
            recv_sem=recv_sem.at[index],
            device_id=peer,
            device_id_type=MESH,
        )

    length = length_ref[0]

    def gain(j):
        return gain_ref[j : j + 1, :]

    def bias(j):
        return bias_ref[j : j + 1, :]

    def blocks(c, body, size=CHUNK):
        def step(b, carry):
            start = pl.multiple_of(c * size + b * BLOCK, BLOCK)
            body(start, pl.ds(start, BLOCK))
            return carry

        lax.fori_loop(0, size // BLOCK, step, 0)

    def real_rows(start):
        index = start + lax.broadcasted_iota(jnp.int32, (BLOCK, 1), 0)
        return jnp.where(index < length, 1.0, 0.0)

    acc[...] = jnp.zeros_like(acc)

    def query_rows(at):
        q[at, :] = (dot(nin[at, :], wq[...], NN) * 0.125).astype(BF16)

    def norm_in(start, at):
        hat, _ = normalize(tokens[at, :].astype(F32))
        nin[at, :] = (hat * gain(0) + bias(0)).astype(BF16)

    spans = rows // PROJECT
    for c in range(spans // 2):
        token_load(c).wait()
        blocks(c, norm_in, PROJECT)
        if c == 0:
            pl.semaphore_wait(barrier, levels + 1)
            for side in range(2):
                wo_cross(side).start()
    for c in range(spans // 2, spans):
        token_load(c).wait()
    for copy in loads[3:]:
        copy.start()
    for copy in loads[:3]:
        copy.wait()
    for h in range(2):
        at = pl.ds(h * rows // 2, rows // 2)
        normed = nin[at, :]
        k[at, :] = dot(normed, wk[...], NN).astype(BF16)
        v[at, :] = dot(normed, wv[...], NN).astype(BF16)
        if h == 0:
            for b in range(rows // 2 // BLOCK):
                start = rows // 2 + b * BLOCK
                norm_in(start, pl.ds(start, BLOCK))
    query_rows(span_of(0))
    save(0, nin, nin_hbm).start()

    key_bias = jnp.where(lane_index((1, rows)) < length, 0.0, NEG)

    def attend(c, carry):
        at = rows_of(c)

        ratio = PROJECT // CHUNK

        @pl.when(jnp.logical_and(lax.rem(c, ratio) == 0, c > 0))
        def _():
            query_rows(span_of(c // ratio))

        def pair(p, carry):
            cols = pl.ds(pl.multiple_of(p * LANES, LANES), LANES)
            keys, values = k[:, cols], v[:, cols]
            scores = dot(stack_pair(q[at, cols]), keys, NT) + key_bias
            top = jnp.max(scores, axis=1, keepdims=True)
            weights = jnp.exp(scores - top)
            total = jnp.sum(weights, axis=1, keepdims=True)
            mixed = dot(weights.astype(BF16), values, NN) / total
            first, second = jnp.split(top + jnp.log(total), 2, axis=0)
            logs = lse[at, :]
            lane = lane_index(logs.shape)
            lse[at, :] = jnp.where(lane == 2 * p, first, jnp.where(lane == 2 * p + 1, second, logs))
            att[at, cols] = join_pair(mixed).astype(BF16)
            return carry

        lax.fori_loop(0, pairs, pair, 0, unroll=UNROLL)
        exchange(0, c, att, att_peer).start()

        @pl.when(c == 2)
        def _():
            for side in range(2):
                wo_cross(side).wait_recv()
                wo_share(0, side).start()
                wo_share(1, side).start()

        @pl.when(c == chunks - 2)
        def _():
            for side in range(2):
                wo_share(0, side).wait_recv()
                wo_share(2, side).start()

        return carry

    lax.fori_loop(0, chunks, attend, 0)
    for copy in loads[3:6]:
        copy.wait()
    for side in range(2):
        wo_share(0, side).wait_send()
        wo_share(1, side).wait()
        wo_share(2, side).wait()
    save(0, nin, nin_hbm).wait()
    nmid = nin

    def feed(c, carry):
        at = rows_of(c)
        exchange(0, c, att, att_peer).wait_recv()
        ours = dot(att[at, :], wo[...], NN).astype(BF16).astype(F32)
        other = att_peer[at, :]
        for side in range(2):
            cols = pl.ds(side * local, local)
            weight = gffn[pl.ds(side * local, local), pl.ds(width - local, local)]
            theirs = dot(other, weight, NN).astype(BF16).astype(F32)
            attn_total[at, cols] = ours[:, side * local : (side + 1) * local] + theirs

        def norms(start, at):
            hat, scale = normalize(attn_total[at, :])
            attn_total[at, :] = hat
            lse[at, :] = jnp.where(lane_index((BLOCK, LANES)) == 2 * pairs, scale, lse[at, :])
            mid = tokens[at, :].astype(F32) + (hat * gain(1) + bias(1))
            middle[at, :] = mid
            hat, _ = normalize(mid)
            nmid[at, :] = (hat * gain(2) + bias(2)).astype(BF16)

        blocks(c, norms)
        normed = nmid[at, :]
        span = 512
        for n in range(inner // span):
            cols = pl.ds(n * span, span)
            value, grade = gelu_both(dot(normed, wu[:, cols], NN))
            hid[at, cols] = value.astype(BF16)
            slope[at, cols] = grade.astype(BF16)
        own2[at, :] = dot(hid[at, :], wd[...], NN).astype(BF16)
        exchange(1, c, own2, got2).start()
        return carry

    lax.fori_loop(0, chunks, feed, 0)
    loads[6].wait()

    def feed_back(c, carry):
        at = rows_of(c)
        exchange(1, c, own2, got2).wait_recv()

        def norms(start, at):
            hat, scale = normalize(own2[at, :].astype(F32) + got2[at, :].astype(F32))
            out = middle[at, :] + (hat * gain(3) + bias(3))
            result_ref[at, :] = out.astype(BF16)
            grad = cot[at, :].astype(F32) * real_rows(start)
            gffn[at, :] = norm_pull(hat, scale, gain(3), grad).astype(BF16)
            acc[2] += fold_rows(grad * hat)
            acc[5] += fold_rows(grad)
            hat, scale = normalize(middle[at, :])
            middle[at, :] = hat
            lse[at, :] = jnp.where(lane_index((BLOCK, LANES)) == 2 * pairs + 1, scale, lse[at, :])

        blocks(c, norms)
        grad = gffn[at, :]
        span = 512
        for n in range(inner // span):
            cols = pl.ds(n * span, span)
            grown = dot(grad, wd[cols, :], NT)
            slope[at, cols] = (grown * slope[at, cols].astype(F32)).astype(BF16)
        exchange(1, c, own2, got2).wait_send()
        own2[at, :] = dot(slope[at, :], wu[...], NT).astype(BF16)
        exchange(2, c, own2, got3).start()
        return carry

    lax.fori_loop(0, chunks, feed_back, 0)
    release(range(2 * count), 0)

    def parts(source, first_unit):
        units = range(first_unit, first_unit + count)
        return [(cols_at(source, i * wide, wide), held(u), 0, table[u][3]) for i, u in enumerate(units)]

    weight_grad(gffn, parts(hid, 0))
    release(range(2 * count), 1)
    for u in range(count):
        send(u, 0)
    weight_grad(nmid, parts(slope, count))
    for level in range(levels):
        release(range(attn_first, norm_unit), level)
    for u in range(count, 2 * count):
        send(u, 0)
    nin_back = pltpu.make_async_copy(nin_hbm, nin, save_sem.at[1])
    nin_back.start()
    for u in range(count):
        take(u, 0)
    gk[...] = jnp.zeros_like(gk)
    gv[...] = jnp.zeros_like(gv)

    agenda = {}
    for (u, level), slot in sorted(SLOTS.items(), key=lambda item: item[1]):
        agenda.setdefault(slot, []).append((u, level))

    tokens_back = pltpu.make_async_copy(tokens_hbm, got2, save_sem.at[2])

    gatt = hid.at[pl.ds(0, CHUNK), pl.ds(0, local)]

    def attend_back(c, carry):
        at = rows_of(c)

        @pl.when(c == chunks - 1)
        def _():
            attn_total[:CHUNK, :] = dot(q[:CHUNK, :], wq[...], NT)

        for slot, work in agenda.items():

            @pl.when(c == slot)
            def _(work=work):
                for unit, level in work:
                    take(unit, level)

        exchange(2, c, own2, got3).wait_recv()

        def norms(start, at):
            grad = own2[at, :].astype(F32) + got3[at, :].astype(F32)
            hat, scale = middle[at, :], lse[at, 2 * pairs + 1 : 2 * pairs + 2]
            out = cot[at, :].astype(F32) * real_rows(start)
            mid = out + norm_pull(hat, scale, gain(2), grad)
            acc[1] += fold_rows(grad * hat)
            acc[4] += fold_rows(grad)
            middle[at, :] = mid
            hat, scale = attn_total[at, :], lse[at, 2 * pairs : 2 * pairs + 1]
            gattn[at, :] = norm_pull(hat, scale, gain(1), mid).astype(BF16)
            acc[0] += fold_rows(mid * hat)
            acc[3] += fold_rows(mid)

        blocks(c, norms)

        @pl.when(c == chunks - 1)
        def _():
            pl.semaphore_signal(free_sem.at[4 * levels], inc=1, device_id=peer, device_id_type=MESH)
            tokens_back.start()

        gatt[...] = dot(gattn[at, :], wo[...], NT).astype(BF16)

        def pair(p, first, last, with_queries=True):
            cols = pl.ds(p * LANES, LANES)
            span = slice(0, last)
            keys, values, grad = k[span, cols], v[span, cols], gatt[:, cols]
            query, grads = stack_pair(q[at, cols]), stack_pair(grad)
            through = stack_pair(grad.astype(F32) * att[at, cols].astype(F32))
            shift = jnp.sum(through, axis=1, keepdims=True)
            logs = lse[at, :]
            log = jnp.concatenate([logs[:, 2 * p : 2 * p + 1], logs[:, 2 * p + 1 : 2 * p + 2]], axis=0)
            weights = jnp.exp(dot(query, keys, NT) + key_bias[:, span] - log)
            slopes = (weights * (dot(grads, values, NT) - shift)).astype(BF16)
            if with_queries:
                q[at, cols] = (join_pair(dot(slopes, keys, NN)) * 0.125).astype(BF16)
            gk[cols, first:last] += dot(query, slopes[:, first:], TN)
            gv[cols, first:last] += dot(grads, weights.astype(BF16)[:, first:], TN)

        @pl.when(c < chunks - 1)
        def _():
            for p in range(pairs):
                pair(p, 0, rows)

        @pl.when(c == chunks - 1)
        def _():
            for p in range(pairs):
                pair(p, 0, CHUNK, False)
            pl.semaphore_wait(free_sem.at[4 * levels], 1)
            exchange(2, 0, own2, got3).wait_send()
            part = attn_total[:CHUNK, :] + dot(gk[:, :CHUNK].astype(BF16).T, wk[...], NT)
            part = part + dot(gv[:, :CHUNK].astype(BF16).T, wv[...], NT)
            own2[:CHUNK, :] = part.astype(BF16)
            exchange(3, 0, own2, got3).start()
            for p in range(pairs):
                pair(p, CHUNK, rows)

        return carry

    lax.fori_loop(0, chunks, attend_back, 0)
    back = got2

    turned = set()

    def turn(c):
        if c not in turned:
            turned.add(c)
            at = rows_of(c)
            k[at, :] = gk[:, at].astype(BF16).T
            v[at, :] = gv[:, at].astype(BF16).T

    def input_part(first, number):
        at = pl.ds(first * CHUNK, number * CHUNK)
        for c in range(first, first + number):
            turn(c)
            exchange(2, c, own2, got3).wait_send()
        part = dot(q[at, :], wq[...], NT) + dot(k[at, :], wk[...], NT) + dot(v[at, :], wv[...], NT)
        own2[at, :] = part.astype(BF16)
        for c in range(first, first + number):
            exchange(3, c, own2, got3).start()

    def project_grads(which):
        for c in range(chunks):
            turn(c)
        if 0 in which:
            nin_back.wait()
        sources = (q, k, v)
        weight_grad(nin, [(sources[i], hid, i * local, WAYS[attn_first + i]) for i in which])
        for i in which:
            send(attn_first + i, 0)

    def out_grad():
        weight_grad(gattn, [(att, hid, 3 * local, WAYS[attn_first + 3])])
        send(attn_first + 3, 0)

    def norm_grads():
        tokens_back.wait()

        def first_norm(c, carry):
            def sums(start, at):
                hat, _ = normalize(back[at, :].astype(F32))
                grad = own2[at, :].astype(F32)
                acc[6] += fold_rows(grad * hat)
                acc[7] += fold_rows(grad)

            blocks(c, sums)
            return carry

        lax.fori_loop(0, chunks, first_norm, 0)
        sums = jnp.concatenate([jnp.sum(acc[j], axis=0, keepdims=True) for j in (6, 0, 1, 2, 7, 3, 4, 5)])
        for index in range(dp_size):
            tile, shift = divmod(index * blk, LANES)
            piece = sums[:, tile * LANES : (tile + 1) * LANES]
            if shift:
                piece = pltpu.roll(piece, LANES - shift, 1)
            spot = 8 * fixed_position(index, 1)
            norm_held[spot : spot + 8, :] = piece
        send(norm_unit, 0)

    def input_grad(c):
        at = rows_of(c)
        exchange(3, c, own2, got3).wait_recv()

        def norms(start, at):
            grad = own2[at, :].astype(F32) + got3[at, :].astype(F32)
            hat, scale = normalize(back[at, :].astype(F32))
            total = middle[at, :] + norm_pull(hat, scale, gain(0), grad)
            ingrad_ref[at, :] = total.astype(BF16)

        blocks(c, norms)

    tell = pltpu.make_async_remote_copy(
        src_ref=norm_ref,
        dst_ref=norm_peer,
        send_sem=send_sem.at[4 * chunks],
        recv_sem=recv_sem.at[4 * chunks],
        device_id=peer,
        device_id_type=MESH,
    )
    everything = [(u, level) for level in range(levels) for u in range(norm_unit + 1)]
    early = set(SLOTS) | {(u, 0) for u in range(count)}
    plan = PLAN
    if levels != 4:
        plan = [("part", 1, chunks - 1), "query", "keyvalue", "out", "norm"] + [x for x in everything if x not in early]
        plan += [("grad", c) for c in range(chunks)]
    assert sorted(x for x in plan if not isinstance(x[0], str)) == sorted(set(everything) - early)
    def finished(level):
        for u in range(norm_unit + 1):
            if level < levels - 1 or u != norm_unit - 1:
                hop(u, level).wait_send()

    if levels == 4:
        for level, spot in ((3, ("grad", chunks - 1)), (2, (7, 3)), (1, (7, 2)), (0, ("grad", 3))):
            plan = plan[: plan.index(spot)] + [("done", level)] + plan[plan.index(spot) :]
    else:
        plan = plan + [("done", level) for level in range(levels)]
    for item in plan:
        if item == "query":
            project_grads((0,))
        elif item == "keyvalue":
            project_grads((1, 2))
        elif item == "out":
            out_grad()
        elif item == "norm":
            norm_grads()
        elif item[0] == "done":
            finished(item[1])
        elif item[0] == "part":
            input_part(*item[1:])
        elif item[0] == "grad":
            input_grad(item[1])
        else:
            take(*item)
            if item == (norm_unit, levels - 1):
                tell.start()
    tell.wait()
    row = lax.broadcasted_iota(jnp.int32, norm_ref.shape, 0)
    norm_ref[...] += jnp.where(lax.rem(row, 4) == 0, norm_peer[...], 0.0)

    def drain(c, carry):
        exchange(0, c, att, att_peer).wait_send()
        exchange(3, c, own2, got3).wait_send()
        return carry

    lax.fori_loop(0, chunks, drain, 0)
    for side in range(2):
        wo_cross(side).wait_send()
    hop(norm_unit - 1, levels - 1).wait_send()


def run_layer(lengths, tokens, wq, wk, wv, wo, wu, wd, gains, biases, cot):
    dp_size = lax.axis_size("dp")
    rows, width = tokens.shape
    local, inner = wq.shape[1], wu.shape[1]
    chunks = rows // CHUNK
    levels = dp_size.bit_length() - 1
    units = 2 * (inner // 1024) + 5
    shape = jax.ShapeDtypeStruct
    anywhere = pl.BlockSpec(memory_space=pl.ANY)
    vmem = pl.BlockSpec(memory_space=pltpu.VMEM)
    wide = (rows, width)
    thin = (rows, local)
    blk = width // dp_size
    outs = [
        pltpu.VMEM(wide, BF16), pltpu.VMEM(wide, BF16), shape(wide, BF16),
        pltpu.VMEM((blk, inner), F32), pltpu.VMEM((blk, inner), F32), pltpu.VMEM((blk, 4 * local), F32),
        pltpu.VMEM((8, LANES), F32),
    ]
    scratch = [
        pltpu.VMEM(wide, BF16), pltpu.VMEM(wq.shape, BF16), pltpu.VMEM(wk.shape, BF16), pltpu.VMEM(wv.shape, BF16),
        pltpu.VMEM(wo.shape, BF16), pltpu.VMEM(wu.shape, BF16), pltpu.VMEM(wd.shape, BF16), pltpu.VMEM(wide, BF16),
        pltpu.VMEM(wide, BF16), pltpu.VMEM(thin, BF16), pltpu.VMEM(thin, BF16), pltpu.VMEM(thin, BF16),
        pltpu.VMEM(thin, BF16), pltpu.VMEM((rows, LANES), F32),
        pltpu.VMEM(wide, F32), pltpu.VMEM(wide, BF16), pltpu.VMEM(wide, BF16), pltpu.VMEM(wide, BF16),
        pltpu.VMEM(wide, F32), pltpu.VMEM((rows, inner), BF16), pltpu.VMEM((rows, inner), BF16),
        pltpu.VMEM(wide, BF16), pltpu.VMEM(wide, BF16),
        pltpu.VMEM((local, rows), F32), pltpu.VMEM((local, rows), F32),
        pltpu.VMEM((8, 8, width), F32),
        pltpu.VMEM((8 * dp_size, LANES), F32), pltpu.VMEM((8 * dp_size, LANES), F32), pltpu.VMEM((8, LANES), F32),
        pltpu.SemaphoreType.DMA((rows // PROJECT,)), pltpu.SemaphoreType.DMA((7,)), pltpu.SemaphoreType.DMA((16,)), pltpu.SemaphoreType.DMA((3,)),
        pltpu.SemaphoreType.DMA((4 * chunks + 1,)), pltpu.SemaphoreType.DMA((4 * chunks + 1,)),
        pltpu.SemaphoreType.DMA((units * levels,)), pltpu.SemaphoreType.DMA((units * levels,)),
        pltpu.SemaphoreType.REGULAR((4 * levels + 1,)),
    ]
    return pl.pallas_call(
        functools.partial(layer_kernel, dp_size),
        out_shape=outs,
        in_specs=[pl.BlockSpec(memory_space=pltpu.SMEM)] + [anywhere] * 7 + [vmem, vmem, anywhere],
        out_specs=[vmem, vmem, anywhere] + [vmem] * 4,
        scratch_shapes=scratch,
        compiler_params=pltpu.CompilerParams(
            collective_id=0, has_side_effects=True, vmem_limit_bytes=VMEM_BYTES - 4 * rows * width - 8 * blk * (inner + 2 * local)
        ),
        name="layer",
    )(lengths, tokens, wq, wk, wv, wo, wu, wd, gains, biases, cot)


def finish_kernel(
    result_in, ingrad_in, up_in, down_in, attn_in, norm_in, result, ingrad, query, key, value, out, up, down, gain, bias, sem
):
    local = query.shape[1]
    pairs = [(result_in, result), (ingrad_in, ingrad), (up_in, up), (down_in, down)]
    pairs += [(attn_in.at[:, pl.ds(i * local, local)], ref) for i, ref in enumerate((query, key, value, out))]
    copies = [pltpu.make_async_copy(source, target, sem.at[i]) for i, (source, target) in enumerate(pairs)]
    for copy in copies:
        copy.start()
    blk = gain.shape[1]
    gain[...] = norm_in[:4, :blk]
    bias[...] = norm_in[4:, :blk]
    for copy in copies:
        copy.wait()


def on_device(tokens, lengths, wq, wk, wv, wo, wu, wd, gains, biases, cot):
    local, inner = wq.shape[1], wu.shape[1]
    result, input_grad, _, up, down, attn, norms = run_layer(
        lengths, tokens, wq, wk, wv, wo, wu, wd, gains, biases, cot
    )
    blk = up.shape[0]
    shape = jax.ShapeDtypeStruct
    anywhere = pl.BlockSpec(memory_space=pl.ANY)
    vmem = pl.BlockSpec(memory_space=pltpu.VMEM)
    result, input_grad, query, key, value, out, up, down, gain, bias = pl.pallas_call(
        finish_kernel,
        out_shape=[shape(result.shape, BF16), shape(result.shape, BF16)]
        + [shape((blk, local), F32)] * 4
        + [shape((blk, inner), F32)] * 2
        + [shape((4, blk), F32)] * 2,
        in_specs=[vmem] * 6,
        out_specs=[anywhere] * 8 + [vmem] * 2,
        scratch_shapes=[pltpu.SemaphoreType.DMA((8,))],
        compiler_params=pltpu.CompilerParams(vmem_limit_bytes=4 * 1024 * 1024),
        name="finish",
    )(result, input_grad, up, down, attn, norms)
    return result, input_grad, query, key, value, out.T, up, down.T, gain, bias


def solution(mesh):
    in_specs = (
        P("dp", None), P("dp"), P(None, "tensor"), P(None, "tensor"), P(None, "tensor"), P("tensor", None),
        P(None, "tensor"), P("tensor", None), P(), P(), P("dp", None),
    )
    out_specs = (
        P("dp", None), P("dp", None), P("dp", "tensor"), P("dp", "tensor"), P("dp", "tensor"), P("tensor", "dp"),
        P("dp", "tensor"), P("tensor", "dp"), P(None, "dp"), P(None, "dp"),
    )
    return jax.shard_map(on_device, mesh=mesh, in_specs=in_specs, out_specs=out_specs, check_vma=False)
```

```python
import functools

import jax
import jax.numpy as jnp
from jax import lax
from jax.experimental import pallas as pl
from jax.experimental.pallas import tpu as pltpu
from jax.sharding import PartitionSpec as P

HD = 64
LANES = 128
EPS = 1e-05
CHUNK = 128
PROJECT = 256
BLOCK = 128
NEG = -1000000000.0
F32 = jnp.float32
BF16 = jnp.bfloat16
MESH = pl.DeviceIdType.MESH
NN = (((1,), (0,)), ((), ()))
NT = (((1,), (1,)), ((), ()))
TN = (((0,), (0,)), ((), ()))
ROOT = 0.7978845608028654
CUBE = 0.044715
UNROLL = 2
VMEM_BYTES = 255 * 256 * 1024
WAYS = (0, 0, 1, 0, 0, 0, 0, 1)
SLOTS = {(2, 0): 1, (3, 0): 2, (0, 1): 4, (2, 1): 5, (1, 1): 7, (0, 2): 7}
PLAN = [
    ("part", 1, 1), "query", (3, 1), ("part", 2, 2), (4, 0), "keyvalue", (2, 2), "out", (5, 0), (1, 2), (0, 3), (7, 0), ("part", 4, 2),
    (6, 0), ("part", 6, 2), "norm", (3, 2), (8, 0), (2, 3), ("grad", 0), ("grad", 1), (4, 1), ("grad", 2), (1, 3), (5, 1), (7, 1), (8, 1),
    ("grad", 3), (6, 1), (4, 2), (3, 3), (8, 2), (5, 2), ("grad", 4), (7, 2), (4, 3), (6, 2), (8, 3), (5, 3), ("grad", 5), (7, 3), (6, 3),
    ("grad", 6), ("grad", 7),
]


def dot(left, right, dims):
    return lax.dot_general(left, right, dims, preferred_element_type=F32)


def row_mean(values):
    return jnp.sum(values, axis=-1, keepdims=True) * (1.0 / values.shape[-1])


def normalize(values):
    centered = values - row_mean(values)
    scale = lax.rsqrt(row_mean(centered * centered) + EPS)
    return centered * scale, scale


def norm_pull(hat, scale, gain, grad):
    weighed = grad * gain
    return scale * (weighed - row_mean(weighed) - hat * row_mean(weighed * hat))


def gelu_both(v):
    square = v * v
    tanh = jnp.tanh(v * (ROOT + (ROOT * CUBE) * square))
    half = 0.5 + 0.5 * tanh
    slope = half + (0.5 * v) * (1.0 - tanh * tanh) * (ROOT + (3.0 * ROOT * CUBE) * square)
    return v * half, slope


def lane_index(shape):
    return lax.broadcasted_iota(jnp.int32, shape, 1)


def head_of_pair(values, side):
    low = lane_index(values.shape) < HD
    return jnp.where(low if side == 0 else jnp.logical_not(low), values, jnp.zeros_like(values))


def stack_pair(values):
    return jnp.concatenate([head_of_pair(values, 0), head_of_pair(values, 1)], axis=0)


def join_pair(stacked):
    first, second = jnp.split(stacked, 2, axis=0)
    return jnp.where(lane_index(first.shape) < HD, first, second)


def fold_rows(values):
    return jnp.sum(values.reshape(-1, 8, values.shape[-1]), axis=0)


def layer_kernel(
    dp_size,
    length_ref, tokens_hbm, wq_hbm, wk_hbm, wv_hbm, wo_hbm, wu_hbm, wd_hbm, gain_ref, bias_ref, cot_hbm,
    result_ref, ingrad_ref, nin_hbm, up_ref, down_ref, attn_ref, norm_ref,
    tokens, wq, wk, wv, wo, wu, wd, cot,
    nin, q, k, v, att, lse, attn_total, own2, got2, got3, middle, hid, slope, gffn, gattn, gk, gv,
    acc, norm_held, norm_box, norm_peer,
    token_sem, load_sem, wo_sem, save_sem, send_sem, recv_sem, give_sem, take_sem, free_sem,
):
    rows = tokens.shape[0]
    chunks = rows // CHUNK
    local = q.shape[1]
    pairs = local // LANES
    inner = hid.shape[1]
    peer = {"tensor": 1 - lax.axis_index("tensor")}

    def load(index, source, target):
        return pltpu.make_async_copy(source, target, load_sem.at[index])

    def save(index, source, target):
        return pltpu.make_async_copy(source, target, save_sem.at[index])

    def span_of(c):
        return pl.ds(pl.multiple_of(c * PROJECT, PROJECT), PROJECT)

    def token_load(c):
        at = span_of(c)
        return pltpu.make_async_copy(tokens_hbm.at[at], tokens.at[at], token_sem.at[c])

    for c in range(rows // PROJECT):
        token_load(c).start()
    loads = [
        load(0, wq_hbm, wq), load(1, wk_hbm, wk), load(2, wv_hbm, wv),
        load(3, wo_hbm, wo), load(4, wu_hbm, wu), load(5, wd_hbm, wd), load(6, cot_hbm, cot),
    ]
    for copy in loads[:3]:
        copy.start()

    levels = dp_size.bit_length() - 1
    me = lax.axis_index("dp")
    bits = [lax.rem(me // (1 << b), 2) for b in range(levels)]
    partner = [{"dp": me + (1 << b) * (1 - 2 * bits[b])} for b in range(levels)]
    half = [dp_size >> (level + 1) for level in range(levels)]
    routes = [list(range(levels)), [0] + list(range(2, levels)) + [1]]
    keep, give = [], []
    for route in routes:
        base, kept, given = 0, [], []
        for level in range(levels):
            kept.append(base + bits[route[level]] * half[level])
            given.append(base + (1 - bits[route[level]]) * half[level])
            base = kept[-1]
        keep.append(kept)
        give.append(given)

    def position(index, way):
        return sum(lax.rem(index // (1 << b), 2) * half[level] for level, b in enumerate(routes[way]))

    def fixed_position(index, way):
        return sum((index >> b) % 2 * half[level] for level, b in enumerate(routes[way]))

    barrier = pltpu.get_barrier_semaphore()
    for other in [peer] + partner:
        pl.semaphore_signal(barrier, inc=1, device_id=other, device_id_type=MESH)

    width = tokens.shape[1]
    blk = width // dp_size

    split = local // 4
    mine, far = lax.rem(me, 4), lax.rem(me + 2, 4)
    att_peer = gffn.at[:, pl.ds(0, local)]

    def wo_piece(which, side):
        start = pl.multiple_of(side * local + which * split, split)
        return gffn.at[pl.ds(start, split), pl.ds(width - local, local)]

    def wo_cross(side):
        return pltpu.make_async_remote_copy(
            src_ref=wo_hbm.at[pl.ds(pl.multiple_of(mine * split, split), split), pl.ds(side * local, local)],
            dst_ref=wo_piece(mine, side),
            send_sem=wo_sem.at[side],
            recv_sem=wo_sem.at[2 + side],
            device_id=peer,
            device_id_type=MESH,
        )

    def wo_share(step, side):
        which = far if step == 2 else mine
        return pltpu.make_async_remote_copy(
            src_ref=wo_piece(which, side),
            dst_ref=wo_piece(which, side),
            send_sem=wo_sem.at[4 * step + 4 + side],
            recv_sem=wo_sem.at[4 * step + 6 + side],
            device_id=partner[1] if step == 0 else partner[0],
            device_id_type=MESH,
        )

    wide = 1024
    count = inner // wide
    rows_at = lambda ref, start, size: ref.at[pl.ds(start, size), :]
    cols_at = lambda ref, start, size: ref.at[:, pl.ds(start, size)]
    table = [(rows_at(wd, u * width, width), cols_at(down_ref, u * wide, wide), None, WAYS[u]) for u in range(count)]
    table += [
        (cols_at(wu, u * wide, wide), cols_at(up_ref, u * wide, wide), None, WAYS[count + u]) for u in range(count)
    ]
    attn_first = 2 * count
    for i in range(4):
        cols = pl.ds(i * local, local)
        table.append((hid.at[:, cols], attn_ref.at[:, cols], cols, WAYS[attn_first + i]))
    norm_unit = len(table)
    table.append((norm_held, norm_ref, None, 1))

    def held(unit):
        return table[unit][0]

    def inbox(unit, level):
        if unit == norm_unit:
            return norm_box.at[pl.ds(8 * (dp_size - 2 * half[level]), 8 * half[level]), :]
        size = half[level] * blk
        if unit >= attn_first:
            return slope.at[pl.ds(width - 2 * size, size), table[unit][2]]
        if level == 0:
            return rows_at(got2 if unit < count else tokens, (unit % count) * size, size)
        if level == 1:
            return rows_at(gffn, unit * size, size)
        return rows_at(tokens, 2 * count * (width // 4 - 2 * size) + unit * size, size)

    def block_of(unit):
        return 8 if unit == norm_unit else blk

    def hop(unit, level):
        way = table[unit][3]
        rows_each = block_of(unit)
        index = unit * levels + level
        start = pl.multiple_of(give[way][level] * rows_each, 8)
        return pltpu.make_async_remote_copy(
            src_ref=held(unit).at[pl.ds(start, half[level] * rows_each), :],
            dst_ref=inbox(unit, level),
            send_sem=give_sem.at[index],
            recv_sem=take_sem.at[index],
            device_id=partner[routes[way][level]],
            device_id_type=MESH,
        )

    def credit(unit, level):
        return free_sem.at[(2 * levels if unit >= attn_first else 0) + 2 * level + table[unit][3]]

    def release(which, level):
        for way in range(2):
            same = [u for u in which if table[u][3] == way]
            if same:
                pl.semaphore_signal(
                    credit(same[0], level), inc=len(same), device_id=partner[routes[way][level]], device_id_type=MESH
                )

    def send(unit, level):
        if unit != norm_unit:
            pl.semaphore_wait(credit(unit, level), 1)
        hop(unit, level).start()

    def take(unit, level):
        hop(unit, level).wait_recv()
        rows_each = block_of(unit)
        size = half[level] * rows_each
        step_rows = min(size, 32)
        ours, came = held(unit), inbox(unit, level)
        last = level == levels - 1
        target = table[unit][1]
        first = keep[table[unit][3]][level] * rows_each

        def add(b, carry):
            here = pl.multiple_of(b * step_rows, step_rows)
            there = pl.multiple_of(first + b * step_rows, 8)
            total = ours[pl.ds(there, step_rows), :].astype(F32) + came[pl.ds(here, step_rows), :].astype(F32)
            if last:
                target[pl.ds(here, step_rows), :] = total
            else:
                ours[pl.ds(there, step_rows), :] = total.astype(ours.dtype)
            return carry

        lax.fori_loop(0, size // step_rows, add, 0)
        if unit == 2 * count - 1 and level == 0:
            for other in range(2, levels):
                release(range(2 * count), other)
        if not last:
            send(unit, level + 1)

    def weight_grad(left, groups):
        span = 256

        def part(j, carry):
            turned = left[:, pl.ds(pl.multiple_of(j * span, span), span)].T
            for right, ref, at, way in groups:
                grad = dot(turned, right[...], NN).astype(BF16)
                for i in range(span // blk):
                    start = pl.multiple_of(position(j * (span // blk) + i, way) * blk, 8)
                    ref[pl.ds(start, blk), pl.ds(at, grad.shape[1])] = grad[i * blk : (i + 1) * blk]
            return carry

        lax.fori_loop(0, width // span, part, 0)

    def rows_of(c):
        return pl.ds(pl.multiple_of(c * CHUNK, CHUNK), CHUNK)

    def exchange(step, c, source, target):
        index = step * chunks + c
        return pltpu.make_async_remote_copy(
            src_ref=source.at[rows_of(c)],
            dst_ref=target.at[rows_of(c)],
            send_sem=send_sem.at[index],
            recv_sem=recv_sem.at[index],
            device_id=peer,
            device_id_type=MESH,
        )

    length = length_ref[0]

    def gain(j):
        return gain_ref[j : j + 1, :]

    def bias(j):
        return bias_ref[j : j + 1, :]

    def blocks(c, body, size=CHUNK):
        def step(b, carry):
            start = pl.multiple_of(c * size + b * BLOCK, BLOCK)
            body(start, pl.ds(start, BLOCK))
            return carry

        lax.fori_loop(0, size // BLOCK, step, 0)

    def real_rows(start):
        index = start + lax.broadcasted_iota(jnp.int32, (BLOCK, 1), 0)
        return jnp.where(index < length, 1.0, 0.0)

    acc[...] = jnp.zeros_like(acc)

    def query_rows(at):
        q[at, :] = (dot(nin[at, :], wq[...], NN) * 0.125).astype(BF16)

    def norm_in(start, at):
        hat, _ = normalize(tokens[at, :].astype(F32))
        nin[at, :] = (hat * gain(0) + bias(0)).astype(BF16)

    spans = rows // PROJECT
    for c in range(spans // 2):
        token_load(c).wait()
        blocks(c, norm_in, PROJECT)
        if c == 0:
            pl.semaphore_wait(barrier, levels + 1)
            for side in range(2):
                wo_cross(side).start()
    for c in range(spans // 2, spans):
        token_load(c).wait()
    for copy in loads[3:]:
        copy.start()
    for copy in loads[:3]:
        copy.wait()
    for h in range(2):
        at = pl.ds(h * rows // 2, rows // 2)
        normed = nin[at, :]
        k[at, :] = dot(normed, wk[...], NN).astype(BF16)
        v[at, :] = dot(normed, wv[...], NN).astype(BF16)
        if h == 0:
            for b in range(rows // 2 // BLOCK):
                start = rows // 2 + b * BLOCK
                norm_in(start, pl.ds(start, BLOCK))
    query_rows(span_of(0))
    save(0, nin, nin_hbm).start()

    key_bias = jnp.where(lane_index((1, rows)) < length, 0.0, NEG)

    def attend(c, carry):
        at = rows_of(c)

        ratio = PROJECT // CHUNK

        @pl.when(jnp.logical_and(lax.rem(c, ratio) == 0, c > 0))
        def _():
            query_rows(span_of(c // ratio))

        def pair(p, carry):
            cols = pl.ds(pl.multiple_of(p * LANES, LANES), LANES)
            keys, values = k[:, cols], v[:, cols]
            scores = dot(stack_pair(q[at, cols]), keys, NT) + key_bias
            top = jnp.max(scores, axis=1, keepdims=True)
            weights = jnp.exp(scores - top)
            total = jnp.sum(weights, axis=1, keepdims=True)
            mixed = dot(weights.astype(BF16), values, NN) / total
            first, second = jnp.split(top + jnp.log(total), 2, axis=0)
            logs = lse[at, :]
            lane = lane_index(logs.shape)
            lse[at, :] = jnp.where(lane == 2 * p, first, jnp.where(lane == 2 * p + 1, second, logs))
            att[at, cols] = join_pair(mixed).astype(BF16)
            return carry

        lax.fori_loop(0, pairs, pair, 0, unroll=UNROLL)
        exchange(0, c, att, att_peer).start()

        @pl.when(c == 2)
        def _():
            for side in range(2):
                wo_cross(side).wait_recv()
                wo_share(0, side).start()
                wo_share(1, side).start()

        @pl.when(c == chunks - 2)
        def _():
            for side in range(2):
                wo_share(0, side).wait_recv()
                wo_share(2, side).start()

        return carry

    lax.fori_loop(0, chunks, attend, 0)
    for copy in loads[3:6]:
        copy.wait()
    for side in range(2):
        wo_share(0, side).wait_send()
        wo_share(1, side).wait()
        wo_share(2, side).wait()
    save(0, nin, nin_hbm).wait()
    nmid = nin

    def feed(c, carry):
        at = rows_of(c)
        exchange(0, c, att, att_peer).wait_recv()
        ours = dot(att[at, :], wo[...], NN).astype(BF16).astype(F32)
        other = att_peer[at, :]
        for side in range(2):
            cols = pl.ds(side * local, local)
            weight = gffn[pl.ds(side * local, local), pl.ds(width - local, local)]
            theirs = dot(other, weight, NN).astype(BF16).astype(F32)
            attn_total[at, cols] = ours[:, side * local : (side + 1) * local] + theirs

        def norms(start, at):
            hat, scale = normalize(attn_total[at, :])
            attn_total[at, :] = hat
            lse[at, :] = jnp.where(lane_index((BLOCK, LANES)) == 2 * pairs, scale, lse[at, :])
            mid = tokens[at, :].astype(F32) + (hat * gain(1) + bias(1))
            middle[at, :] = mid
            hat, _ = normalize(mid)
            nmid[at, :] = (hat * gain(2) + bias(2)).astype(BF16)

        blocks(c, norms)
        normed = nmid[at, :]
        span = 512
        for n in range(inner // span):
            cols = pl.ds(n * span, span)
            value, grade = gelu_both(dot(normed, wu[:, cols], NN))
            hid[at, cols] = value.astype(BF16)
            slope[at, cols] = grade.astype(BF16)
        own2[at, :] = dot(hid[at, :], wd[...], NN).astype(BF16)
        exchange(1, c, own2, got2).start()
        return carry

    lax.fori_loop(0, chunks, feed, 0)
    loads[6].wait()

    def feed_back(c, carry):
        at = rows_of(c)
        exchange(1, c, own2, got2).wait_recv()

        def norms(start, at):
            hat, scale = normalize(own2[at, :].astype(F32) + got2[at, :].astype(F32))
            out = middle[at, :] + (hat * gain(3) + bias(3))
            result_ref[at, :] = out.astype(BF16)
            grad = cot[at, :].astype(F32) * real_rows(start)
            gffn[at, :] = norm_pull(hat, scale, gain(3), grad).astype(BF16)
            acc[2] += fold_rows(grad * hat)
            acc[5] += fold_rows(grad)
            hat, scale = normalize(middle[at, :])
            middle[at, :] = hat
            lse[at, :] = jnp.where(lane_index((BLOCK, LANES)) == 2 * pairs + 1, scale, lse[at, :])

        blocks(c, norms)
        grad = gffn[at, :]
        span = 512
        for n in range(inner // span):
            cols = pl.ds(n * span, span)
            grown = dot(grad, wd[cols, :], NT)
            slope[at, cols] = (grown * slope[at, cols].astype(F32)).astype(BF16)
        exchange(1, c, own2, got2).wait_send()
        own2[at, :] = dot(slope[at, :], wu[...], NT).astype(BF16)
        exchange(2, c, own2, got3).start()
        return carry

    lax.fori_loop(0, chunks, feed_back, 0)
    release(range(2 * count), 0)

    def parts(source, first_unit):
        units = range(first_unit, first_unit + count)
        return [(cols_at(source, i * wide, wide), held(u), 0, table[u][3]) for i, u in enumerate(units)]

    weight_grad(gffn, parts(hid, 0))
    release(range(2 * count), 1)
    for u in range(count):
        send(u, 0)
    weight_grad(nmid, parts(slope, count))
    for level in range(levels):
        release(range(attn_first, norm_unit), level)
    for u in range(count, 2 * count):
        send(u, 0)
    nin_back = pltpu.make_async_copy(nin_hbm, nin, save_sem.at[1])
    nin_back.start()
    for u in range(count):
        take(u, 0)
    gk[...] = jnp.zeros_like(gk)
    gv[...] = jnp.zeros_like(gv)

    agenda = {}
    for (u, level), slot in sorted(SLOTS.items(), key=lambda item: item[1]):
        agenda.setdefault(slot, []).append((u, level))

    tokens_back = pltpu.make_async_copy(tokens_hbm, got2, save_sem.at[2])

    gatt = hid.at[pl.ds(0, CHUNK), pl.ds(0, local)]

    def attend_back(c, carry):
        at = rows_of(c)

        @pl.when(c == chunks - 1)
        def _():
            attn_total[:CHUNK, :] = dot(q[:CHUNK, :], wq[...], NT)

        for slot, work in agenda.items():

            @pl.when(c == slot)
            def _(work=work):
                for unit, level in work:
                    take(unit, level)

        exchange(2, c, own2, got3).wait_recv()

        def norms(start, at):
            grad = own2[at, :].astype(F32) + got3[at, :].astype(F32)
            hat, scale = middle[at, :], lse[at, 2 * pairs + 1 : 2 * pairs + 2]
            out = cot[at, :].astype(F32) * real_rows(start)
            mid = out + norm_pull(hat, scale, gain(2), grad)
            acc[1] += fold_rows(grad * hat)
            acc[4] += fold_rows(grad)
            middle[at, :] = mid
            hat, scale = attn_total[at, :], lse[at, 2 * pairs : 2 * pairs + 1]
            gattn[at, :] = norm_pull(hat, scale, gain(1), mid).astype(BF16)
            acc[0] += fold_rows(mid * hat)
            acc[3] += fold_rows(mid)

        blocks(c, norms)

        @pl.when(c == chunks - 1)
        def _():
            pl.semaphore_signal(free_sem.at[4 * levels], inc=1, device_id=peer, device_id_type=MESH)
            tokens_back.start()

        gatt[...] = dot(gattn[at, :], wo[...], NT).astype(BF16)

        def pair(p, first, last, with_queries=True):
            cols = pl.ds(p * LANES, LANES)
            span = slice(0, last)
            keys, values, grad = k[span, cols], v[span, cols], gatt[:, cols]
            query, grads = stack_pair(q[at, cols]), stack_pair(grad)
            through = stack_pair(grad.astype(F32) * att[at, cols].astype(F32))
            shift = jnp.sum(through, axis=1, keepdims=True)
            logs = lse[at, :]
            log = jnp.concatenate([logs[:, 2 * p : 2 * p + 1], logs[:, 2 * p + 1 : 2 * p + 2]], axis=0)
            weights = jnp.exp(dot(query, keys, NT) + key_bias[:, span] - log)
            slopes = (weights * (dot(grads, values, NT) - shift)).astype(BF16)
            if with_queries:
                q[at, cols] = (join_pair(dot(slopes, keys, NN)) * 0.125).astype(BF16)
            gk[cols, first:last] += dot(query, slopes[:, first:], TN)
            gv[cols, first:last] += dot(grads, weights.astype(BF16)[:, first:], TN)

        @pl.when(c < chunks - 1)
        def _():
            for p in range(pairs):
                pair(p, 0, rows)

        @pl.when(c == chunks - 1)
        def _():
            for p in range(pairs):
                pair(p, 0, CHUNK, False)
            pl.semaphore_wait(free_sem.at[4 * levels], 1)
            exchange(2, 0, own2, got3).wait_send()
            part = attn_total[:CHUNK, :] + dot(gk[:, :CHUNK].astype(BF16).T, wk[...], NT)
            part = part + dot(gv[:, :CHUNK].astype(BF16).T, wv[...], NT)
            own2[:CHUNK, :] = part.astype(BF16)
            exchange(3, 0, own2, got3).start()
            for p in range(pairs):
                pair(p, CHUNK, rows)

        return carry

    lax.fori_loop(0, chunks, attend_back, 0)
    back = got2

    turned = set()

    def turn(c):
        if c not in turned:
            turned.add(c)
            at = rows_of(c)
            k[at, :] = gk[:, at].astype(BF16).T
            v[at, :] = gv[:, at].astype(BF16).T

    def input_part(first, number):
        at = pl.ds(first * CHUNK, number * CHUNK)
        for c in range(first, first + number):
            turn(c)
            exchange(2, c, own2, got3).wait_send()
        part = dot(q[at, :], wq[...], NT) + dot(k[at, :], wk[...], NT) + dot(v[at, :], wv[...], NT)
        own2[at, :] = part.astype(BF16)
        for c in range(first, first + number):
            exchange(3, c, own2, got3).start()

    def project_grads(which):
        for c in range(chunks):
            turn(c)
        if 0 in which:
            nin_back.wait()
        sources = (q, k, v)
        weight_grad(nin, [(sources[i], hid, i * local, WAYS[attn_first + i]) for i in which])
        for i in which:
            send(attn_first + i, 0)

    def out_grad():
        weight_grad(gattn, [(att, hid, 3 * local, WAYS[attn_first + 3])])
        send(attn_first + 3, 0)

    def norm_grads():
        tokens_back.wait()

        def first_norm(c, carry):
            def sums(start, at):
                hat, _ = normalize(back[at, :].astype(F32))
                grad = own2[at, :].astype(F32)
                acc[6] += fold_rows(grad * hat)
                acc[7] += fold_rows(grad)

            blocks(c, sums)
            return carry

        lax.fori_loop(0, chunks, first_norm, 0)
        sums = jnp.concatenate([jnp.sum(acc[j], axis=0, keepdims=True) for j in (6, 0, 1, 2, 7, 3, 4, 5)])
        for index in range(dp_size):
            tile, shift = divmod(index * blk, LANES)
            piece = sums[:, tile * LANES : (tile + 1) * LANES]
            if shift:
                piece = pltpu.roll(piece, LANES - shift, 1)
            spot = 8 * fixed_position(index, 1)
            norm_held[spot : spot + 8, :] = piece
        send(norm_unit, 0)

    def input_grad(c):
        at = rows_of(c)
        exchange(3, c, own2, got3).wait_recv()

        def norms(start, at):
            grad = own2[at, :].astype(F32) + got3[at, :].astype(F32)
            hat, scale = normalize(back[at, :].astype(F32))
            total = middle[at, :] + norm_pull(hat, scale, gain(0), grad)
            ingrad_ref[at, :] = total.astype(BF16)

        blocks(c, norms)

    tell = pltpu.make_async_remote_copy(
        src_ref=norm_ref,
        dst_ref=norm_peer,
        send_sem=send_sem.at[4 * chunks],
        recv_sem=recv_sem.at[4 * chunks],
        device_id=peer,
        device_id_type=MESH,
    )
    everything = [(u, level) for level in range(levels) for u in range(norm_unit + 1)]
    early = set(SLOTS) | {(u, 0) for u in range(count)}
    plan = PLAN
    if levels != 4:
        plan = [("part", 1, chunks - 1), "query", "keyvalue", "out", "norm"] + [x for x in everything if x not in early]
        plan += [("grad", c) for c in range(chunks)]
    assert sorted(x for x in plan if not isinstance(x[0], str)) == sorted(set(everything) - early)
    def finished(level):
        for u in range(norm_unit + 1):
            if level < levels - 1 or u != norm_unit - 1:
                hop(u, level).wait_send()

    if levels == 4:
        for level, spot in ((3, ("grad", chunks - 1)), (2, (7, 3)), (1, (7, 2)), (0, ("grad", 3))):
            plan = plan[: plan.index(spot)] + [("done", level)] + plan[plan.index(spot) :]
    else:
        plan = plan + [("done", level) for level in range(levels)]
    for item in plan:
        if item == "query":
            project_grads((0,))
        elif item == "keyvalue":
            project_grads((1, 2))
        elif item == "out":
            out_grad()
        elif item == "norm":
            norm_grads()
        elif item[0] == "done":
            finished(item[1])
        elif item[0] == "part":
            input_part(*item[1:])
        elif item[0] == "grad":
            input_grad(item[1])
        else:
            take(*item)
            if item == (norm_unit, levels - 1):
                tell.start()
    tell.wait()
    row = lax.broadcasted_iota(jnp.int32, norm_ref.shape, 0)
    norm_ref[...] += jnp.where(lax.rem(row, 4) == 0, norm_peer[...], 0.0)

    def drain(c, carry):
        exchange(0, c, att, att_peer).wait_send()
        exchange(3, c, own2, got3).wait_send()
        return carry

    lax.fori_loop(0, chunks, drain, 0)
    for side in range(2):
        wo_cross(side).wait_send()
    hop(norm_unit - 1, levels - 1).wait_send()


def run_layer(lengths, tokens, wq, wk, wv, wo, wu, wd, gains, biases, cot):
    dp_size = lax.axis_size("dp")
    rows, width = tokens.shape
    local, inner = wq.shape[1], wu.shape[1]
    chunks = rows // CHUNK
    levels = dp_size.bit_length() - 1
    units = 2 * (inner // 1024) + 5
    shape = jax.ShapeDtypeStruct
    anywhere = pl.BlockSpec(memory_space=pl.ANY)
    vmem = pl.BlockSpec(memory_space=pltpu.VMEM)
    wide = (rows, width)
    thin = (rows, local)
    blk = width // dp_size
    outs = [
        pltpu.VMEM(wide, BF16), pltpu.VMEM(wide, BF16), shape(wide, BF16),
        pltpu.VMEM((blk, inner), F32), pltpu.VMEM((blk, inner), F32), pltpu.VMEM((blk, 4 * local), F32),
        pltpu.VMEM((8, LANES), F32),
    ]
    scratch = [
        pltpu.VMEM(wide, BF16), pltpu.VMEM(wq.shape, BF16), pltpu.VMEM(wk.shape, BF16), pltpu.VMEM(wv.shape, BF16),
        pltpu.VMEM(wo.shape, BF16), pltpu.VMEM(wu.shape, BF16), pltpu.VMEM(wd.shape, BF16), pltpu.VMEM(wide, BF16),
        pltpu.VMEM(wide, BF16), pltpu.VMEM(thin, BF16), pltpu.VMEM(thin, BF16), pltpu.VMEM(thin, BF16),
        pltpu.VMEM(thin, BF16), pltpu.VMEM((rows, LANES), F32),
        pltpu.VMEM(wide, F32), pltpu.VMEM(wide, BF16), pltpu.VMEM(wide, BF16), pltpu.VMEM(wide, BF16),
        pltpu.VMEM(wide, F32), pltpu.VMEM((rows, inner), BF16), pltpu.VMEM((rows, inner), BF16),
        pltpu.VMEM(wide, BF16), pltpu.VMEM(wide, BF16),
        pltpu.VMEM((local, rows), F32), pltpu.VMEM((local, rows), F32),
        pltpu.VMEM((8, 8, width), F32),
        pltpu.VMEM((8 * dp_size, LANES), F32), pltpu.VMEM((8 * dp_size, LANES), F32), pltpu.VMEM((8, LANES), F32),
        pltpu.SemaphoreType.DMA((rows // PROJECT,)), pltpu.SemaphoreType.DMA((7,)), pltpu.SemaphoreType.DMA((16,)), pltpu.SemaphoreType.DMA((3,)),
        pltpu.SemaphoreType.DMA((4 * chunks + 1,)), pltpu.SemaphoreType.DMA((4 * chunks + 1,)),
        pltpu.SemaphoreType.DMA((units * levels,)), pltpu.SemaphoreType.DMA((units * levels,)),
        pltpu.SemaphoreType.REGULAR((4 * levels + 1,)),
    ]
    return pl.pallas_call(
        functools.partial(layer_kernel, dp_size),
        out_shape=outs,
        in_specs=[pl.BlockSpec(memory_space=pltpu.SMEM)] + [anywhere] * 7 + [vmem, vmem, anywhere],
        out_specs=[vmem, vmem, anywhere] + [vmem] * 4,
        scratch_shapes=scratch,
        compiler_params=pltpu.CompilerParams(
            collective_id=0, has_side_effects=True, vmem_limit_bytes=VMEM_BYTES - 4 * rows * width - 8 * blk * (inner + 2 * local)
        ),
        name="layer",
    )(lengths, tokens, wq, wk, wv, wo, wu, wd, gains, biases, cot)


def finish_kernel(
    result_in, ingrad_in, up_in, down_in, attn_in, norm_in, result, ingrad, query, key, value, out, up, down, gain, bias, sem
):
    local = query.shape[1]
    pairs = [(result_in, result), (ingrad_in, ingrad), (up_in, up), (down_in, down)]
    pairs += [(attn_in.at[:, pl.ds(i * local, local)], ref) for i, ref in enumerate((query, key, value, out))]
    copies = [pltpu.make_async_copy(source, target, sem.at[i]) for i, (source, target) in enumerate(pairs)]
    for copy in copies:
        copy.start()
    blk = gain.shape[1]
    gain[...] = norm_in[:4, :blk]
    bias[...] = norm_in[4:, :blk]
    for copy in copies:
        copy.wait()


def on_device(tokens, lengths, wq, wk, wv, wo, wu, wd, gains, biases, cot):
    local, inner = wq.shape[1], wu.shape[1]
    result, input_grad, _, up, down, attn, norms = run_layer(
        lengths, tokens, wq, wk, wv, wo, wu, wd, gains, biases, cot
    )
    blk = up.shape[0]
    shape = jax.ShapeDtypeStruct
    anywhere = pl.BlockSpec(memory_space=pl.ANY)
    vmem = pl.BlockSpec(memory_space=pltpu.VMEM)
    result, input_grad, query, key, value, out, up, down, gain, bias = pl.pallas_call(
        finish_kernel,
        out_shape=[shape(result.shape, BF16), shape(result.shape, BF16)]
        + [shape((blk, local), F32)] * 4
        + [shape((blk, inner), F32)] * 2
        + [shape((4, blk), F32)] * 2,
        in_specs=[vmem] * 6,
        out_specs=[anywhere] * 8 + [vmem] * 2,
        scratch_shapes=[pltpu.SemaphoreType.DMA((8,))],
        compiler_params=pltpu.CompilerParams(vmem_limit_bytes=4 * 1024 * 1024),
        name="finish",
    )(result, input_grad, up, down, attn, norms)
    return result, input_grad, query, key, value, out.T, up, down.T, gain, bias


def solution(mesh):
    in_specs = (
        P("dp", None), P("dp"), P(None, "tensor"), P(None, "tensor"), P(None, "tensor"), P("tensor", None),
        P(None, "tensor"), P("tensor", None), P(), P(), P("dp", None),
    )
    out_specs = (
        P("dp", None), P("dp", None), P("dp", "tensor"), P("dp", "tensor"), P("dp", "tensor"), P("tensor", "dp"),
        P("dp", "tensor"), P("tensor", "dp"), P(None, "dp"), P(None, "dp"),
    )
    return jax.shard_map(on_device, mesh=mesh, in_specs=in_specs, out_specs=out_specs, check_vma=False)
```
